32 devices in a mesh: dp: 8 (over z, y), tensor: 4 (over x, core).
Axes of the slice: x: 2, y: 2, z: 4, core: 2. Of those that a mesh axis runs over, the one named last changes fastest.
Arguments:
- tokens: bfloat16 [8192, 1024], P(('dp', 'tensor')), may hold values from -6 to 6
- cotangent: float32 [8192, 1024], P(('dp', 'tensor')), may hold values from -6 to 6
- lengths: int32 [8, 2], P('dp'), may hold values from 64 to 512, as said below
- order: int32 [8, 1024], P('dp'), may hold values from 0 to 1023, each once within a row
- adapter_ids: int32 [8, 2], P('dp'), may hold values from 0 to 7
- norm1_gain: float32 [1024], replicated, may hold values from 0.25 to 1.75
- norm1_shift: float32 [1024], replicated, may hold values from -1.5 to 1.5
- qkv_weight: bfloat16 [1024, 3, 1024], P(None, None, 'tensor'), may hold values from -0.1875 to 0.1875
- qv_bias: float32 [2, 1024], P(None, 'tensor'), may hold values from -1.5 to 1.5
- proj_weight: bfloat16 [1024, 1024], P('tensor'), may hold values from -1.5 to 1.5
- proj_bias: float32 [1024], replicated, may hold values from -1.5 to 1.5
- norm2_gain: float32 [1024], replicated, may hold values from 0.25 to 1.75
- norm2_shift: float32 [1024], replicated, may hold values from -1.5 to 1.5
- up_weight: bfloat16 [1024, 4096], P(None, 'tensor'), may hold values from -0.1875 to 0.1875
- up_bias: float32 [4096], P('tensor'), may hold values from -1.5 to 1.5
- down_weight: bfloat16 [4096, 1024], P('tensor'), may hold values from -0.09375 to 0.09375
- down_bias: float32 [1024], replicated, may hold values from -1.5 to 1.5
- adapt_qkv_in: bfloat16 [1024, 128], replicated, may hold values from -0.1875 to 0.1875
- adapt_qkv_out: bfloat16 [128, 3, 1024], P(None, None, 'tensor'), may hold values from -0.75 to 0.75
- adapt_proj_in: bfloat16 [1024, 128], P('tensor'), may hold values from -0.75 to 0.75
- adapt_proj_out: bfloat16 [128, 1024], replicated, may hold values from -0.75 to 0.75
- adapt_up_in: bfloat16 [1024, 128], replicated, may hold values from -0.1875 to 0.1875
- adapt_up_out: bfloat16 [128, 4096], P(None, 'tensor'), may hold values from -0.75 to 0.75
- adapt_down_in: bfloat16 [4096, 128], P('tensor'), may hold values from -0.09375 to 0.09375
- adapt_down_out: bfloat16 [128, 1024], replicated, may hold values from -0.75 to 0.75
Outputs:
- result: float32 [8192, 1024], P(('dp', 'tensor'))
- grad_input: float32 [8192, 1024], P(('dp', 'tensor'))
- grad_qkv_in: float32 [1024, 128], replicated
- grad_qkv_out: float32 [128, 3, 1024], P(None, None, 'tensor')
- grad_proj_in: float32 [1024, 128], P('tensor')
- grad_proj_out: float32 [128, 1024], replicated
- grad_up_in: float32 [1024, 128], replicated
- grad_up_out: float32 [128, 4096], P(None, 'tensor')
- grad_down_in: float32 [4096, 128], P('tensor')
- grad_down_out: float32 [128, 1024], replicated
The draws below stay inside these ranges and needn't reach their ends.
Inputs may be any that keep to these rules, and one draw needn't show every extreme that they name: `lengths`: in every group one sequence has exactly 512 valid tokens; the others have at least 512 // 8 (and at least one). `order`: each row is a permutation of the group's 1024 stored rows.
All inputs are finite; a program needn't handle non-finite values.
Results may differ from the reference program's by a relative error of at most 0.023.
Values may be sent and summed in bfloat16 or wider, within the bound.
No kernel may reach another device: no remote copies, remote signals or barrier semaphores. Data moves between devices by JAX's collectives and lax.ppermute only.
A program may use at most 128 MiB of HBM per device.

```python
import math
import jax
import jax.numpy as jnp
from jax import lax

D = 1024
H = 16
HD = 64
FF = 4096
RANK = 16
ADAPTERS = 8
GROUPS = 8
GROUP_TOK = 1024
SEQS = 2
SEQ_LEN = 512
TOKENS = 8192
ADAPT_COLS = 128
N_TENSOR = 4


def draw_lengths(key, part):
    first_key = jax.random.fold_in(key, 11)
    second_key = jax.random.fold_in(key, 23)
    drawn = jax.random.randint(first_key, (GROUPS, SEQS), max(SEQ_LEN // 8, 1), SEQ_LEN + 1)
    longest = jax.random.randint(second_key, (GROUPS, 1), 0, SEQS)
    slots = jnp.arange(SEQS, dtype=jnp.int32)[None, :]
    return jnp.where(slots == longest, SEQ_LEN, drawn).astype(jnp.int32)


def plant(entries, own_key, smallest, largest):
    extent = entries.shape
    spot = [jax.random.randint(jax.random.fold_in(own_key, axis), (), 0, extent[axis]) for axis in range(len(extent))]
    entries = entries.at[tuple(spot)].set(smallest)
    longest = extent.index(max(extent))
    spot[longest] = (spot[longest] + 1) % extent[longest]
    return entries.at[tuple(spot)].set(largest)


def block_levels(rng, dims, cuts, low, top_value):
    def one(axis_at, blocks):
        steps = jax.random.uniform(jax.random.fold_in(jax.random.fold_in(rng, 6), axis_at), (blocks,), jnp.float32, low / len(cuts), top_value / len(cuts))
        return jnp.repeat(jnp.exp(steps), dims[axis_at] // blocks).reshape((-1,) + (1,) * (len(dims) - axis_at - 1))

    level = one(*cuts[0])
    for cut in cuts[1:]:
        level = level * one(*cut)
    return level


def noise(stream_key, dims, deviation, bound, cuts=(), kind=jnp.bfloat16):
    values = deviation * jax.random.normal(stream_key, dims, jnp.float32)
    if cuts:
        values = values * block_levels(stream_key, dims, cuts, -0.22, 0.18)
    return jnp.clip(values, -bound, bound).astype(kind)


def setup_inputs(seed: int = 0) -> dict:
    arg_keys = jax.random.split(jax.random.key(seed), 26)
    tokens = noise(arg_keys[0], (TOKENS, D), 1.0, 6.0, ((0, 32),))
    cotangent = noise(arg_keys[1], (TOKENS, D), 1.0, 6.0, ((0, 32),), jnp.float32)
    lengths = draw_lengths(jax.random.fold_in(arg_keys[25], 71), 0)
    order = jax.vmap(lambda own: jax.random.permutation(own, GROUP_TOK))(jax.random.split(arg_keys[3], GROUPS)).reshape((GROUPS, GROUP_TOK)).astype(jnp.int32)
    adapter_ids = plant(jax.random.randint(arg_keys[4], (GROUPS, SEQS), 0, ADAPTERS), jax.random.fold_in(arg_keys[4], 1), 0, ADAPTERS - 1).astype(jnp.int32)
    norm1_gain = jnp.clip(1.0 + 0.15 * jax.random.normal(arg_keys[5], (D,), jnp.float32), 0.25, 1.75)
    norm1_shift = noise(arg_keys[6], (D,), 0.3, 1.5, (), jnp.float32)
    qkv_weight = noise(arg_keys[7], (D, 3, D), D ** -0.5, 0.1875, ((2, 4),))
    qv_bias = noise(arg_keys[8], (2, D), 0.3, 1.5, ((1, 4),), jnp.float32)
    proj_weight = noise(arg_keys[9], (D, D), (HD // 4) ** -0.5, 1.5, ((0, 4),))
    proj_bias = noise(arg_keys[10], (D,), 0.3, 1.5, (), jnp.float32)
    norm2_gain = jnp.clip(1.0 + 0.15 * jax.random.normal(arg_keys[11], (D,), jnp.float32), 0.25, 1.75)
    norm2_shift = noise(arg_keys[12], (D,), 0.3, 1.5, (), jnp.float32)
    up_weight = noise(arg_keys[13], (D, FF), D ** -0.5, 0.1875, ((1, 4),))
    up_bias = noise(arg_keys[14], (FF,), 0.3, 1.5, ((0, 4),), jnp.float32)
    down_weight = noise(arg_keys[15], (FF, D), FF ** -0.5, 0.09375, ((0, 4),))
    down_bias = noise(arg_keys[16], (D,), 0.3, 1.5, (), jnp.float32)
    adapt_qkv_in = noise(arg_keys[17], (D, ADAPT_COLS), D ** -0.5, 0.1875)
    adapt_qkv_out = noise(arg_keys[18], (ADAPT_COLS, 3, D), (4 * RANK) ** -0.5, 0.75, ((2, 4),))
    adapt_proj_in = noise(arg_keys[19], (D, ADAPT_COLS), (D // 16) ** -0.5, 0.75, ((0, 4),))
    adapt_proj_out = noise(arg_keys[20], (ADAPT_COLS, D), (4 * RANK) ** -0.5, 0.75)
    adapt_up_in = noise(arg_keys[21], (D, ADAPT_COLS), D ** -0.5, 0.1875)
    adapt_up_out = noise(arg_keys[22], (ADAPT_COLS, FF), (4 * RANK) ** -0.5, 0.75, ((1, 4),))
    adapt_down_in = noise(arg_keys[23], (FF, ADAPT_COLS), FF ** -0.5, 0.09375, ((0, 4),))
    adapt_down_out = noise(arg_keys[24], (ADAPT_COLS, D), (4 * RANK) ** -0.5, 0.75)
    return {"tokens": tokens, "cotangent": cotangent, "lengths": lengths, "order": order, "adapter_ids": adapter_ids, "norm1_gain": norm1_gain, "norm1_shift": norm1_shift, "qkv_weight": qkv_weight, "qv_bias": qv_bias, "proj_weight": proj_weight, "proj_bias": proj_bias, "norm2_gain": norm2_gain, "norm2_shift": norm2_shift, "up_weight": up_weight, "up_bias": up_bias, "down_weight": down_weight, "down_bias": down_bias, "adapt_qkv_in": adapt_qkv_in, "adapt_qkv_out": adapt_qkv_out, "adapt_proj_in": adapt_proj_in, "adapt_proj_out": adapt_proj_out, "adapt_up_in": adapt_up_in, "adapt_up_out": adapt_up_out, "adapt_down_in": adapt_down_in, "adapt_down_out": adapt_down_out}


EPSILON = 1e-05
NEGATIVE = -1000000000.0
HIGH = lax.Precision.HIGHEST

@jax.custom_vjp
def low(v):
    return lax.optimization_barrier(v.astype(jnp.bfloat16)).astype(jnp.float32)

@jax.custom_vjp
def low_back(v):
    return v

def low_keep(v):
    return (low(v), None)

def low_pass(kept, grad):
    return (grad,)

def back_keep(v):
    return (v, None)

def back_low(kept, grad):
    return (low(grad),)
low.defvjp(low_keep, low_pass)
low_back.defvjp(back_keep, back_low)

def layer_norm(values, gain, shift):
    centre = values - lax.optimization_barrier(jnp.mean(values, -1, keepdims=True))
    spread = lax.optimization_barrier(jnp.mean(centre * centre, -1, keepdims=True))
    return centre * lax.rsqrt(spread + EPSILON) * gain + shift

def highdot(left, right):
    return jnp.dot(left, right, precision=HIGH)

def attend_sequence(queries, keys, values, length):
    scale = 1.0 / math.sqrt(HD)
    raw = jnp.einsum('qhc,khc->hqk', queries, keys, precision=HIGH)
    scores = low_back(raw) * scale
    positions = jnp.arange(queries.shape[0], dtype=jnp.int32)
    allowed = (positions[None, :] <= positions[:, None]) & (positions[None, :] < length)
    scores = jnp.where(allowed[None], scores, NEGATIVE)
    probs = low(jax.nn.softmax(scores, axis=-1))
    return jnp.einsum('hqk,khc->qhc', probs, values, precision=HIGH)

def attend_entry(entry):
    block, length = entry
    return attend_sequence(block[:, 0], block[:, 1], block[:, 2], length)

def group_layer(xg, adapters, frozen, order_row, inverse, select, lengths_row):
    qkv_in, qkv_out, proj_in, proj_out, up_in, up_out, down_in, down_out = adapters
    gain_one, shift_one, w_qkv, bias_three, w_proj, b_proj, gain_two, shift_two, w_up, b_up, w_down, b_down = frozen
    width_here = D // N_TENSOR
    hidden_here = FF // N_TENSOR
    heads_here = H // N_TENSOR
    normed1 = low(layer_norm(xg, gain_one, shift_one))
    low1 = low(low_back(highdot(normed1, qkv_in) * select))
    attn_sum = jnp.zeros((GROUP_TOK, D), jnp.float32)
    proj_sum = jnp.zeros((GROUP_TOK, ADAPT_COLS), jnp.float32)
    for shard in range(N_TENSOR):
        cols = slice(shard * width_here, (shard + 1) * width_here)
        rows_copy = low_back(normed1)
        low_copy = low_back(low1)
        qkv = jnp.einsum('rd,dkc->rkc', rows_copy, w_qkv[:, :, cols], precision=HIGH)
        qkv = qkv + jnp.einsum('ra,akc->rkc', low_copy, qkv_out[:, :, cols], precision=HIGH) + bias_three[None, :, cols]
        qkv = low(low_back(qkv))
        ordered = qkv[order_row].reshape(SEQS, SEQ_LEN, 3, heads_here, HD)
        attended = lax.map(jax.checkpoint(attend_entry), (ordered, lengths_row))
        attended = low(low_back(attended.reshape(GROUP_TOK, width_here)))
        stored = attended[inverse]
        attn_sum = attn_sum + low(highdot(stored, w_proj[cols, :]))
        proj_sum = proj_sum + low(highdot(stored, proj_in[cols, :]) * select)
    proj_low = low(low_back(proj_sum))
    branch_one = low_back(attn_sum + highdot(proj_low, proj_out))
    mid = xg + branch_one + b_proj
    normed2 = low(layer_norm(mid, gain_two, shift_two))
    low2 = low(low_back(highdot(normed2, up_in) * select))
    mlp_sum = jnp.zeros((GROUP_TOK, D), jnp.float32)
    down_sum = jnp.zeros((GROUP_TOK, ADAPT_COLS), jnp.float32)
    for shard in range(N_TENSOR):
        cols = slice(shard * hidden_here, (shard + 1) * hidden_here)
        rows_copy = low_back(normed2)
        low_copy = low_back(low2)
        upper = highdot(rows_copy, w_up[:, cols]) + highdot(low_copy, up_out[:, cols]) + b_up[cols]
        upper = low_back(upper)
        active = low(jax.nn.gelu(upper, approximate=True))
        mlp_sum = mlp_sum + low(highdot(active, w_down[cols, :]))
        down_sum = down_sum + low(highdot(active, down_in[cols, :]) * select)
    down_low = low(low_back(down_sum))
    branch_two = low_back(mlp_sum + highdot(down_low, down_out))
    return mid + branch_two + b_down

def reference(tokens, cotangent, lengths, order, adapter_ids, norm1_gain, norm1_shift, qkv_weight, qv_bias, proj_weight, proj_bias, norm2_gain, norm2_shift, up_weight, up_bias, down_weight, down_bias, adapt_qkv_in, adapt_qkv_out, adapt_proj_in, adapt_proj_out, adapt_up_in, adapt_up_out, adapt_down_in, adapt_down_out):
    adapters = (adapt_qkv_in.astype(jnp.float32), adapt_qkv_out.astype(jnp.float32), adapt_proj_in.astype(jnp.float32), adapt_proj_out.astype(jnp.float32), adapt_up_in.astype(jnp.float32), adapt_up_out.astype(jnp.float32), adapt_down_in.astype(jnp.float32), adapt_down_out.astype(jnp.float32))
    bias_three = jnp.stack([qv_bias[0], jnp.zeros((D,), jnp.float32), qv_bias[1]]).astype(jnp.float32)
    frozen = (norm1_gain.astype(jnp.float32), norm1_shift.astype(jnp.float32), qkv_weight.astype(jnp.float32), bias_three, proj_weight.astype(jnp.float32), proj_bias.astype(jnp.float32), norm2_gain.astype(jnp.float32), norm2_shift.astype(jnp.float32), up_weight.astype(jnp.float32), up_bias.astype(jnp.float32), down_weight.astype(jnp.float32), down_bias.astype(jnp.float32))
    inputs = tokens.astype(jnp.float32).reshape(GROUPS, GROUP_TOK, D)
    cotangents = cotangent.astype(jnp.float32).reshape(GROUPS, GROUP_TOK, D)

    def one_group(carry, entry):
        xg, dyg, order_row, lengths_row, ids_row = entry
        inverse = jnp.zeros((GROUP_TOK,), jnp.int32).at[order_row].set(jnp.arange(GROUP_TOK, dtype=jnp.int32))
        seq_of = inverse // SEQ_LEN
        adapter_of = lax.optimization_barrier(jnp.sum(jnp.where(seq_of[:, None] == jnp.arange(SEQS, dtype=jnp.int32)[None, :], ids_row[None, :], 0), axis=1)).astype(jnp.int32)
        select = (jnp.arange(ADAPT_COLS, dtype=jnp.int32)[None, :] // RANK == adapter_of[:, None]).astype(jnp.float32)

        def forward(x_in, adapters_in):
            return group_layer(x_in, adapters_in, frozen, order_row, inverse, select, lengths_row)
        output, pullback = jax.vjp(forward, xg, adapters)
        grad_x, grad_adapters = pullback(dyg)
        carry = jax.tree.map(jnp.add, carry, grad_adapters)
        return (carry, (output, grad_x))
    zeros = jax.tree.map(jnp.zeros_like, adapters)
    sums, (outputs, grads) = lax.scan(one_group, zeros, (inputs, cotangents, order, lengths, adapter_ids))
    return (outputs.reshape(TOKENS, D), grads.reshape(TOKENS, D), sums[0], sums[1], sums[2], sums[3], sums[4], sums[5], sums[6], sums[7])
```

```python
import functools
import math

import jax
import jax.numpy as jnp
from jax import lax
from jax.experimental import pallas as pl
from jax.experimental.pallas import tpu as pltpu
from jax.sharding import PartitionSpec as P

HD = 64
RANK = 16
PAIR = 2 * HD
EPSILON = 1e-05
NEGATIVE = -1000000000.0
BF = jnp.bfloat16
F32 = jnp.float32
LIMIT = 56 * 1024 * 1024
GELU_A = math.sqrt(2.0 / math.pi)
GELU_B = 0.044715


def dot(left, right):
    return jnp.dot(left, right, preferred_element_type=F32)


def dot_back(left, right):
    return lax.dot_general(left, right, (((1,), (1,)), ((), ())), preferred_element_type=F32)


def dot_over(left, right):
    return lax.dot_general(left, right, (((0,), (0,)), ((), ())), preferred_element_type=F32)


def shape(dims, kind):
    return jax.ShapeDtypeStruct(tuple(dims), kind)


def whole_call(body, inputs, outs, name, smem=(), scratch=()):
    smem_spec = pl.BlockSpec(memory_space=pltpu.SMEM)
    vmem_spec = pl.BlockSpec(memory_space=pltpu.VMEM)
    return pl.pallas_call(
        body,
        out_shape=list(outs),
        in_specs=[smem_spec] * len(smem) + [vmem_spec] * len(inputs),
        out_specs=[vmem_spec] * len(outs),
        scratch_shapes=list(scratch),
        compiler_params=pltpu.CompilerParams(vmem_limit_bytes=LIMIT),
        name=name,
    )(*smem, *inputs)


def norm_parts(values):
    centre = values - jnp.mean(values, -1, keepdims=True)
    spread = jnp.mean(centre * centre, -1, keepdims=True)
    inv = lax.rsqrt(spread + EPSILON)
    return centre * inv, inv


def norm_back(normed, inv, upstream):
    return inv * (
        upstream
        - jnp.mean(upstream, -1, keepdims=True)
        - normed * jnp.mean(upstream * normed, -1, keepdims=True)
    )


def prep_body(pick, qkv_in, qkv_out, proj_in, proj_out, up_in, up_out, down_in, down_out, *outs):
    o_qkv_in, o_qkv_out, o_proj_in, o_proj_out, o_up_in, o_up_out, o_down_in, o_down_out = outs
    chosen = pick[...]
    o_qkv_in[...] = dot_back(chosen, qkv_in[...]).astype(BF)
    for k in range(3):
        o_qkv_out[k] = dot(chosen, qkv_out[k]).astype(BF)
    o_proj_in[...] = dot_back(chosen, proj_in[...]).astype(BF)
    o_proj_out[...] = dot(chosen, proj_out[...]).astype(BF)
    o_up_in[...] = dot_back(chosen, up_in[...]).astype(BF)
    o_up_out[...] = dot(chosen, up_out[...]).astype(BF)
    o_down_in[...] = dot_back(chosen, down_in[...]).astype(BF)
    o_down_out[...] = dot(chosen, down_out[...]).astype(BF)


def qkv_body(count, mask, gain, shift, weight, bias, low_in, low_out, *refs):
    blocks = refs[:count]
    normed_ref, low_ref, qkv_ref = refs[count:]
    rows = blocks[0].shape[0]
    width = weight.shape[2]
    for i in range(count):
        part = pl.ds(i * rows, rows)
        unit, _ = norm_parts(blocks[i][...].astype(F32))
        normed = (unit * gain[...] + shift[...]).astype(BF)
        normed_ref[part, :] = normed
        low = (dot_back(normed, low_in[...]) * mask[part, :]).astype(BF)
        low_ref[part, :] = low
        for k in range(3):
            value = dot(normed, weight[k]) + dot(low, low_out[k]) + bias[k : k + 1, :]
            qkv_ref[part, k * width : (k + 1) * width] = value.astype(BF)


def one_hot_rows(order_col, size, start=0, stop=None):
    stop = size if stop is None else stop
    at = lax.broadcasted_iota(jnp.int32, (order_col.shape[0], stop - start), 1) + start
    return jnp.where(at == order_col, 1.0, 0.0).astype(BF)


def one_hot_cols(order_row, start, stop):
    at = lax.broadcasted_iota(jnp.int32, (stop - start, order_row.shape[1]), 0) + start
    return jnp.where(at == order_row, 1.0, 0.0).astype(BF)


def head_lanes(values, head):
    lane = lax.broadcasted_iota(jnp.int32, values.shape, 1)
    return jnp.where((lane // HD) == head, values, jnp.zeros_like(values))


def key_limit(start, count, length):
    at = lax.broadcasted_iota(jnp.int32, (1, count), 1) + (start + 1)
    return jnp.minimum(at, length)


def attend_body(block, lengths, index, order_row, order_col, local, remote, out, seq, lse, turned):
    rows = order_col.shape[0]
    near = local.shape[0]
    width = local.shape[1] // 3
    seqs = lengths.shape[0]
    seq_len = rows // seqs
    heads = width // HD
    step = min(256, seq_len)
    scale = 1.0 / math.sqrt(HD)
    for s in range(seqs):
        part = pl.ds(s * seq_len, seq_len)
        col = order_col[part, :]
        moved = dot(one_hot_rows(col, rows, 0, near), local[...])
        moved = moved + dot(one_hot_rows(col, rows, near, rows), remote[...])
        seq[part, :width] = (moved[:, :width] * scale).astype(BF)
        seq[part, width:] = moved[:, width:].astype(BF)
    for s in range(seqs):
        base = s * seq_len
        length = lengths[s]
        for pair in range(heads // 2):
            lanes = pl.ds(pair * PAIR, PAIR)
            keys = seq[pl.ds(base, seq_len), pl.ds(width + pair * PAIR, PAIR)]
            values = seq[pl.ds(base, seq_len), pl.ds(2 * width + pair * PAIR, PAIR)]
            values_t = values.astype(F32).T.astype(BF)
            for q in range(seq_len // step):
                queries = seq[pl.ds(base + q * step, step), lanes]
                seen = (q + 1) * step
                limit = key_limit(q * step, step, length)
                at = lax.broadcasted_iota(jnp.int32, (seen, step), 0)
                allowed = at < limit
                for h in range(2):
                    scores = dot_back(keys[:seen], head_lanes(queries, h))
                    scores = jnp.where(allowed, scores, NEGATIVE)
                    top = jnp.max(scores, 0, keepdims=True)
                    weights = jnp.exp(scores - top)
                    total = jnp.sum(weights, 0, keepdims=True)
                    probs = (weights * (1.0 / total)).astype(BF)
                    head = pair * 2 + h
                    turned[pl.ds(head * HD, HD), pl.ds(base + q * step, step)] = dot(
                        values_t[h * HD : (h + 1) * HD, :seen], probs
                    ).astype(BF)
                    lse[pl.ds(head, 1), pl.ds(base + q * step, step)] = top + jnp.log(total)
    for i in range(rows // block):
        place = one_hot_cols(order_row[...], i * block, (i + 1) * block)
        start = pl.multiple_of(index[i] * block, block)
        out[pl.ds(start, block), :] = dot_back(place, turned[...]).astype(BF)


def mid_body(count, index, mask, proj_out, bias, gain, shift, up_in, *refs):
    tokens = refs[:count]
    attended = refs[count : 2 * count]
    weight = refs[2 * count : 3 * count]
    low_in = refs[3 * count : 4 * count]
    near_ref, far_ref, low_near, low_far, proj_low, mid_ref = refs[4 * count :]
    block = tokens[0].shape[0]
    for i in range(count):
        start = pl.multiple_of(index[i] * block, block)
        rows = [a[pl.ds(start, block), :] for a in attended]
        keep = mask[pl.ds(i * block, block), :]
        total = dot(rows[0], weight[0][...])
        low = dot_back(rows[0], low_in[0][...])
        for d in range(1, count):
            total = total + dot(rows[d], weight[d][...])
            low = low + dot_back(rows[d], low_in[d][...])
        low = (low * keep).astype(BF)
        total = total + dot(low, proj_out[...])
        mid = tokens[i][...].astype(F32) + total + bias[...]
        unit, _ = norm_parts(mid)
        normed = (unit * gain[...] + shift[...]).astype(BF)
        low2 = (dot_back(normed, up_in[...]) * keep).astype(BF)
        if i == 0:
            mid_ref[...] = mid
            proj_low[...] = low
        if i < 2:
            near_ref[pl.ds(i * block, block), :] = normed
            low_near[pl.ds(i * block, block), :] = low2
        else:
            far_ref[pl.ds((i - 2) * block, block), :] = normed
            low_far[pl.ds((i - 2) * block, block), :] = low2


def hidden_body(count, mask, normed, low2, up_w, up_b, up_out, up_in, down_w, down_in, down_out, *refs):
    grads = refs[:count]
    out_a, out_b, low_part, grad_down_low, act_ref, gup_ref = refs[count : count + 6]
    acc, low_acc, grad_all = refs[count + 6 :]
    j = pl.program_id(0)
    block = grads[0].shape[0]

    @pl.when(j == 0)
    def _():
        for i in range(count):
            part = pl.ds(i * block, block)
            grad = grads[i][...]
            grad_all[part, :] = grad
            grad_down_low[part, :] = (dot_back(grad, down_out[...]) * mask[part, :]).astype(BF)
        acc[...] = jnp.zeros_like(acc)
        low_acc[...] = jnp.zeros_like(low_acc)

    upper = dot(normed[...], up_w[...]) + dot(low2[...], up_out[...]) + up_b[...]
    grad = dot_back(grad_all[...], down_w[...]) + dot(grad_down_low[...], down_in[...])
    square = upper * upper
    inner = GELU_A * upper * (1.0 + GELU_B * square)
    curve = jnp.tanh(inner)
    half = 0.5 * (1.0 + curve)
    act_ref[...] = (upper * half).astype(BF)
    slope = half + 0.5 * upper * (1.0 - curve * curve) * (GELU_A * (1.0 + 3.0 * GELU_B * square))
    grad_upper = (grad * slope).astype(BF)
    gup_ref[...] = grad_upper
    acc[...] += dot_back(grad_upper, up_w[...])
    low_acc[...] += dot_back(grad_upper, up_out[...])

    @pl.when(j == pl.num_programs(0) - 1)
    def _():
        low = (low_acc[...] * mask[...]).astype(BF)
        low_part[...] = low
        total = acc[...] + dot(low, up_in[...])
        for i in range(count):
            target = out_a if i % 2 == 0 else out_b
            target[pl.ds((i // 2) * block, block), :] = total[i * block : (i + 1) * block].astype(BF)


def hidden_call(mask, normed, low2, grads, up_w, up_b, up_out, up_in, down_w, down_in, down_out, name):
    rows, wide = normed.shape
    hid = up_w.shape[1]
    chunk = min(256, hid)
    count = len(grads)
    ranks = low2.shape[1]
    full = lambda dims: pl.BlockSpec(tuple(dims), lambda j: (0,) * len(dims))
    half = rows // 2
    return pl.pallas_call(
        functools.partial(hidden_body, count),
        grid=(hid // chunk,),
        out_shape=[
            shape((half, wide), BF),
            shape((half, wide), BF),
            shape((rows, ranks), BF),
            shape((rows, ranks), BF),
            shape((rows, hid), BF),
            shape((rows, hid), BF),
        ],
        in_specs=[
            full(mask.shape),
            full(normed.shape),
            full(low2.shape),
            pl.BlockSpec((wide, chunk), lambda j: (0, j)),
            pl.BlockSpec((1, chunk), lambda j: (0, j)),
            pl.BlockSpec((ranks, chunk), lambda j: (0, j)),
            full(up_in.shape),
            pl.BlockSpec((chunk, wide), lambda j: (j, 0)),
            pl.BlockSpec((ranks, chunk), lambda j: (0, j)),
            full(down_out.shape),
        ]
        + [full(g.shape) for g in grads],
        out_specs=[
            full((half, wide)),
            full((half, wide)),
            full((rows, ranks)),
            full((rows, ranks)),
            pl.BlockSpec((rows, chunk), lambda j: (0, j)),
            pl.BlockSpec((rows, chunk), lambda j: (0, j)),
        ],
        scratch_shapes=[
            pltpu.VMEM((rows, wide), F32),
            pltpu.VMEM((rows, ranks), F32),
            pltpu.VMEM((rows, wide), BF),
        ],
        compiler_params=pltpu.CompilerParams(vmem_limit_bytes=LIMIT, dimension_semantics=("arbitrary",)),
        name=name,
    )(mask, normed, low2, up_w, up_b, up_out, up_in, down_w, down_in, down_out, *grads)


def down_body(count, mask, act_near, act_far, down_w, down_in, down_out, *refs):
    out_a, out_b, low_near, low_far = refs
    block = mask.shape[0] // count
    near = act_near.shape[0]
    for first, act, low_ref in ((0, act_near, low_near), (near, act_far, low_far)):
        for i in range(act.shape[0] // (2 * block)):
            part = pl.ds(i * 2 * block, 2 * block)
            rows = act[part, :]
            low = (dot_back(rows, down_in[...]) * mask[pl.ds(first + i * 2 * block, 2 * block), :]).astype(BF)
            low_ref[part, :] = low
            total = (dot(rows, down_w[...]) + dot(low, down_out[...])).astype(BF)
            spot = first // (2 * block) + i
            out_a[pl.ds(spot * block, block), :] = total[:block]
            out_b[pl.ds(spot * block, block), :] = total[block:]


def hidden_grads_body(
    count, low2_near, low2_far, gup_near, gup_far, gdl_near, gdl_far, act_near, act_far,
    lp2_near, lp2_far, n2_near, n2_far, dlow_near, dlow_far, *refs
):
    grads = refs[:count]
    up_out, down_in, up_in, down_out = refs[count:]
    block = grads[0].shape[0]
    up_out[...] = (
        dot_over(low2_near[...], gup_near[...]) + dot_over(low2_far[...], gup_far[...])
    ).astype(BF)
    down_in[...] = (
        dot_over(gdl_near[...], act_near[...]) + dot_over(gdl_far[...], act_far[...])
    ).astype(BF)
    up_in[...] = dot_over(lp2_near[...], n2_near[...]) + dot_over(lp2_far[...], n2_far[...])
    total = dot_over(dlow_near[pl.ds(0, block), :], grads[0][...])
    total = total + dot_over(dlow_near[pl.ds(block, block), :], grads[1][...])
    for i in range(2, count):
        total = total + dot_over(dlow_far[pl.ds((i - 2) * block, block), :], grads[i][...])
    down_out[...] = total


def mid_back_body(count, mask, cotangent, mid, gain, proj_out, *refs):
    pieces = refs[: count[0]]
    weight = refs[count[0] : count[0] + count[1]]
    low_in = refs[count[0] + count[1] : count[0] + 2 * count[1]]
    grad_mid, grad_attn, grad_low = refs[count[0] + 2 * count[1] : count[0] + 2 * count[1] + 3]
    outs = refs[count[0] + 2 * count[1] + 3 :]
    upstream = pieces[0][...].astype(F32)
    for piece in pieces[1:]:
        upstream = upstream + piece[...].astype(F32)
    unit, inv = norm_parts(mid[...])
    total = cotangent[...] + norm_back(unit, inv, upstream * gain[...])
    grad_mid[...] = total
    attn = total.astype(BF)
    grad_attn[...] = attn
    low = (dot_back(attn, proj_out[...]) * mask[...]).astype(BF)
    grad_low[...] = low
    for d in range(count[1]):
        outs[d][...] = (dot_back(attn, weight[d][...]) + dot(low, low_in[d][...])).astype(BF)


def message_body(count, index, up_in, down_out, proj_low, grad_attn, grad_low, *refs):
    attended = refs[:count]
    outs = refs[count : 2 * count]
    proj_out = refs[2 * count]
    rank = up_in.shape[0]
    block = grad_low.shape[0]
    width = outs[0].shape[1]
    proj_out[...] = dot_over(proj_low[...], grad_attn[...])
    start = pl.multiple_of(index[0] * block, block)
    for d in range(count):
        lanes = pl.ds(pl.multiple_of(index[d] * width, width), width)
        outs[d][pl.ds(0, rank), :] = up_in[:, lanes].astype(BF)
        outs[d][pl.ds(rank, rank), :] = down_out[:, lanes].astype(BF)
        outs[d][pl.ds(2 * rank, rank), :] = proj_out[:, lanes].astype(BF)
        outs[d][pl.ds(3 * rank, rank), :] = dot_over(
            grad_low[...], attended[d][pl.ds(start, block), :]
        ).astype(BF)


def pack_body(count, plain, pick, *refs):
    fixed = refs[:plain]
    messages = refs[plain : plain + count]
    out = refs[plain + count]
    rank = pick.shape[0]
    at = 0
    for ref in fixed:
        out[:, at : at + ref.shape[1]] = ref[...]
        at += ref.shape[1]
    width = messages[0].shape[1]
    for k in range(messages[0].shape[0] // rank):
        total = messages[0][pl.ds(k * rank, rank), :].astype(F32)
        for d in range(1, count):
            total = total + messages[d][pl.ds(k * rank, rank), :].astype(F32)
        out[:, at : at + width] = total.astype(BF)
        at += width
    out[:, at : at + pick.shape[1]] = pick[...]


def attend_back_body(count, lengths, order_col, seq, lse, *refs):
    grads = refs[:count]
    grad_q, grad_k, grad_v, grad_seq = refs[count:]
    rows = order_col.shape[0]
    block = grads[0].shape[0]
    width = grads[0].shape[1]
    seqs = lengths.shape[0]
    seq_len = rows // seqs
    heads = width // HD
    step = min(256, seq_len)
    scale = 1.0 / math.sqrt(HD)
    for s in range(seqs):
        part = pl.ds(s * seq_len, seq_len)
        col = order_col[part, :]
        moved = dot(one_hot_rows(col, rows, 0, block), grads[0][...])
        for i in range(1, count):
            moved = moved + dot(one_hot_rows(col, rows, i * block, (i + 1) * block), grads[i][...])
        grad_seq[part, :] = moved.astype(BF)
    for s in range(seqs):
        base = s * seq_len
        length = lengths[s]
        for pair in range(heads // 2):
            lanes = pl.ds(pair * PAIR, PAIR)
            keys = seq[pl.ds(base, seq_len), pl.ds(width + pair * PAIR, PAIR)]
            values = seq[pl.ds(base, seq_len), pl.ds(2 * width + pair * PAIR, PAIR)]
            keys_t = keys.astype(F32).T.astype(BF)
            steps = seq_len // step
            sums_k = [None] * steps
            sums_v = [None] * steps
            for q in range(steps):
                queries = seq[pl.ds(base + q * step, step), lanes]
                grad = grad_seq[pl.ds(base + q * step, step), lanes]
                seen = (q + 1) * step
                limit = key_limit(q * step, step, length)
                at = lax.broadcasted_iota(jnp.int32, (seen, step), 0)
                allowed = at < limit
                for h in range(2):
                    head = pair * 2 + h
                    own_q = head_lanes(queries, h)
                    own_g = head_lanes(grad, h)
                    scores = dot_back(keys[:seen], own_q)
                    log_total = lse[pl.ds(head, 1), pl.ds(base + q * step, step)]
                    probs = jnp.exp(jnp.where(allowed, scores, NEGATIVE) - log_total)
                    grad_probs = dot_back(values[:seen], own_g)
                    mixed = probs * grad_probs
                    centre = jnp.sum(mixed, 0, keepdims=True)
                    raw = (mixed - probs * centre).astype(BF)
                    grad_q[pl.ds(head * HD, HD), pl.ds(base + q * step, step)] = (
                        dot(keys_t[h * HD : (h + 1) * HD, :seen], raw) * scale
                    ).astype(BF)
                    to_k = dot(raw, own_q)
                    to_v = dot(probs.astype(BF), own_g)
                    for b in range(q + 1):
                        cut = slice(b * step, (b + 1) * step)
                        sums_k[b] = to_k[cut] if sums_k[b] is None else sums_k[b] + to_k[cut]
                        sums_v[b] = to_v[cut] if sums_v[b] is None else sums_v[b] + to_v[cut]
            for b in range(steps):
                grad_k[pl.ds(base + b * step, step), lanes] = sums_k[b].astype(BF)
                grad_v[pl.ds(base + b * step, step), lanes] = sums_v[b].astype(BF)


def qkv_back_body(first, count, order_row, mask, weight, low_in, low_out, grad_q, grad_k, grad_v, *refs):
    out_a, out_b, low_part, grad_ref = refs
    block = low_part.shape[0] // count
    width = grad_k.shape[1]
    for i in range(count):
        begin = first + i * block
        place = one_hot_cols(order_row[...], begin, begin + block)
        parts = (
            dot_back(place, grad_q[...]).astype(BF),
            dot(place, grad_k[...]).astype(BF),
            dot(place, grad_v[...]).astype(BF),
        )
        total = dot_back(parts[0], weight[0])
        low = dot_back(parts[0], low_out[0])
        for k in range(1, 3):
            total = total + dot_back(parts[k], weight[k])
            low = low + dot_back(parts[k], low_out[k])
        rows = pl.ds(i * block, block)
        for k in range(3):
            grad_ref[rows, k * width : (k + 1) * width] = parts[k]
        low = (low * mask[pl.ds(begin, block), :]).astype(BF)
        low_part[rows, :] = low
        total = (total + dot(low, low_in[...])).astype(BF)
        target = out_a if i % 2 == 0 else out_b
        target[pl.ds((i // 2) * block, block), :] = total


def qkv_grads_body(
    count, index, low_near, low_far, grad_near, grad_far, part_near, part_far, n1_near, n1_far, *refs
):
    qkv_out = refs[0]
    outs = refs[1 : 1 + count]
    total_in = refs[1 + count]
    width = outs[0].shape[1]
    qkv_out[...] = (
        dot_over(low_near[...], grad_near[...]) + dot_over(low_far[...], grad_far[...])
    ).astype(BF)
    total_in[...] = dot_over(part_near[...], n1_near[...]) + dot_over(part_far[...], n1_far[...])
    for d in range(count):
        lanes = pl.ds(pl.multiple_of(index[d] * width, width), width)
        outs[d][...] = total_in[:, lanes].astype(BF)


def input_back_body(tokens, grad_mid, gain, *refs):
    out = refs[-1]
    upstream = refs[0][...].astype(F32)
    for piece in refs[1:-1]:
        upstream = upstream + piece[...].astype(F32)
    unit, inv = norm_parts(tokens[...].astype(F32))
    out[...] = grad_mid[...] + norm_back(unit, inv, upstream * gain[...])


def result_body(mid, bias, *refs):
    out = refs[-1]
    total = mid[...] + bias[...]
    for piece in refs[:-1]:
        total = total + piece[...].astype(F32)
    out[...] = total


def spread_body(hid, width, early, late, up_out, down_in, proj_in, qkv_out, wide):
    cols = early.shape[1]
    pick = early[:, cols - 128 :]
    up_out[...] = dot_over(pick, early[:, :hid])
    down_in[...] = dot_over(early[:, hid : 2 * hid], pick)
    at = 2 * hid
    wide[pl.ds(0, 128), :] = dot_over(pick, early[:, at : at + width]).astype(BF)
    wide[pl.ds(128, 128), :] = dot_over(pick, early[:, at + width : at + 2 * width]).astype(BF)
    wide[pl.ds(256, 128), :] = dot_over(pick, early[:, at + 2 * width : at + 3 * width]).astype(BF)
    proj_in[...] = dot_over(early[:, at + 3 * width : at + 4 * width], pick)
    pick = late[:, 4 * width :]
    qkv_out[...] = dot_over(pick, late[:, : 3 * width])
    wide[pl.ds(384, 128), :] = dot_over(pick, late[:, 3 * width : 4 * width]).astype(BF)


def place_body(count, index, *refs):
    messages = refs[:count]
    up_in, down_out, proj_out, qkv_in = refs[count:]
    width = messages[0].shape[1]
    for d in range(count):
        start = pl.multiple_of(index[d] * width, width)
        span = pl.ds(start, width)
        up_in[span, :] = messages[d][pl.ds(0, 128), :].astype(F32).T
        down_out[:, span] = messages[d][pl.ds(128, 128), :].astype(F32)
        proj_out[:, span] = messages[d][pl.ds(256, 128), :].astype(F32)
        qkv_in[span, :] = messages[d][pl.ds(384, 128), :].astype(F32).T


def body(
    tensor_size,
    dp_size,
    tokens,
    cotangent,
    lengths,
    order,
    adapter_ids,
    norm1_gain,
    norm1_shift,
    qkv_weight,
    qv_bias,
    proj_weight,
    proj_bias,
    norm2_gain,
    norm2_shift,
    up_weight,
    up_bias,
    down_weight,
    down_bias,
    adapt_qkv_in,
    adapt_qkv_out,
    adapt_proj_in,
    adapt_proj_out,
    adapt_up_in,
    adapt_up_out,
    adapt_down_in,
    adapt_down_out,
):
    count = tensor_size
    chips = count // 2
    own, wide = tokens.shape
    width = qkv_weight.shape[2]
    hid = up_weight.shape[1]
    rows = order.shape[1]
    seqs = lengths.shape[1]
    seq_len = rows // seqs
    ranks = seqs * RANK
    near = 2 * own
    far = rows - near
    cols = adapt_qkv_in.shape[1]
    me = lax.axis_index("tensor")

    core_perm = [(t, t ^ 1) for t in range(count)]

    def hop(k):
        return [(t, ((t // 2 + k) % chips) * 2 + t % 2) for t in range(count)]

    def core_swap(value):
        return lax.ppermute(value, "tensor", core_perm)

    def chip_hop(value, k):
        return lax.ppermute(value, "tensor", hop(k % chips))

    def gather(value):
        found = [value, core_swap(value)]
        for k in range(1, chips):
            moved = chip_hop(value, k)
            found += [moved, core_swap(moved)]
        return found

    def exchange(messages):
        got = [messages[0], core_swap(messages[1])]
        for k in range(1, chips):
            flat = [(t, ((t // 2 - k) % chips) * 2 + t % 2) for t in range(count)]
            cross = [(t, ((t // 2 - k) % chips) * 2 + (t % 2 ^ 1)) for t in range(count)]
            back = chips - k
            got_flat = lax.ppermute(messages[2 * k], "tensor", flat)
            got_cross = lax.ppermute(messages[2 * k + 1], "tensor", cross)
            got.append((2 * back, got_flat))
            got.append((2 * back + 1, got_cross))
        out = list(got[:2]) + [None] * (count - 2)
        for slot, value in got[2:]:
            out[slot] = value
        return out

    def reduce_far(part_a, part_b):
        received = core_swap(part_b)
        joined = (part_a.astype(F32) + received.astype(F32)).astype(BF)
        return [chip_hop(joined[(k - 1) * own : k * own], -k) for k in range(1, chips)]

    relative = jnp.arange(count, dtype=jnp.int32)
    index = ((me // 2 - relative // 2) % chips) * 2 + ((me % 2) ^ (relative % 2))
    order_row = order
    owner = order_row // own
    hops = (me // 2 - owner // 2) % chips
    order_rel = (hops * 2 + ((me % 2) ^ (owner % 2))) * own + order_row % own
    order_col = order_rel.reshape(rows, 1)
    ids = adapter_ids[0]
    lengths_row = lengths[0]

    slot_seq = jnp.arange(rows, dtype=jnp.int32) // seq_len
    seq_of = jnp.sum(
        jnp.where(order_rel == jnp.arange(rows, dtype=jnp.int32)[:, None], slot_seq[None, :], 0), axis=1
    )
    lane_seq = jnp.arange(ranks, dtype=jnp.int32) // RANK
    mask = (seq_of[:, None] == lane_seq[None, :]).astype(F32)
    target = jnp.repeat(ids, RANK) * RANK + jnp.arange(ranks, dtype=jnp.int32) % RANK
    pick = (target[:, None] == jnp.arange(cols, dtype=jnp.int32)[None, :]).astype(BF)
    bias_three = jnp.stack([qv_bias[0], jnp.zeros_like(qv_bias[0]), qv_bias[1]])
    weight_three = jnp.transpose(qkv_weight, (1, 0, 2))
    out_three = jnp.transpose(adapt_qkv_out, (1, 0, 2))
    row = lambda v: v.reshape(1, -1)

    token_blocks = gather(tokens)
    grad_mlp = cotangent.astype(BF)
    grad_mlp_tied, _ = lax.optimization_barrier((grad_mlp, token_blocks[2]))
    proj_tied, proj_in_tied, _ = lax.optimization_barrier((proj_weight, adapt_proj_in, token_blocks[2]))

    c_qkv_in, c_qkv_out, c_proj_in, c_proj_out, c_up_in, c_up_out, c_down_in, c_down_out = whole_call(
        prep_body,
        [pick, adapt_qkv_in, out_three, adapt_proj_in, adapt_proj_out, adapt_up_in, adapt_up_out,
         adapt_down_in, adapt_down_out],
        [shape((ranks, wide), BF), shape((3, ranks, width), BF), shape((ranks, width), BF),
         shape((ranks, wide), BF), shape((ranks, wide), BF), shape((ranks, hid), BF),
         shape((ranks, hid), BF), shape((ranks, wide), BF)],
        "prep",
    )
    proj_blocks = gather(proj_tied)
    proj_in_blocks = gather(c_proj_in)

    def project(blocks, keep, name):
        size = len(blocks) * own
        return whole_call(
            functools.partial(qkv_body, len(blocks)),
            [keep, row(norm1_gain), row(norm1_shift), weight_three, bias_three, c_qkv_in, c_qkv_out] + blocks,
            [shape((size, wide), BF), shape((size, ranks), BF), shape((size, 3 * width), BF)],
            name,
        )

    n1_near, low1_near, qkv_near = project(token_blocks[:2], mask[:near], "qkv_near")
    n1_far, low1_far, qkv_far = project(token_blocks[2:], mask[near:], "qkv_far")

    heads = width // HD
    attended, qkv_seq, lse = whole_call(
        functools.partial(attend_body, own),
        [order_rel, order_col, qkv_near, qkv_far],
        [shape((rows, width), BF), shape((rows, 3 * width), BF), shape((max(heads, 8), rows), F32)],
        "attend",
        smem=[lengths_row, index],
        scratch=[pltpu.VMEM((width, rows), BF)],
    )
    attended_blocks = gather(attended)
    grad_blocks = gather(grad_mlp_tied)

    n2_near, n2_far, low2_near, low2_far, proj_low, mid = whole_call(
        functools.partial(mid_body, count),
        [mask, c_proj_out, row(proj_bias), row(norm2_gain), row(norm2_shift), c_up_in]
        + token_blocks + attended_blocks + proj_blocks + proj_in_blocks,
        [shape((near, wide), BF), shape((far, wide), BF), shape((near, ranks), BF), shape((far, ranks), BF),
         shape((own, ranks), BF), shape((own, wide), F32)],
        "mid",
        smem=[index],
    )

    weights = (up_weight, row(up_bias), c_up_out, c_up_in, down_weight, c_down_in, c_down_out)
    far_a, far_b, lp2_far, gdl_far, act_far, gup_far = hidden_call(
        mask[near:], n2_far, low2_far, grad_blocks[2:], *weights, name="hidden_far"
    )
    up_far = reduce_far(far_a, far_b)
    near_a, near_b, lp2_near, gdl_near, act_near, gup_near = hidden_call(
        mask[:near], n2_near, low2_near, grad_blocks[:2], *weights, name="hidden_near"
    )
    up_pieces = [near_a, core_swap(near_b)] + up_far

    down_a, down_b, dlow_near, dlow_far = whole_call(
        functools.partial(down_body, count),
        [mask, act_near, act_far, down_weight, c_down_in, c_down_out],
        [shape((rows // 2, wide), BF), shape((rows // 2, wide), BF), shape((near, ranks), BF), shape((far, ranks), BF)],
        "down",
    )
    g_up_out, g_down_in, p_up_in, p_down_out = whole_call(
        functools.partial(hidden_grads_body, count),
        [low2_near, low2_far, gup_near, gup_far, gdl_near, gdl_far, act_near, act_far, lp2_near, lp2_far,
         n2_near, n2_far, dlow_near, dlow_far] + grad_blocks,
        [shape((ranks, hid), BF), shape((ranks, hid), BF), shape((ranks, wide), F32), shape((ranks, wide), F32)],
        "hidden_grads",
    )

    mid_back = whole_call(
        functools.partial(mid_back_body, (len(up_pieces), count)),
        [mask[:own], cotangent, mid, row(norm2_gain), c_proj_out] + up_pieces + proj_blocks + proj_in_blocks,
        [shape((own, wide), F32), shape((own, wide), BF), shape((own, ranks), BF)]
        + [shape((own, width), BF)] * count,
        "mid_back",
    )
    grad_mid, grad_attn, grad_proj_low = mid_back[:3]
    grad_att_blocks = exchange(mid_back[3:])

    down_tied_a, down_tied_b, _ = lax.optimization_barrier((down_a, down_b, grad_att_blocks[count - 1]))
    down_pieces = [down_tied_a[:own], core_swap(down_tied_b[:own])] + reduce_far(
        down_tied_a[own:], down_tied_b[own:]
    )
    (result,) = whole_call(
        result_body, [mid, row(down_bias)] + down_pieces, [shape((own, wide), F32)], "result"
    )

    messages = whole_call(
        functools.partial(message_body, count),
        [p_up_in, p_down_out, proj_low, grad_attn, grad_proj_low] + attended_blocks,
        [shape((4 * ranks, width), BF)] * count,
        "message",
        smem=[index],
        scratch=[pltpu.VMEM((ranks, wide), F32)],
    )
    messages, _ = lax.optimization_barrier((messages, grad_att_blocks[count - 1]))
    messages = exchange(messages)
    (early,) = whole_call(
        functools.partial(pack_body, count, 2),
        [pick, g_up_out, g_down_in] + messages,
        [shape((ranks, 2 * hid + 4 * width + cols), BF)],
        "pack_early",
    )
    early_all = lax.all_gather(early, "dp", axis=0, tiled=True)

    grad_q, grad_k, grad_v = whole_call(
        functools.partial(attend_back_body, count),
        [order_col, qkv_seq, lse] + grad_att_blocks,
        [shape((width, rows), BF), shape((rows, width), BF), shape((rows, width), BF)],
        "attend_back",
        smem=[lengths_row],
        scratch=[pltpu.VMEM((rows, width), BF)],
    )

    def unproject(first, blocks, name):
        size = blocks * own
        return whole_call(
            functools.partial(qkv_back_body, first, blocks),
            [order_rel, mask, weight_three, c_qkv_in, c_qkv_out, grad_q, grad_k, grad_v],
            [shape((size // 2, wide), BF), shape((size // 2, wide), BF), shape((size, ranks), BF),
             shape((size, 3 * width), BF)],
            name,
        )

    far_a, far_b, part1_far, gqkv_far = unproject(near, count - 2, "qkv_back_far")
    qkv_far_pieces = reduce_far(far_a, far_b)
    near_a, near_b, part1_near, gqkv_near = unproject(0, 2, "qkv_back_near")
    qkv_pieces = [near_a, core_swap(near_b)] + qkv_far_pieces

    late = whole_call(
        functools.partial(qkv_grads_body, count),
        [low1_near, low1_far, gqkv_near, gqkv_far, part1_near, part1_far, n1_near, n1_far],
        [shape((ranks, 3 * width), BF)] + [shape((ranks, width), BF)] * count,
        "qkv_grads",
        smem=[index],
        scratch=[pltpu.VMEM((ranks, wide), F32)],
    )
    late_messages = exchange(late[1:])
    (gathered,) = whole_call(
        functools.partial(pack_body, count, 1),
        [pick, late[0]] + late_messages,
        [shape((ranks, 4 * width + cols), BF)],
        "pack_late",
    )
    stride = dp_size // 2
    while stride:
        moved = lax.ppermute(gathered, "dp", [(i, i ^ stride) for i in range(dp_size)])
        gathered = jnp.concatenate([gathered, moved], 0)
        stride //= 2

    (grad_input,) = whole_call(
        input_back_body, [tokens, grad_mid, row(norm1_gain)] + qkv_pieces, [shape((own, wide), F32)], "input_back"
    )

    up_out_full, down_in_full, proj_in_full, qkv_out_full, wide_part = whole_call(
        functools.partial(spread_body, hid, width),
        [early_all, gathered],
        [shape((cols, hid), F32), shape((hid, cols), F32), shape((width, cols), F32),
         shape((cols, 3 * width), F32), shape((4 * cols, width), BF)],
        "spread",
    )
    wide_blocks = gather(wide_part)
    up_in_full, down_out_full, proj_out_full, qkv_in_full = whole_call(
        functools.partial(place_body, count),
        wide_blocks,
        [shape((wide, cols), F32), shape((cols, wide), F32), shape((cols, wide), F32), shape((wide, cols), F32)],
        "place",
        smem=[index],
    )
    return (
        result,
        grad_input,
        qkv_in_full,
        qkv_out_full.reshape(cols, 3, width),
        proj_in_full,
        proj_out_full,
        up_in_full,
        up_out_full,
        down_in_full,
        down_out_full,
    )


def solution(mesh):
    in_specs = (
        P(("dp", "tensor"), None),
        P(("dp", "tensor"), None),
        P("dp", None),
        P("dp", None),
        P("dp", None),
        P(),
        P(),
        P(None, None, "tensor"),
        P(None, "tensor"),
        P("tensor", None),
        P(),
        P(),
        P(),
        P(None, "tensor"),
        P("tensor"),
        P("tensor", None),
        P(),
        P(),
        P(None, None, "tensor"),
        P("tensor", None),
        P(),
        P(),
        P(None, "tensor"),
        P("tensor", None),
        P(),
    )
    out_specs = (
        P(("dp", "tensor"), None),
        P(("dp", "tensor"), None),
        P(),
        P(None, None, "tensor"),
        P("tensor", None),
        P(),
        P(),
        P(None, "tensor"),
        P("tensor", None),
        P(),
    )
    run = functools.partial(body, mesh.shape["tensor"], mesh.shape["dp"])
    return jax.shard_map(run, mesh=mesh, in_specs=in_specs, out_specs=out_specs, check_vma=False)
```

```python
import functools
import math

import jax
import jax.numpy as jnp
from jax import lax
from jax.experimental import pallas as pl
from jax.experimental.pallas import tpu as pltpu
from jax.sharding import PartitionSpec as P

HD = 64
RANK = 16
PAIR = 2 * HD
EPSILON = 1e-05
NEGATIVE = -1000000000.0
BF = jnp.bfloat16
F32 = jnp.float32
LIMIT = 14 * 1024 * 1024
GELU_A = math.sqrt(2.0 / math.pi)
GELU_B = 0.044715


def dot(left, right):
    return jnp.dot(left, right, preferred_element_type=F32)


def dot_back(left, right):
    return lax.dot_general(left, right, (((1,), (1,)), ((), ())), preferred_element_type=F32)


def dot_over(left, right):
    return lax.dot_general(left, right, (((0,), (0,)), ((), ())), preferred_element_type=F32)


def shape(dims, kind):
    return jax.ShapeDtypeStruct(tuple(dims), kind)


def whole_call(body, inputs, outs, name, smem=(), scratch=(), final=(), loose=()):
    smem_spec = pl.BlockSpec(memory_space=pltpu.SMEM)
    vmem_spec = pl.BlockSpec(memory_space=pltpu.VMEM)
    held = [x if i in loose else pltpu.with_memory_space_constraint(x, pltpu.VMEM) for i, x in enumerate(inputs)]
    kinds = [o if i in final else pltpu.VMEM(o.shape, o.dtype) for i, o in enumerate(outs)]
    return pl.pallas_call(
        body,
        out_shape=kinds,
        in_specs=[smem_spec] * len(smem) + [vmem_spec] * len(inputs),
        out_specs=[vmem_spec] * len(outs),
        scratch_shapes=list(scratch),
        compiler_params=pltpu.CompilerParams(vmem_limit_bytes=LIMIT),
        name=name,
    )(*smem, *held)


def norm_parts(values):
    centre = values - jnp.mean(values, -1, keepdims=True)
    spread = jnp.mean(centre * centre, -1, keepdims=True)
    inv = lax.rsqrt(spread + EPSILON)
    return centre * inv, inv


def norm_back(normed, inv, upstream):
    return inv * (
        upstream
        - jnp.mean(upstream, -1, keepdims=True)
        - normed * jnp.mean(upstream * normed, -1, keepdims=True)
    )


def prep_body(
    seq_len, order_row, order_col, pick, qkv_in, qkv_out, proj_in, proj_out, up_in, up_out, down_in, down_out, *outs
):
    o_qkv_in, o_qkv_out, o_proj_in, o_proj_out, o_up_in, o_up_out, o_down_in, o_down_out = outs[:8]
    pull_near, pull_far, push, mask = outs[8:]
    chosen = pick[...]
    o_proj_in[...] = dot_back(chosen, proj_in[...]).astype(BF)
    o_qkv_in[...] = dot_back(chosen, qkv_in[...]).astype(BF)
    for k in range(3):
        o_qkv_out[k] = dot(chosen, qkv_out[k]).astype(BF)
    o_proj_out[...] = dot(chosen, proj_out[...]).astype(BF)
    o_up_in[...] = dot_back(chosen, up_in[...]).astype(BF)
    o_up_out[...] = dot(chosen, up_out[...]).astype(BF)
    o_down_in[...] = dot_back(chosen, down_in[...]).astype(BF)
    o_down_out[...] = dot(chosen, down_out[...]).astype(BF)
    near = pull_near.shape[1]
    rows = push.shape[0]
    for ref, start in ((pull_near, 0), (pull_far, near)):
        at = lax.broadcasted_iota(jnp.int32, ref.shape, 1) + start
        ref[...] = jnp.where(at == order_col[...], 1.0, 0.0).astype(BF)
    at = lax.broadcasted_iota(jnp.int32, (rows, rows), 0)
    push[...] = jnp.where(at == order_row[...], 1.0, 0.0).astype(BF)
    seq_at = lax.broadcasted_iota(jnp.int32, mask.shape, 0) // seq_len
    lane_at = lax.broadcasted_iota(jnp.int32, mask.shape, 1) // RANK
    mask[...] = dot(push[...], jnp.where(seq_at == lane_at, 1.0, 0.0).astype(BF))


def qkv_body(ids, last, mask, gain, shift, weight, bias, low_in, low_out, pull, *refs):
    count = len(ids)
    blocks = refs[:count]
    rest = refs[count:]
    earlier = None
    if last:
        earlier, rest = rest[0], rest[1:]
    normed_ref, low_ref, moved_ref, joined = rest
    rows = blocks[0].shape[0]
    width = weight.shape[2]
    for i in range(count):
        part = pl.ds(i * rows, rows)
        unit, _ = norm_parts(blocks[i][...].astype(F32))
        normed = (unit * gain[...] + shift[...]).astype(BF)
        normed_ref[part, :] = normed
        low = (dot_back(normed, low_in[...]) * mask[pl.ds(ids[i] * rows, rows), :]).astype(BF)
        low_ref[part, :] = low
        for k in range(3):
            value = dot(normed, weight[k]) + dot(low, low_out[k])
            if k != 1:
                value = value + bias[k // 2 : k // 2 + 1, :]
            joined[part, k * width : (k + 1) * width] = value.astype(BF)
    total = moved_ref.shape[0]
    step = min(256, total)
    for i in range(total // step):
        part = pl.ds(i * step, step)
        moved = dot(pull[part, :], joined[...])
        if last:
            moved = moved + earlier[part, :]
            moved_ref[part, :width] = (moved[:, :width] * (1.0 / math.sqrt(HD))).astype(BF)
            moved_ref[part, width:] = moved[:, width:].astype(BF)
        else:
            moved_ref[part, :] = moved


def head_lanes(values, head):
    lane = lax.broadcasted_iota(jnp.int32, values.shape, 1)
    return jnp.where((lane // HD) == head, values, jnp.zeros_like(values))


def attend_body(seq_len, pair, limit, seq, push, out, lse, turned):
    rows = seq.shape[0]
    width = seq.shape[1] // 3
    step = min(256, seq_len)
    for s in range(rows // seq_len):
        base = s * seq_len
        keys = seq[pl.ds(base, seq_len), pl.ds(width + pair * PAIR, PAIR)]
        values = seq[pl.ds(base, seq_len), pl.ds(2 * width + pair * PAIR, PAIR)]
        values_t = values.astype(F32).T.astype(BF)
        for q in range(seq_len // step):
            span = pl.ds(base + q * step, step)
            queries = seq[span, pl.ds(pair * PAIR, PAIR)]
            seen = (q + 1) * step
            allowed = lax.broadcasted_iota(jnp.int32, (seen, step), 0) < limit[:, span]
            for h in range(2):
                scores = dot_back(keys[:seen], head_lanes(queries, h))
                scores = jnp.where(allowed, scores, NEGATIVE)
                top = jnp.max(scores, 0, keepdims=True)
                weights = jnp.exp(scores - top)
                total = jnp.sum(weights, 0, keepdims=True)
                probs = (weights * (1.0 / total)).astype(BF)
                turned[pl.ds(h * HD, HD), span] = dot(values_t[h * HD : (h + 1) * HD, :seen], probs).astype(BF)
                lse[pl.ds(h, 1), span] = top + jnp.log(total)
    out[...] = dot_back(push[...], turned[...]).astype(BF)


def join_body(count, low_near, low_far, push, weight, *refs):
    proj = refs[:count]
    low_in = refs[count : 2 * count]
    w_all, in_all, w_cat, low_t = refs[2 * count :]
    width = proj[0].shape[0]
    near = low_near.shape[0]
    for d in range(count):
        w_all[pl.ds(d * width, width), :] = proj[d][...]
        in_all[:, d * width : (d + 1) * width] = low_in[d][...]
    for k in range(3):
        w_cat[:, k * width : (k + 1) * width] = weight[k]
    rows = push.shape[0]
    low_t[...] = (
        dot_over(low_near[...], push[pl.ds(0, near), :]) + dot_over(low_far[...], push[pl.ds(near, rows - near), :])
    ).astype(BF)


def place_of(block, sender, chips):
    return ((block // 2 - sender // 2) % chips) * 2 + ((block % 2) ^ (sender % 2))


def block_body(
    ids, count, pairs, chunk, mask, w_all, in_all, proj_out, proj_bias, gain, shift, up_in, up_w, up_b, up_out,
    down_w, down_in, down_out, *refs
):
    size = len(ids)
    tokens = refs[:size]
    grads = refs[size : 2 * size]
    attended = refs[2 * size : 2 * size + count * pairs]
    rest = refs[2 * size + count * pairs :]
    outs = rest[: len(rest) - 3]
    heads, grad_all, acc = rest[len(rest) - 3 :]
    part_ref, normed_ref, low_ref, low_part, grad_down_low, act_ref, gup_ref, down_low = outs[:8]
    block = tokens[0].shape[0]
    width = in_all.shape[1] // count
    for i in range(size):
        part = pl.ds(i * block, block)
        for d in range(count):
            spot = place_of(ids[i], d, count // 2) * block
            for p in range(pairs):
                at = d * width + p * PAIR
                heads[part, at : at + PAIR] = attended[d * pairs + p][pl.ds(spot, block), :]
        keep = mask[pl.ds(ids[i] * block, block), :]
        grad = grads[i][...]
        grad_all[part, :] = grad
        grad_down_low[part, :] = (dot_back(grad, down_out[...]) * keep).astype(BF)
        rows = heads[part, :]
        low = (dot_back(rows, in_all[...]) * keep).astype(BF)
        mid = dot(rows, w_all[...]) + dot(low, proj_out[...]) + proj_bias[...] + tokens[i][...].astype(F32)
        unit, _ = norm_parts(mid)
        normed = (unit * gain[...] + shift[...]).astype(BF)
        normed_ref[part, :] = normed
        low_ref[part, :] = (dot_back(normed, up_in[...]) * keep).astype(BF)
        if len(outs) > 8 and i == 0:
            outs[8][...] = low
            outs[9][...] = mid
    low_sum = None
    down_sum = None
    hid = up_w.shape[1]
    for j in range(hid // chunk):
        cut = pl.ds(j * chunk, chunk)
        upper = dot(normed_ref[...], up_w[:, cut]) + dot(low_ref[...], up_out[:, cut]) + up_b[:, cut]
        grad = dot_back(grad_all[...], down_w[cut, :]) + dot(grad_down_low[...], down_in[:, cut])
        square = upper * upper
        curve = jnp.tanh(GELU_A * upper * (1.0 + GELU_B * square))
        half = 0.5 * (1.0 + curve)
        active = (upper * half).astype(BF)
        act_ref[:, cut] = active
        slope = half + 0.5 * upper * (1.0 - curve * curve) * (GELU_A * (1.0 + 3.0 * GELU_B * square))
        grad_upper = (grad * slope).astype(BF)
        gup_ref[:, cut] = grad_upper
        part = dot_back(grad_upper, up_w[:, cut])
        low = dot_back(grad_upper, up_out[:, cut])
        down = dot_back(active, down_in[:, cut])
        acc[...] = part if j == 0 else acc[...] + part
        low_sum = low if j == 0 else low_sum + low
        down_sum = down if j == 0 else down_sum + down
    for i in range(size):
        cut = slice(i * block, (i + 1) * block)
        part = pl.ds(i * block, block)
        keep = mask[pl.ds(ids[i] * block, block), :]
        low = (low_sum[cut] * keep).astype(BF)
        low_part[part, :] = low
        down_low[part, :] = (down_sum[cut] * keep).astype(BF)
        part_ref[part, :] = (acc[part, :] + dot(low, up_in[...])).astype(BF)


def down_body(groups, down_w, down_out, *refs):
    for g in range(groups):
        act, low, out = refs[g], refs[groups + g], refs[2 * groups + g]
        out[...] = (dot(act[...], down_w[...]) + dot(low[...], down_out[...])).astype(BF)


def hidden_grads_body(groups, sizes, pick, *refs):
    low2 = refs[:groups]
    gup = refs[groups : 2 * groups]
    gdl = refs[2 * groups : 3 * groups]
    act = refs[3 * groups : 4 * groups]
    part = refs[4 * groups : 5 * groups]
    normed = refs[5 * groups : 6 * groups]
    down = refs[6 * groups : 7 * groups]
    rest = refs[7 * groups :]
    total = sum(sizes)
    grads = rest[:total]
    pack, up_in, down_out = rest[total:]
    hid = gup[0].shape[1]
    block = grads[0].shape[0]
    add = lambda left, right: sum([dot_over(a[...], b[...]) for a, b in zip(left[1:], right[1:])], dot_over(left[0][...], right[0][...]))
    pack[:, :hid] = add(low2, gup).astype(BF)
    pack[:, hid : 2 * hid] = add(gdl, act).astype(BF)
    pack[:, 2 * hid :] = pick[...]
    up_in[...] = add(part, normed)
    at = 0
    out = None
    for g in range(groups):
        for i in range(sizes[g]):
            term = dot_over(down[g][pl.ds(i * block, block), :], grads[at][...])
            out = term if out is None else out + term
            at += 1
    down_out[...] = out


def add_body(left, right, out):
    out[...] = (left[...].astype(F32) + right[...].astype(F32)).astype(BF)


def mid_back_body(count, mask, cotangent, mid, gain, proj_out, w_all, in_all, *refs):
    pieces = refs[: count[0]]
    grad_mid, grad_attn, grad_low = refs[count[0] : count[0] + 3]
    outs = refs[count[0] + 3 :]
    block = mid.shape[0]
    upstream = pieces[0][pl.ds(0, block), :].astype(F32)
    for piece in pieces[1:]:
        upstream = upstream + piece[...].astype(F32)
    unit, inv = norm_parts(mid[...])
    total = cotangent[...] + norm_back(unit, inv, upstream * gain[...])
    grad_mid[...] = total
    attn = total.astype(BF)
    grad_attn[...] = attn
    low = (dot_back(attn, proj_out[...]) * mask[pl.ds(0, block), :]).astype(BF)
    grad_low[...] = low
    value = (dot_back(attn, w_all[...]) + dot(low, in_all[...])).astype(BF)
    width = outs[0].shape[1]
    for d in range(count[1]):
        outs[d][...] = value[:, d * width : (d + 1) * width]


def message_body(count, pairs, index, up_in, down_out, proj_low, grad_attn, grad_low, *refs):
    attended = refs[: count * pairs]
    outs = refs[count * pairs : count * pairs + count]
    proj_out = refs[count * pairs + count]
    rank = up_in.shape[0]
    block = grad_low.shape[0]
    width = outs[0].shape[1]
    proj_out[...] = dot_over(proj_low[...], grad_attn[...])
    for d in range(count):
        spot = place_of(0, d, count // 2) * block
        lanes = pl.ds(pl.multiple_of(index[d] * width, width), width)
        outs[d][pl.ds(0, rank), :] = up_in[:, lanes].astype(BF)
        outs[d][pl.ds(rank, rank), :] = down_out[:, lanes].astype(BF)
        outs[d][pl.ds(2 * rank, rank), :] = proj_out[:, lanes].astype(BF)
        for p in range(pairs):
            outs[d][pl.ds(3 * rank, rank), p * PAIR : (p + 1) * PAIR] = dot_over(
                grad_low[...], attended[d * pairs + p][pl.ds(spot, block), :]
            ).astype(BF)


def pack_body(count, plain, pick, *refs):
    fixed = refs[:plain]
    messages = refs[plain : plain + count]
    out = refs[plain + count]
    rank = pick.shape[0]
    at = 0
    for ref in fixed:
        out[:, at : at + ref.shape[1]] = ref[...]
        at += ref.shape[1]
    width = messages[0].shape[1]
    for k in range(messages[0].shape[0] // rank):
        total = messages[0][pl.ds(k * rank, rank), :].astype(F32)
        for d in range(1, count):
            total = total + messages[d][pl.ds(k * rank, rank), :].astype(F32)
        out[:, at : at + width] = total.astype(BF)
        at += width
    out[:, at : at + pick.shape[1]] = pick[...]


def attend_back_body(
    count, pairs, seq_len, index, limit, seq, pull_near, pull_far, push, low_t, n1_near, n1_far, low_out, *refs
):
    lse = refs[:pairs]
    grads = refs[pairs : pairs + count]
    grad_q, grad_k, grad_v, part_t, qkv_out = refs[pairs + count : pairs + count + 5]
    messages = refs[pairs + count + 5 : pairs + 2 * count + 5]
    grad_seq, grad_all, part_seq, total_in = refs[pairs + 2 * count + 5 :]
    rows = seq.shape[0]
    block = grads[0].shape[0]
    width = grads[0].shape[1]
    near = pull_near.shape[1]
    step = min(256, seq_len)
    scale = 1.0 / math.sqrt(HD)
    for i in range(count):
        grad_all[pl.ds(i * block, block), :] = grads[i][...]
    grad_seq[...] = (
        dot(pull_near[...], grad_all[pl.ds(0, near), :]) + dot(pull_far[...], grad_all[pl.ds(near, rows - near), :])
    ).astype(BF)
    for s in range(rows // seq_len):
        base = s * seq_len
        for pair in range(pairs):
            lanes = pl.ds(pair * PAIR, PAIR)
            keys = seq[pl.ds(base, seq_len), pl.ds(width + pair * PAIR, PAIR)]
            values = seq[pl.ds(base, seq_len), pl.ds(2 * width + pair * PAIR, PAIR)]
            keys_t = keys.astype(F32).T.astype(BF)
            steps = seq_len // step
            sums_k = [None] * steps
            sums_v = [None] * steps
            for q in range(steps):
                span = pl.ds(base + q * step, step)
                queries = seq[span, lanes]
                grad = grad_seq[span, lanes]
                seen = (q + 1) * step
                allowed = lax.broadcasted_iota(jnp.int32, (seen, step), 0) < limit[:, span]
                for h in range(2):
                    head = pair * 2 + h
                    own_q = head_lanes(queries, h)
                    own_g = head_lanes(grad, h)
                    scores = dot_back(keys[:seen], own_q)
                    log_total = lse[pair][pl.ds(h, 1), span]
                    probs = jnp.exp(jnp.where(allowed, scores, NEGATIVE) - log_total)
                    grad_probs = dot_back(values[:seen], own_g)
                    mixed = probs * grad_probs
                    centre = jnp.sum(mixed, 0, keepdims=True)
                    raw = (mixed - probs * centre).astype(BF)
                    grad_q[pl.ds(head * HD, HD), span] = (
                        dot(keys_t[h * HD : (h + 1) * HD, :seen], raw) * scale
                    ).astype(BF)
                    to_k = dot(raw, own_q)
                    to_v = dot(probs.astype(BF), own_g)
                    for b in range(q + 1):
                        cut = slice(b * step, (b + 1) * step)
                        sums_k[b] = to_k[cut] if sums_k[b] is None else sums_k[b] + to_k[cut]
                        sums_v[b] = to_v[cut] if sums_v[b] is None else sums_v[b] + to_v[cut]
            for b in range(steps):
                grad_k[pl.ds(base + b * step, step), lanes] = sums_k[b].astype(BF)
                grad_v[pl.ds(base + b * step, step), lanes] = sums_v[b].astype(BF)
    part = dot(low_out[0], grad_q[...]) + dot_back(low_out[1], grad_k[...]) + dot_back(low_out[2], grad_v[...])
    lane_at = lax.broadcasted_iota(jnp.int32, part.shape, 1) // seq_len
    rank_at = lax.broadcasted_iota(jnp.int32, part.shape, 0) // RANK
    part_seq[...] = jnp.where(lane_at == rank_at, part, 0.0).astype(BF)
    part_t[...] = dot_back(part_seq[...], push[...]).astype(BF)
    total_in[...] = dot(part_t[:, :near], n1_near[...]) + dot(part_t[:, near:], n1_far[...])
    qkv_out[:, :width] = dot_back(low_t[...], grad_q[...]).astype(BF)
    qkv_out[:, width : 2 * width] = dot(low_t[...], grad_k[...]).astype(BF)
    qkv_out[:, 2 * width :] = dot(low_t[...], grad_v[...]).astype(BF)
    for d in range(count):
        lanes = pl.ds(pl.multiple_of(index[d] * width, width), width)
        messages[d][...] = total_in[:, lanes].astype(BF)


def qkv_back_body(ids, push, w_cat, low_in, grad_q, grad_k, grad_v, part_t, out, joined):
    block = out.shape[0] // len(ids)
    width = grad_k.shape[1]
    for i, at in enumerate(ids):
        rows = pl.ds(i * block, block)
        place = push[pl.ds(at * block, block), :]
        joined[rows, :width] = dot_back(place, grad_q[...]).astype(BF)
        joined[rows, width : 2 * width] = dot(place, grad_k[...]).astype(BF)
        joined[rows, 2 * width :] = dot(place, grad_v[...]).astype(BF)
    for i, at in enumerate(ids):
        rows = pl.ds(i * block, block)
        low = dot_over(part_t[:, at * block : (at + 1) * block], low_in[...])
        out[rows, :] = (dot_back(joined[rows, :], w_cat[...]) + low).astype(BF)


def input_back_body(tokens, grad_mid, gain, *refs):
    out = refs[-1]
    block = tokens.shape[0]
    upstream = refs[0][pl.ds(0, block), :].astype(F32)
    for piece in refs[1:-1]:
        upstream = upstream + piece[...].astype(F32)
    unit, inv = norm_parts(tokens[...].astype(F32))
    out[...] = grad_mid[...] + norm_back(unit, inv, upstream * gain[...])


def result_body(mid, bias, *refs):
    out = refs[-1]
    block = mid.shape[0]
    total = mid[...] + bias[...] + refs[0][pl.ds(0, block), :].astype(F32)
    for piece in refs[1:-1]:
        total = total + piece[...].astype(F32)
    out[...] = total


def spread_hidden_body(hid, found, up_out, down_in):
    pick = found[:, 2 * hid :]
    up_out[...] = dot_over(pick, found[:, :hid])
    down_in[...] = dot_over(found[:, hid : 2 * hid], pick)


def spread_wide_body(width, found, proj_in, wide):
    pick = found[:, 4 * width :]
    for k in range(3):
        wide[pl.ds(k * 128, 128), :] = dot_over(pick, found[:, k * width : (k + 1) * width]).astype(BF)
    proj_in[...] = dot_over(found[:, 3 * width : 4 * width], pick)


def spread_late_body(width, found, qkv_out, wide):
    pick = found[:, 4 * width :]
    qkv_out[...] = dot_over(pick, found[:, : 3 * width])
    wide[...] = dot_over(pick, found[:, 3 * width : 4 * width]).astype(BF)


def place_wide_body(count, index, *refs):
    messages = refs[:count]
    up_in, down_out, proj_out = refs[count:]
    width = messages[0].shape[1]
    for d in range(count):
        span = pl.ds(pl.multiple_of(index[d] * width, width), width)
        up_in[span, :] = messages[d][pl.ds(0, 128), :].astype(F32).T
        down_out[:, span] = messages[d][pl.ds(128, 128), :].astype(F32)
        proj_out[:, span] = messages[d][pl.ds(256, 128), :].astype(F32)


def place_late_body(count, index, *refs):
    messages = refs[:count]
    qkv_in = refs[count]
    width = messages[0].shape[1]
    for d in range(count):
        qkv_in[pl.ds(pl.multiple_of(index[d] * width, width), width), :] = messages[d][...].astype(F32).T


def tie(value, *others):
    return lax.optimization_barrier((value, *others))[0]


def body(
    tensor_size,
    dp_size,
    tokens,
    cotangent,
    lengths,
    order,
    adapter_ids,
    norm1_gain,
    norm1_shift,
    qkv_weight,
    qv_bias,
    proj_weight,
    proj_bias,
    norm2_gain,
    norm2_shift,
    up_weight,
    up_bias,
    down_weight,
    down_bias,
    adapt_qkv_in,
    adapt_qkv_out,
    adapt_proj_in,
    adapt_proj_out,
    adapt_up_in,
    adapt_up_out,
    adapt_down_in,
    adapt_down_out,
):
    count = tensor_size
    chips = count // 2
    own, wide = tokens.shape
    width = qkv_weight.shape[2]
    pairs = width // PAIR
    hid = up_weight.shape[1]
    rows = order.shape[1]
    seqs = lengths.shape[1]
    seq_len = rows // seqs
    ranks = seqs * RANK
    near = 2 * own
    far = rows - near
    cols = adapt_qkv_in.shape[1]
    near_ids = (0, 1)
    even_ids = tuple(range(2, count, 2))
    odd_ids = tuple(range(3, count, 2))
    me = lax.axis_index("tensor")

    core_perm = [(t, t ^ 1) for t in range(count)]

    def core_swap(value):
        return lax.ppermute(value, "tensor", core_perm)

    def chip_hop(value, k):
        return lax.ppermute(value, "tensor", [(t, ((t // 2 + k) % chips) * 2 + t % 2) for t in range(count)])

    def hops_of(value):
        return [chip_hop(value, k) for k in range(1, chips)]

    def weave(value, swapped, moved):
        found = [value, swapped]
        for item in moved:
            found += [item, core_swap(item)]
        return found

    def exchange(messages):
        out = [messages[0], core_swap(messages[1])] + [None] * (count - 2)
        for k in range(1, chips):
            flat = [(t, ((t // 2 - k) % chips) * 2 + t % 2) for t in range(count)]
            cross = [(t, ((t // 2 - k) % chips) * 2 + (t % 2 ^ 1)) for t in range(count)]
            out[2 * (chips - k)] = lax.ppermute(messages[2 * k], "tensor", flat)
            out[2 * (chips - k) + 1] = lax.ppermute(messages[2 * k + 1], "tensor", cross)
        return out

    def join(left, right, name):
        return whole_call(add_body, [left, right], [shape(left.shape, BF)], name)[0]

    def send_far(joined):
        return [chip_hop(joined[(k - 1) * own : k * own] if chips > 2 else joined, -k) for k in range(1, chips)]

    def widen(value, after=()):
        stride = dp_size // 2
        step = 0
        while stride:
            moved = lax.ppermute(value, "dp", [(i, i ^ stride) for i in range(dp_size)])
            if step < len(after):
                moved = tie(moved, after[step])
            value = jnp.concatenate([value, moved], 0)
            stride //= 2
            step += 1
        return value

    relative = jnp.arange(count, dtype=jnp.int32)
    index = ((me // 2 - relative // 2) % chips) * 2 + ((me % 2) ^ (relative % 2))
    owner = order // own
    order_rel = (((me // 2 - owner // 2) % chips) * 2 + ((me % 2) ^ (owner % 2))) * own + order % own
    order_col = order_rel.reshape(rows, 1)
    slot = jnp.arange(rows, dtype=jnp.int32)
    limit = jnp.minimum(
        slot % seq_len + 1, jnp.sum(jnp.where(slot[:, None] // seq_len == jnp.arange(seqs)[None, :], lengths, 0), 1)
    ).reshape(1, rows)
    lane = jnp.arange(ranks, dtype=jnp.int32)
    target = jnp.sum(jnp.where(lane[:, None] // RANK == jnp.arange(seqs)[None, :], adapter_ids, 0), 1)
    pick = ((target * RANK + lane % RANK)[:, None] == jnp.arange(cols, dtype=jnp.int32)[None, :]).astype(BF)
    weight_three = jnp.transpose(qkv_weight, (1, 0, 2))
    out_three = jnp.transpose(adapt_qkv_out, (1, 0, 2))
    row = lambda v: v.reshape(1, -1)

    token_core = core_swap(tokens)
    token_hops = hops_of(tokens)
    proj_own = tie(proj_weight, token_core)
    proj_core = core_swap(proj_own)
    proj_hops = hops_of(proj_own)
    grad_own = tie(cotangent, proj_core).astype(BF)
    grad_core = core_swap(grad_own)
    grad_hops = hops_of(grad_own)

    prepared = whole_call(
        functools.partial(prep_body, seq_len),
        [order_rel, order_col, pick, adapt_qkv_in, out_three, adapt_proj_in, adapt_proj_out, adapt_up_in,
         adapt_up_out, adapt_down_in, adapt_down_out],
        [shape((ranks, wide), BF), shape((3, ranks, width), BF), shape((ranks, width), BF),
         shape((ranks, wide), BF), shape((ranks, wide), BF), shape((ranks, hid), BF),
         shape((ranks, hid), BF), shape((ranks, wide), BF), shape((rows, near), BF), shape((rows, far), BF),
         shape((rows, rows), BF), shape((rows, ranks), F32)],
        "prep",
        loose=tuple(range(11)),
    )
    c_qkv_in, c_qkv_out, c_proj_in, c_proj_out, c_up_in, c_up_out, c_down_in, c_down_out = prepared[:8]
    pull_near, pull_far, push, mask = prepared[8:]
    in_core = core_swap(c_proj_in)
    in_hops = hops_of(c_proj_in)

    norm1 = [row(norm1_gain), row(norm1_shift), weight_three, qv_bias, c_qkv_in, c_qkv_out]
    n1_near, low1_near, moved_near = whole_call(
        functools.partial(qkv_body, near_ids, False),
        [mask] + norm1 + [pull_near, tokens, token_core],
        [shape((near, wide), BF), shape((near, ranks), BF), shape((rows, 3 * width), F32)],
        "qkv_near",
        scratch=[pltpu.VMEM((near, 3 * width), BF)],
    )
    token_hops = [tie(item, low1_near) for item in token_hops]
    token_blocks = weave(tokens, token_core, token_hops)
    n1_far, low1_far, qkv_seq = whole_call(
        functools.partial(qkv_body, tuple(range(2, count)), True),
        [mask] + norm1 + [pull_far] + token_blocks[2:] + [moved_near],
        [shape((far, wide), BF), shape((far, ranks), BF), shape((rows, 3 * width), BF)],
        "qkv_far",
        scratch=[pltpu.VMEM((far, 3 * width), BF)],
    )

    sums = []
    attended = []
    seq_in = qkv_seq
    for pair in range(pairs):
        part, lse = whole_call(
            functools.partial(attend_body, seq_len, pair),
            [limit, seq_in, push],
            [shape((rows, PAIR), BF), shape((2, rows), F32)],
            f"attend{pair}",
            scratch=[pltpu.VMEM((PAIR, rows), BF)],
        )
        seq_in = tie(qkv_seq, lse)
        sums.append(lse)
        attended.append(part)
    after = sums[-1]
    gathered_heads = [weave(part, core_swap(part), hops_of(part)) for part in attended]
    heads = [gathered_heads[p][d] for d in range(count) for p in range(pairs)]

    proj_blocks = weave(proj_own, proj_core, [tie(item, after) for item in proj_hops])
    in_blocks = weave(c_proj_in, in_core, [tie(item, after) for item in in_hops])
    grad_blocks = weave(grad_own, grad_core, [tie(item, after) for item in grad_hops])
    w_all, in_all, w_cat, low_t = whole_call(
        functools.partial(join_body, count),
        [low1_near, low1_far, push, weight_three] + proj_blocks + in_blocks,
        [shape((wide, wide), BF), shape((ranks, wide), BF), shape((wide, 3 * width), BF), shape((ranks, rows), BF)],
        "join",
    )

    def block_call(ids, gate, name):
        size = len(ids) * own
        extra = [shape((own, ranks), BF), shape((own, wide), F32)] if 0 in ids else []
        keep = mask if gate is None else tie(mask, gate)
        return whole_call(
            functools.partial(block_body, ids, count, pairs, min(256, hid)),
            [keep, w_all, in_all, c_proj_out, row(proj_bias), row(norm2_gain), row(norm2_shift), c_up_in, up_weight,
             row(up_bias), c_up_out, down_weight, c_down_in, c_down_out]
            + [token_blocks[i] for i in ids] + [grad_blocks[i] for i in ids] + heads,
            [shape((size, wide), BF), shape((size, wide), BF), shape((size, ranks), BF), shape((size, ranks), BF),
             shape((size, ranks), BF), shape((size, hid), BF), shape((size, hid), BF), shape((size, ranks), BF)]
            + extra,
            name,
            scratch=[pltpu.VMEM((size, wide), BF), pltpu.VMEM((size, wide), BF), pltpu.VMEM((size, wide), F32)],
        )

    odd = block_call(odd_ids, None, "block_odd")
    odd_moved = core_swap(odd[0])
    even = block_call(even_ids, odd[3], "block_even")
    up_joined = join(even[0], odd_moved, "up_join")
    up_hops = send_far(up_joined)
    mine = block_call(near_ids, up_joined, "block_near")
    up_swap = core_swap(mine[0][own:])
    groups = (mine, even, odd)
    order_ids = (near_ids, even_ids, odd_ids)
    pack_hidden, p_up_in, p_down_out = whole_call(
        functools.partial(hidden_grads_body, 3, tuple(len(i) for i in order_ids)),
        [pick] + [g[k] for k in (2, 6, 4, 5, 3, 1, 7) for g in groups]
        + [grad_blocks[i] for ids in order_ids for i in ids],
        [shape((ranks, 2 * hid + cols), BF), shape((ranks, wide), F32), shape((ranks, wide), F32)],
        "hidden_grads",
    )
    up_hops = [tie(item, p_up_in) for item in up_hops]
    proj_low, mid = mine[8:]
    back = whole_call(
        functools.partial(mid_back_body, (2 + len(up_hops), count)),
        [mask, cotangent, mid, row(norm2_gain), c_proj_out, w_all, in_all, mine[0], up_swap] + up_hops,
        [shape((own, wide), F32), shape((own, wide), BF), shape((own, ranks), BF)]
        + [shape((own, width), BF)] * count,
        "mid_back",
    )
    grad_mid, grad_attn, grad_proj_low = back[:3]
    grad_att = exchange(back[3:])

    messages = whole_call(
        functools.partial(message_body, count, pairs),
        [p_up_in, p_down_out, proj_low, grad_attn, grad_proj_low] + heads,
        [shape((4 * ranks, width), BF)] * count,
        "message",
        smem=[index],
        scratch=[pltpu.VMEM((ranks, wide), F32)],
    )
    wide_messages = exchange(messages)
    down_parts = whole_call(
        functools.partial(down_body, 3),
        [tie(down_weight, messages[0]), c_down_out] + [g[5] for g in groups] + [g[7] for g in groups],
        [shape(g[0].shape, BF) for g in groups],
        "down",
    )
    down_mine, down_even, down_odd = down_parts
    down_joined = join(down_even, core_swap(down_odd), "down_join")
    down_hops = send_far(down_joined)
    down_swap = core_swap(down_mine[own:])
    wide_messages = [wide_messages[0]] + [tie(item, down_joined) for item in wide_messages[1:]]
    (pack_wide,) = whole_call(
        functools.partial(pack_body, count, 0),
        [pick] + wide_messages,
        [shape((ranks, 4 * width + cols), BF)],
        "pack_wide",
    )
    grad_att = [grad_att[0]] + [tie(item, pack_wide) for item in grad_att[1:]]

    results = whole_call(
        functools.partial(attend_back_body, count, pairs, seq_len),
        [limit, qkv_seq, pull_near, pull_far, push, low_t, n1_near, n1_far, c_qkv_out] + sums + grad_att,
        [shape((width, rows), BF), shape((rows, width), BF), shape((rows, width), BF), shape((ranks, rows), BF),
         shape((ranks, 3 * width), BF)] + [shape((ranks, width), BF)] * count,
        "attend_back",
        smem=[index],
        scratch=[pltpu.VMEM((rows, width), BF), pltpu.VMEM((rows, width), BF), pltpu.VMEM((ranks, rows), BF),
                 pltpu.VMEM((ranks, wide), F32)],
    )
    grad_q, grad_k, grad_v, part_t, g_qkv_out = results[:5]
    late_messages = exchange(results[5:])

    def unproject(ids, gate, name):
        size = len(ids) * own
        return whole_call(
            functools.partial(qkv_back_body, ids),
            [push, w_cat, c_qkv_in, grad_q, grad_k, grad_v, part_t if gate is None else tie(part_t, gate)],
            [shape((size, wide), BF)],
            name,
            scratch=[pltpu.VMEM((size, 3 * width), BF)],
        )[0]

    odd_part = unproject(odd_ids, None, "qkv_back_odd")
    odd_moved = core_swap(odd_part)
    even_part = unproject(even_ids, odd_part, "qkv_back_even")
    qkv_joined = join(even_part, odd_moved, "qkv_join")
    qkv_hops = send_far(qkv_joined)
    near_part = unproject(near_ids, qkv_joined, "qkv_back_near")
    qkv_swap = core_swap(near_part[own:])

    late_messages = [late_messages[0]] + [tie(item, qkv_joined) for item in late_messages[1:]]
    (pack_late,) = whole_call(
        functools.partial(pack_body, count, 1),
        [pick, g_qkv_out] + late_messages,
        [shape((ranks, 4 * width + cols), BF)],
        "pack_late",
    )

    hidden_found = widen(pack_hidden, (grad_proj_low, pack_wide, part_t))
    wide_found = widen(pack_wide, (part_t, qkv_joined, near_part))
    late_found = widen(pack_late)
    up_out_full, down_in_full = whole_call(
        functools.partial(spread_hidden_body, hid),
        [hidden_found],
        [shape((cols, hid), F32), shape((hid, cols), F32)],
        "spread_hidden",
        final=(0, 1),
    )
    proj_in_full, wide_part = whole_call(
        functools.partial(spread_wide_body, width),
        [wide_found],
        [shape((width, cols), F32), shape((3 * cols, width), BF)],
        "spread_wide",
        final=(0,),
    )
    up_in_full, down_out_full, proj_out_full = whole_call(
        functools.partial(place_wide_body, count),
        weave(wide_part, core_swap(wide_part), hops_of(wide_part)),
        [shape((wide, cols), F32), shape((cols, wide), F32), shape((cols, wide), F32)],
        "place_wide",
        smem=[index],
        final=(0, 1, 2),
    )
    (result,) = whole_call(
        result_body, [mid, row(down_bias), down_mine, down_swap] + down_hops, [shape((own, wide), F32)], "result",
        final=(0,),
    )
    (grad_input,) = whole_call(
        input_back_body,
        [tokens, grad_mid, row(norm1_gain), near_part, qkv_swap] + qkv_hops,
        [shape((own, wide), F32)],
        "input_back",
        final=(0,),
    )
    qkv_out_full, late_part = whole_call(
        functools.partial(spread_late_body, width),
        [late_found],
        [shape((cols, 3 * width), F32), shape((cols, width), BF)],
        "spread_late",
        final=(0,),
    )
    (qkv_in_full,) = whole_call(
        functools.partial(place_late_body, count),
        weave(late_part, core_swap(late_part), hops_of(late_part)),
        [shape((wide, cols), F32)],
        "place_late",
        smem=[index],
        final=(0,),
    )
    return (
        result,
        grad_input,
        qkv_in_full,
        qkv_out_full.reshape(cols, 3, width),
        proj_in_full,
        proj_out_full,
        up_in_full,
        up_out_full,
        down_in_full,
        down_out_full,
    )


def solution(mesh):
    in_specs = (
        P(("dp", "tensor"), None),
        P(("dp", "tensor"), None),
        P("dp", None),
        P("dp", None),
        P("dp", None),
        P(),
        P(),
        P(None, None, "tensor"),
        P(None, "tensor"),
        P("tensor", None),
        P(),
        P(),
        P(),
        P(None, "tensor"),
        P("tensor"),
        P("tensor", None),
        P(),
        P(),
        P(None, None, "tensor"),
        P("tensor", None),
        P(),
        P(),
        P(None, "tensor"),
        P("tensor", None),
        P(),
    )
    out_specs = (
        P(("dp", "tensor"), None),
        P(("dp", "tensor"), None),
        P(),
        P(None, None, "tensor"),
        P("tensor", None),
        P(),
        P(),
        P(None, "tensor"),
        P("tensor", None),
        P(),
    )
    run = functools.partial(body, mesh.shape["tensor"], mesh.shape["dp"])
    return jax.shard_map(run, mesh=mesh, in_specs=in_specs, out_specs=out_specs, check_vma=False)
```

```python
import functools
import math

import jax
import jax.numpy as jnp
from jax import lax
from jax.experimental import pallas as pl
from jax.experimental.pallas import tpu as pltpu
from jax.sharding import PartitionSpec as P

HD = 64
RANK = 16
PAIR = 2 * HD
EPSILON = 1e-05
NEGATIVE = -1000000000.0
BF = jnp.bfloat16
F32 = jnp.float32
LIMIT = 10 * 1024 * 1024
GELU_A = math.sqrt(2.0 / math.pi)
GELU_B = 0.044715


def dot(left, right):
    return jnp.dot(left, right, preferred_element_type=F32)


def dot_back(left, right):
    return lax.dot_general(left, right, (((1,), (1,)), ((), ())), preferred_element_type=F32)


def dot_over(left, right):
    return lax.dot_general(left, right, (((0,), (0,)), ((), ())), preferred_element_type=F32)


def shape(dims, kind):
    return jax.ShapeDtypeStruct(tuple(dims), kind)


def whole_call(body, inputs, outs, name, smem=(), scratch=(), final=(), loose=(), long=False):
    smem_spec = pl.BlockSpec(memory_space=pltpu.SMEM)
    vmem_spec = pl.BlockSpec(memory_space=pltpu.VMEM)
    held = [
        pltpu.with_memory_space_constraint(x, pltpu.HBM if i in loose else pltpu.VMEM) for i, x in enumerate(inputs)
    ]
    kinds = [o if i in final else pltpu.VMEM(o.shape, o.dtype) for i, o in enumerate(outs)]
    return pl.pallas_call(
        body,
        out_shape=kinds,
        in_specs=[smem_spec] * len(smem) + [vmem_spec] * len(inputs),
        out_specs=[vmem_spec] * len(outs),
        scratch_shapes=list(scratch),
        compiler_params=pltpu.CompilerParams(vmem_limit_bytes=LIMIT),
        name=name,
    )(*smem, *held)


def norm_parts(values):
    centre = values - jnp.mean(values, -1, keepdims=True)
    spread = jnp.mean(centre * centre, -1, keepdims=True)
    inv = lax.rsqrt(spread + EPSILON)
    return centre * inv, inv


def norm_back(normed, inv, upstream):
    return inv * (
        upstream
        - jnp.mean(upstream, -1, keepdims=True)
        - normed * jnp.mean(upstream * normed, -1, keepdims=True)
    )


def owner_of(me, d, count):
    return (((me // 2) + count // 2 - d // 2) % (count // 2)) * 2 + ((me % 2 + d % 2) % 2)


def prep_body(
    seq_len, own, count, me, lengths, ids, order, proj_w, qkv_in, qkv_out, proj_in, proj_out, up_in, up_out,
    down_in, down_out, *outs
):
    o_qkv_in, o_qkv_out, o_proj, o_proj_out, o_up_in, o_up_out, o_down_in, o_down_out = outs[:8]
    pull_near, pull_far, push, mask, pick, limit = outs[8:]
    rank_at = lax.broadcasted_iota(jnp.int32, pick.shape, 0)
    col_at = lax.broadcasted_iota(jnp.int32, pick.shape, 1)
    wanted = rank_at + ids[0, 0] * RANK
    slot = lax.broadcasted_iota(jnp.int32, limit.shape, 1)
    bound = jnp.minimum(slot + 1, lengths[0, 0])
    for s in range(1, lengths.shape[1]):
        wanted = jnp.where(rank_at >= s * RANK, rank_at - s * RANK + ids[0, s] * RANK, wanted)
        bound = jnp.where(slot >= s * seq_len, jnp.minimum(slot - s * seq_len + 1, lengths[0, s]), bound)
    limit[...] = bound
    chosen = jnp.where(col_at == wanted, 1.0, 0.0).astype(BF)
    pick[...] = chosen
    width = proj_w.shape[0]
    fold = pick.shape[0] // count
    o_proj[pl.ds(0, width), :] = proj_w[...]
    o_proj[pl.ds(width, 16), :] = jnp.zeros((16, o_proj.shape[1]), BF)
    chosen_in = dot_back(chosen, proj_in[...])
    for j in range(count):
        o_proj[pl.ds(width, fold), j * width : (j + 1) * width] = chosen_in[j * fold : (j + 1) * fold].astype(BF)
    o_qkv_in[...] = dot_back(chosen, qkv_in[...]).astype(BF)
    for k in range(3):
        o_qkv_out[k] = dot(chosen, qkv_out[k]).astype(BF)
    o_proj_out[...] = dot(chosen, proj_out[...]).astype(BF)
    o_up_in[...] = dot_back(chosen, up_in[...]).astype(BF)
    o_up_out[...] = dot(chosen, up_out[...]).astype(BF)
    o_down_in[...] = dot_back(chosen, down_in[...]).astype(BF)
    o_down_out[...] = dot(chosen, down_out[...]).astype(BF)
    stored = order[...]
    relative = stored
    for d in range(count):
        start = owner_of(me[0], d, count) * own
        relative = jnp.where((stored >= start) & (stored < start + own), stored - start + d * own, relative)
    near = pull_near.shape[1]
    rows = push.shape[0]
    tall = jnp.broadcast_to(relative.astype(F32), (8, rows)).T[:, :1].astype(jnp.int32)
    for ref, start in ((pull_near, 0), (pull_far, near)):
        at = lax.broadcasted_iota(jnp.int32, ref.shape, 1) + start
        ref[...] = jnp.where(at == tall, 1.0, 0.0).astype(BF)
    at = lax.broadcasted_iota(jnp.int32, (rows, rows), 0)
    push[...] = jnp.where(at == relative, 1.0, 0.0).astype(BF)
    seq_at = lax.broadcasted_iota(jnp.int32, mask.shape, 0) // seq_len
    lane_at = lax.broadcasted_iota(jnp.int32, mask.shape, 1) // RANK
    mask[...] = dot(push[...], jnp.where(seq_at == lane_at, 1.0, 0.0).astype(BF))


def qkv_body(ids, last, mask, gain, shift, weight, bias, low_in, low_out, pull, *refs):
    count = len(ids)
    blocks = refs[:count]
    rest = refs[count:]
    earlier = None
    if last:
        earlier, rest = rest[0], rest[1:]
    normed_ref, low_ref, moved_ref, joined = rest
    rows = blocks[0].shape[0]
    width = weight.shape[2]
    for i in range(count):
        part = pl.ds(i * rows, rows)
        unit, _ = norm_parts(blocks[i][...].astype(F32))
        normed = (unit * gain[...] + shift[...]).astype(BF)
        normed_ref[part, :] = normed
        low = (dot_back(normed, low_in[...]) * mask[pl.ds(ids[i] * rows, rows), :]).astype(BF)
        low_ref[part, :] = low
        for k in range(3):
            value = dot(normed, weight[k]) + dot(low, low_out[k])
            if k != 1:
                value = value + bias[k // 2 : k // 2 + 1, :]
            joined[part, k * width : (k + 1) * width] = value.astype(BF)
    total = moved_ref.shape[0]
    step = min(256, total)
    for i in range(total // step):
        part = pl.ds(i * step, step)
        moved = dot(pull[part, :], joined[...])
        if last:
            moved = moved + earlier[part, :]
            moved_ref[part, :width] = (moved[:, :width] * (1.0 / math.sqrt(HD))).astype(BF)
            moved_ref[part, width:] = moved[:, width:].astype(BF)
        else:
            moved_ref[part, :] = moved


def head_lanes(values, head):
    lane = lax.broadcasted_iota(jnp.int32, values.shape, 1)
    return jnp.where((lane // HD) == head, values, jnp.zeros_like(values))


def attend_body(seq_len, pair, limit, seq, push, out, kept, turned):
    rows = seq.shape[0]
    width = seq.shape[1] // 3
    step = min(256, seq_len)

    def one_sequence(s):
        base = s * seq_len
        keys = seq[pl.ds(base, seq_len), pl.ds(width + pair * PAIR, PAIR)]
        values = seq[pl.ds(base, seq_len), pl.ds(2 * width + pair * PAIR, PAIR)]
        values_t = values.astype(F32).T.astype(BF)
        for q in range(seq_len // step):
            span = pl.ds(base + q * step, step)
            queries = seq[span, pl.ds(pair * PAIR, PAIR)]
            seen = (q + 1) * step
            allowed = lax.broadcasted_iota(jnp.int32, (seen, step), 0) < limit[:, span]
            for h in range(2):
                scores = dot_back(keys[:seen], head_lanes(queries, h))
                scores = jnp.where(allowed, scores, NEGATIVE)
                weights = jnp.exp(scores - jnp.max(scores, 0, keepdims=True))
                total = jnp.sum(weights, 0, keepdims=True)
                probs = (weights * (1.0 / total)).astype(BF)
                kept[s, h, :seen, q * step : (q + 1) * step] = probs
                turned[pl.ds(h * HD, HD), span] = dot(values_t[h * HD : (h + 1) * HD, :seen], probs).astype(BF)

    for s in range(rows // seq_len):
        one_sequence(s)
    out[...] = dot_back(push[...], turned[...]).astype(BF)


def join_body(count, low_near, low_far, push, weight, *refs):
    proj = refs[:count]
    w_all, in_all, w_cat, low_t = refs[count:]
    width = in_all.shape[1] // count
    fold = in_all.shape[0] // count
    near = low_near.shape[0]
    for d in range(count):
        w_all[pl.ds(d * width, width), :] = proj[d][pl.ds(0, width), :]
        for j in range(count):
            part = proj[d][pl.ds(width, fold), j * width : (j + 1) * width]
            in_all[pl.ds(j * fold, fold), d * width : (d + 1) * width] = part
    for k in range(3):
        w_cat[:, k * width : (k + 1) * width] = weight[k]
    rows = push.shape[0]
    low_t[...] = (
        dot_over(low_near[...], push[pl.ds(0, near), :]) + dot_over(low_far[...], push[pl.ds(near, rows - near), :])
    ).astype(BF)


def place_of(block, sender, chips):
    return ((block // 2 - sender // 2) % chips) * 2 + ((block % 2) ^ (sender % 2))


def block_body(
    ids, count, pairs, chunk, mask, w_all, in_all, proj_out, proj_bias, gain, shift, up_in, up_w, up_b, up_out,
    down_w, down_in, down_out, *refs
):
    size = len(ids)
    tokens = refs[:size]
    grads = refs[size : 2 * size]
    attended = refs[2 * size : 2 * size + count * pairs]
    rest = refs[2 * size + count * pairs :]
    outs = rest[: len(rest) - 3]
    heads, grad_all, acc = rest[len(rest) - 3 :]
    part_ref, normed_ref, low_ref, low_part, grad_down_low, act_ref, gup_ref, down_low = outs[:8]
    block = tokens[0].shape[0]
    width = in_all.shape[1] // count
    for i in range(size):
        part = pl.ds(i * block, block)
        for d in range(count):
            spot = place_of(ids[i], d, count // 2) * block
            for p in range(pairs):
                at = d * width + p * PAIR
                heads[part, at : at + PAIR] = attended[d * pairs + p][pl.ds(spot, block), :]
        keep = mask[pl.ds(ids[i] * block, block), :]
        grad = grads[i][...]
        grad_all[part, :] = grad
        grad_down_low[part, :] = (dot_back(grad, down_out[...]) * keep).astype(BF)
        rows = heads[part, :]
        low = (dot_back(rows, in_all[...]) * keep).astype(BF)
        mid = dot(rows, w_all[...]) + dot(low, proj_out[...]) + proj_bias[...] + tokens[i][...].astype(F32)
        unit, _ = norm_parts(mid)
        normed = (unit * gain[...] + shift[...]).astype(BF)
        normed_ref[part, :] = normed
        low_ref[part, :] = (dot_back(normed, up_in[...]) * keep).astype(BF)
        if len(outs) > 8 and i == 0:
            outs[8][...] = low
            outs[9][...] = mid
    low_sum = None
    down_sum = None
    hid = up_w.shape[1]
    for j in range(hid // chunk):
        cut = pl.ds(j * chunk, chunk)
        upper = dot(normed_ref[...], up_w[:, cut]) + dot(low_ref[...], up_out[:, cut]) + up_b[:, cut]
        grad = dot_back(grad_all[...], down_w[cut, :]) + dot(grad_down_low[...], down_in[:, cut])
        square = upper * upper
        curve = jnp.tanh(GELU_A * upper * (1.0 + GELU_B * square))
        half = 0.5 * (1.0 + curve)
        active = (upper * half).astype(BF)
        act_ref[:, cut] = active
        slope = half + 0.5 * upper * (1.0 - curve * curve) * (GELU_A * (1.0 + 3.0 * GELU_B * square))
        grad_upper = (grad * slope).astype(BF)
        gup_ref[:, cut] = grad_upper
        part = dot_back(grad_upper, up_w[:, cut])
        low = dot_back(grad_upper, up_out[:, cut])
        down = dot_back(active, down_in[:, cut])
        acc[...] = part if j == 0 else acc[...] + part
        low_sum = low if j == 0 else low_sum + low
        down_sum = down if j == 0 else down_sum + down
    for i in range(size):
        cut = slice(i * block, (i + 1) * block)
        part = pl.ds(i * block, block)
        keep = mask[pl.ds(ids[i] * block, block), :]
        low = (low_sum[cut] * keep).astype(BF)
        low_part[part, :] = low
        down_low[part, :] = (down_sum[cut] * keep).astype(BF)
        part_ref[part, :] = (acc[part, :] + dot(low, up_in[...])).astype(BF)


def down_body(groups, down_w, down_out, *refs):
    for g in range(groups):
        act, low, out = refs[g], refs[groups + g], refs[2 * groups + g]
        out[...] = (dot(act[...], down_w[...]) + dot(low[...], down_out[...])).astype(BF)


def hidden_grads_body(groups, sizes, pick, *refs):
    low2 = refs[:groups]
    gup = refs[groups : 2 * groups]
    gdl = refs[2 * groups : 3 * groups]
    act = refs[3 * groups : 4 * groups]
    part = refs[4 * groups : 5 * groups]
    normed = refs[5 * groups : 6 * groups]
    down = refs[6 * groups : 7 * groups]
    rest = refs[7 * groups :]
    total = sum(sizes)
    grads = rest[:total]
    pack, up_in, down_out = rest[total:]
    hid = gup[0].shape[1]
    block = grads[0].shape[0]
    add = lambda left, right: sum([dot_over(a[...], b[...]) for a, b in zip(left[1:], right[1:])], dot_over(left[0][...], right[0][...]))
    pack[:, :hid] = add(low2, gup).astype(BF)
    pack[:, hid : 2 * hid] = add(gdl, act).astype(BF)
    pack[:, 2 * hid :] = pick[...]
    up_in[...] = add(part, normed)
    at = 0
    out = None
    for g in range(groups):
        for i in range(sizes[g]):
            term = dot_over(down[g][pl.ds(i * block, block), :], grads[at][...])
            out = term if out is None else out + term
            at += 1
    down_out[...] = out


def add_body(left, right, out):
    out[...] = (left[...].astype(F32) + right[...].astype(F32)).astype(BF)


def mid_back_body(count, mask, cotangent, mid, gain, proj_out, w_all, in_all, *refs):
    pieces = refs[: count[0]]
    grad_mid, grad_attn, grad_low = refs[count[0] : count[0] + 3]
    outs = refs[count[0] + 3 :]
    block = mid.shape[0]
    upstream = pieces[0][pl.ds(0, block), :].astype(F32)
    for piece in pieces[1:]:
        upstream = upstream + piece[...].astype(F32)
    unit, inv = norm_parts(mid[...])
    total = cotangent[...] + norm_back(unit, inv, upstream * gain[...])
    grad_mid[...] = total
    attn = total.astype(BF)
    grad_attn[...] = attn
    low = (dot_back(attn, proj_out[...]) * mask[pl.ds(0, block), :]).astype(BF)
    grad_low[...] = low
    value = (dot_back(attn, w_all[...]) + dot(low, in_all[...])).astype(BF)
    width = outs[0].shape[1]
    for d in range(count[1]):
        outs[d][...] = value[:, d * width : (d + 1) * width]


def message_body(count, pairs, me, up_in, down_out, proj_low, grad_attn, grad_low, *refs):
    attended = refs[: count * pairs]
    outs = refs[count * pairs : count * pairs + count]
    proj_out = refs[count * pairs + count]
    rank = up_in.shape[0]
    block = grad_low.shape[0]
    width = outs[0].shape[1]
    proj_out[...] = dot_over(proj_low[...], grad_attn[...])
    for d in range(count):
        spot = place_of(0, d, count // 2) * block
        lanes = pl.ds(pl.multiple_of(owner_of(me[0], d, count) * width, width), width)
        outs[d][pl.ds(0, rank), :] = up_in[:, lanes].astype(BF)
        outs[d][pl.ds(rank, rank), :] = down_out[:, lanes].astype(BF)
        outs[d][pl.ds(2 * rank, rank), :] = proj_out[:, lanes].astype(BF)
        for p in range(pairs):
            outs[d][pl.ds(3 * rank, rank), p * PAIR : (p + 1) * PAIR] = dot_over(
                grad_low[...], attended[d * pairs + p][pl.ds(spot, block), :]
            ).astype(BF)


def pack_body(count, plain, pick, *refs):
    fixed = refs[:plain]
    messages = refs[plain : plain + count]
    out = refs[plain + count]
    rank = pick.shape[0]
    at = 0
    for ref in fixed:
        out[:, at : at + ref.shape[1]] = ref[...]
        at += ref.shape[1]
    width = messages[0].shape[1]
    for k in range(messages[0].shape[0] // rank):
        total = messages[0][pl.ds(k * rank, rank), :].astype(F32)
        for d in range(1, count):
            total = total + messages[d][pl.ds(k * rank, rank), :].astype(F32)
        out[:, at : at + width] = total.astype(BF)
        at += width
    out[:, at : at + pick.shape[1]] = pick[...]


def attend_back_body(pair, pairs, count, seq_len, *refs):
    first, last = pair == 0, pair == pairs - 1
    at = 0

    def take(number):
        nonlocal at
        at += number
        return refs[at - number : at]

    if last:
        (me,) = take(1)
    seq, kept = take(2)
    if first:
        pull_near, pull_far = take(2)
        grads = take(count)
    else:
        (grad_seq,) = take(1)
    if last:
        push, low_t, n1_near, n1_far, low_out = take(5)
        earlier = take(3 * (pairs - 1))
    grad_q, grad_k, grad_v = take(3)
    if last:
        part_t, qkv_out = take(2)
        messages = take(count)
    if first:
        grad_seq, grad_all = take(2)
    if last:
        part_seq, total_in = take(2)
    rows = seq.shape[0]
    width = seq.shape[1] // 3
    step = min(256, seq_len)
    scale = 1.0 / math.sqrt(HD)
    if first:
        block = grads[0].shape[0]
        near = pull_near.shape[1]
        for i in range(count):
            grad_all[pl.ds(i * block, block), :] = grads[i][...]
        grad_seq[...] = (
            dot(pull_near[...], grad_all[pl.ds(0, near), :])
            + dot(pull_far[...], grad_all[pl.ds(near, rows - near), :])
        ).astype(BF)
    if last:
        for p in range(pairs - 1):
            span = slice(p * PAIR, (p + 1) * PAIR)
            grad_q[span, :] = earlier[3 * p][...]
            grad_k[:, span] = earlier[3 * p + 1][...]
            grad_v[:, span] = earlier[3 * p + 2][...]
    base_row = pair * PAIR if last else 0

    def one_sequence(s):
        base = s * seq_len
        lanes = pl.ds(pair * PAIR, PAIR)
        keys = seq[pl.ds(base, seq_len), pl.ds(width + pair * PAIR, PAIR)]
        values = seq[pl.ds(base, seq_len), pl.ds(2 * width + pair * PAIR, PAIR)]
        keys_t = keys.astype(F32).T.astype(BF)
        steps = seq_len // step
        sums_k = [None] * steps
        sums_v = [None] * steps
        for q in range(steps):
            span = pl.ds(base + q * step, step)
            queries = seq[span, lanes]
            grad = grad_seq[span, lanes]
            seen = (q + 1) * step
            for h in range(2):
                own_q = head_lanes(queries, h)
                own_g = head_lanes(grad, h)
                probs = kept[s, h, :seen, q * step : (q + 1) * step]
                wide_probs = probs.astype(F32)
                mixed = wide_probs * dot_back(values[:seen], own_g)
                centre = jnp.sum(mixed, 0, keepdims=True)
                raw = (mixed - wide_probs * centre).astype(BF)
                grad_q[pl.ds(base_row + h * HD, HD), span] = (
                    dot(keys_t[h * HD : (h + 1) * HD, :seen], raw) * scale
                ).astype(BF)
                to_k = dot(raw, own_q)
                to_v = dot(probs, own_g)
                for b in range(q + 1):
                    cut = slice(b * step, (b + 1) * step)
                    sums_k[b] = to_k[cut] if sums_k[b] is None else sums_k[b] + to_k[cut]
                    sums_v[b] = to_v[cut] if sums_v[b] is None else sums_v[b] + to_v[cut]
        for b in range(steps):
            span = pl.ds(base + b * step, step)
            grad_k[span, pl.ds(base_row, PAIR)] = sums_k[b].astype(BF)
            grad_v[span, pl.ds(base_row, PAIR)] = sums_v[b].astype(BF)

    for s in range(rows // seq_len):
        one_sequence(s)
    if not last:
        return
    near = n1_near.shape[0]
    part = dot(low_out[0], grad_q[...]) + dot_back(low_out[1], grad_k[...]) + dot_back(low_out[2], grad_v[...])
    lane_at = lax.broadcasted_iota(jnp.int32, part.shape, 1) // seq_len
    rank_at = lax.broadcasted_iota(jnp.int32, part.shape, 0) // RANK
    part_seq[...] = jnp.where(lane_at == rank_at, part, 0.0).astype(BF)
    part_t[...] = dot_back(part_seq[...], push[...]).astype(BF)
    total_in[...] = dot(part_t[:, :near], n1_near[...]) + dot(part_t[:, near:], n1_far[...])
    qkv_out[:, :width] = dot_back(low_t[...], grad_q[...]).astype(BF)
    qkv_out[:, width : 2 * width] = dot(low_t[...], grad_k[...]).astype(BF)
    qkv_out[:, 2 * width :] = dot(low_t[...], grad_v[...]).astype(BF)
    for d in range(count):
        lanes = pl.ds(pl.multiple_of(owner_of(me[0], d, count) * width, width), width)
        messages[d][...] = total_in[:, lanes].astype(BF)


def qkv_back_body(ids, push, w_cat, low_in, grad_q, grad_k, grad_v, part_t, out, joined):
    block = out.shape[0] // len(ids)
    width = grad_k.shape[1]
    for i, at in enumerate(ids):
        rows = pl.ds(i * block, block)
        place = push[pl.ds(at * block, block), :]
        joined[rows, :width] = dot_back(place, grad_q[...]).astype(BF)
        joined[rows, width : 2 * width] = dot(place, grad_k[...]).astype(BF)
        joined[rows, 2 * width :] = dot(place, grad_v[...]).astype(BF)
    for i, at in enumerate(ids):
        rows = pl.ds(i * block, block)
        low = dot_over(part_t[:, at * block : (at + 1) * block], low_in[...])
        out[rows, :] = (dot_back(joined[rows, :], w_cat[...]) + low).astype(BF)


def add_pieces(total, pieces, block):
    total = total + pieces[0][pl.ds(0, block), :].astype(F32) + pieces[1][...].astype(F32)
    halves = pieces[2:]
    number = len(halves) // 2
    for i in range(number):
        total = total + jnp.concatenate(
            [halves[i][...].astype(F32), halves[number + i][...].astype(F32)], 0
        )
    return total


def input_back_body(tokens, grad_mid, gain, *refs):
    out = refs[-1]
    upstream = add_pieces(0.0, refs[:-1], tokens.shape[0])
    unit, inv = norm_parts(tokens[...].astype(F32))
    out[...] = grad_mid[...] + norm_back(unit, inv, upstream * gain[...])


def result_body(mid, bias, *refs):
    refs[-1][...] = add_pieces(mid[...] + bias[...], refs[:-1], mid.shape[0])


def spread_hidden_body(hid, found, up_out, down_in):
    pick = found[:, 2 * hid :]
    up_out[...] = dot_over(pick, found[:, :hid])
    down_in[...] = dot_over(found[:, hid : 2 * hid], pick)


def spread_wide_body(width, found, proj_in, wide):
    pick = found[:, 4 * width :]
    for k in range(3):
        wide[pl.ds(k * 128, 128), :] = dot_over(pick, found[:, k * width : (k + 1) * width]).astype(BF)
    proj_in[...] = dot_over(found[:, 3 * width : 4 * width], pick)


def spread_late_body(width, found, qkv_out, wide):
    pick = found[:, 4 * width :]
    for k in range(3):
        qkv_out[k] = dot_over(pick, found[:, k * width : (k + 1) * width])
    wide[...] = dot_over(pick, found[:, 3 * width : 4 * width]).astype(BF)


def place_wide_body(count, me, *refs):
    messages = refs[:count]
    up_in, down_out, proj_out = refs[count:]
    width = messages[0].shape[1]
    for d in range(count):
        span = pl.ds(pl.multiple_of(owner_of(me[0], d, count) * width, width), width)
        up_in[span, :] = messages[d][pl.ds(0, 128), :].astype(F32).T
        down_out[:, span] = messages[d][pl.ds(128, 128), :].astype(F32)
        proj_out[:, span] = messages[d][pl.ds(256, 128), :].astype(F32)


def place_late_body(count, me, *refs):
    messages = refs[:count]
    qkv_in = refs[count]
    width = messages[0].shape[1]
    for d in range(count):
        qkv_in[pl.ds(pl.multiple_of(owner_of(me[0], d, count) * width, width), width), :] = messages[d][...].astype(F32).T


def tie(value, *others):
    return lax.optimization_barrier((value, *others))[0]


def body(
    tensor_size,
    dp_size,
    tokens,
    cotangent,
    lengths,
    order,
    adapter_ids,
    norm1_gain,
    norm1_shift,
    qkv_weight,
    qv_bias,
    proj_weight,
    proj_bias,
    norm2_gain,
    norm2_shift,
    up_weight,
    up_bias,
    down_weight,
    down_bias,
    adapt_qkv_in,
    adapt_qkv_out,
    adapt_proj_in,
    adapt_proj_out,
    adapt_up_in,
    adapt_up_out,
    adapt_down_in,
    adapt_down_out,
):
    count = tensor_size
    chips = count // 2
    own, wide = tokens.shape
    width = qkv_weight.shape[2]
    pairs = width // PAIR
    hid = up_weight.shape[1]
    rows = order.shape[1]
    seqs = lengths.shape[1]
    seq_len = rows // seqs
    ranks = seqs * RANK
    near = 2 * own
    far = rows - near
    cols = adapt_qkv_in.shape[1]
    near_ids = (0, 1)
    even_ids = tuple(range(2, count, 2))
    odd_ids = tuple(range(3, count, 2))
    me = lax.axis_index("tensor")

    core_perm = [(t, t ^ 1) for t in range(count)]

    def core_swap(value):
        return lax.ppermute(value, "tensor", core_perm)

    def chip_hop(value, k):
        return lax.ppermute(value, "tensor", [(t, ((t // 2 + k) % chips) * 2 + t % 2) for t in range(count)])

    def hops_of(value):
        return [chip_hop(value, k) for k in range(1, chips)]

    def weave(value, swapped, moved):
        found = [value, swapped]
        for item in moved:
            found += [item, core_swap(item)]
        return found

    def exchange(messages):
        out = [messages[0], core_swap(messages[1])] + [None] * (count - 2)
        for k in range(1, chips):
            flat = [(t, ((t // 2 - k) % chips) * 2 + t % 2) for t in range(count)]
            cross = [(t, ((t // 2 - k) % chips) * 2 + (t % 2 ^ 1)) for t in range(count)]
            out[2 * (chips - k)] = lax.ppermute(messages[2 * k], "tensor", flat)
            out[2 * (chips - k) + 1] = lax.ppermute(messages[2 * k + 1], "tensor", cross)
        return out

    def join(left, right, name):
        return whole_call(add_body, [left, right], [shape(left.shape, BF)], name)[0]

    def send_far(joined):
        return [chip_hop(joined[(k - 1) * own : k * own] if chips > 2 else joined, -k) for k in range(1, chips)]

    def send_half(joined, part):
        half = own // 2
        return [
            chip_hop(joined[(k - 1) * own + part * half : (k - 1) * own + (part + 1) * half], -k)
            for k in range(1, chips)
        ]

    def dp_swap(value, stride):
        return lax.ppermute(value, "dp", [(i, i ^ stride) for i in range(dp_size)])

    def double(value, moved):
        return jnp.concatenate([value, moved], 0)

    def widen(value, stride):
        while stride:
            value = double(value, dp_swap(value, stride))
            stride //= 2
        return value

    place = me.reshape(1)
    weight_three = jnp.transpose(qkv_weight, (1, 0, 2))
    out_three = jnp.transpose(adapt_qkv_out, (1, 0, 2))
    row = lambda v: v.reshape(1, -1)

    top = dp_size // 2
    token_core = core_swap(tokens)
    token_hops = hops_of(tokens)
    grad_own = tie(cotangent, token_core).astype(BF)
    grad_core = core_swap(grad_own)

    prepared = whole_call(
        functools.partial(prep_body, seq_len, own, count),
        [order, proj_weight, adapt_qkv_in, out_three, adapt_proj_in, adapt_proj_out, adapt_up_in, adapt_up_out, adapt_down_in,
         adapt_down_out],
        [shape((ranks, wide), BF), shape((3, ranks, width), BF), shape((width + 16, wide), BF),
         shape((ranks, wide), BF), shape((ranks, wide), BF), shape((ranks, hid), BF),
         shape((ranks, hid), BF), shape((ranks, wide), BF), shape((rows, near), BF), shape((rows, far), BF),
         shape((rows, rows), BF), shape((rows, ranks), F32), shape((ranks, cols), BF), shape((1, rows), jnp.int32)],
        "prep",
        smem=[place, lengths, adapter_ids],
        loose=tuple(range(10)),
    )
    c_qkv_in, c_qkv_out, proj_own, c_proj_out, c_up_in, c_up_out, c_down_in, c_down_out = prepared[:8]
    pull_near, pull_far, push, mask, pick, limit = prepared[8:]
    proj_core = core_swap(proj_own)
    proj_hops = hops_of(proj_own)

    norm1 = [row(norm1_gain), row(norm1_shift), weight_three, qv_bias, c_qkv_in, c_qkv_out]
    n1_near, low1_near, moved_near = whole_call(
        functools.partial(qkv_body, near_ids, False),
        [mask] + norm1 + [pull_near, tokens, token_core],
        [shape((near, wide), BF), shape((near, ranks), BF), shape((rows, 3 * width), F32)],
        "qkv_near",
        loose=(1, 2, 3, 4, 8, 9),
        long=True,
        scratch=[pltpu.VMEM((near, 3 * width), BF)],
    )
    token_hops = [tie(item, low1_near) for item in token_hops]
    token_blocks = weave(tokens, token_core, token_hops)
    grad_hops = hops_of(tie(grad_own, *token_blocks[3::2]))
    n1_far, low1_far, qkv_seq = whole_call(
        functools.partial(qkv_body, tuple(range(2, count)), True),
        [mask] + norm1 + [pull_far] + token_blocks[2:] + [moved_near],
        [shape((far, wide), BF), shape((far, ranks), BF), shape((rows, 3 * width), BF)],
        "qkv_far",
        scratch=[pltpu.VMEM((far, 3 * width), BF)],
    )

    sums = []
    attended = []
    seq_in = qkv_seq
    for pair in range(pairs):
        part, kept = whole_call(
            functools.partial(attend_body, seq_len, pair),
            [limit, seq_in, push],
            [shape((rows, PAIR), BF), shape((seqs, 2, seq_len, seq_len), BF)],
            f"attend{pair}",
            scratch=[pltpu.VMEM((PAIR, rows), BF)],
        )
        sums.append(kept)
        attended.append(part)
        if pair == 0:
            seq_in = tie(qkv_seq, part)
    after = attended[-1]
    gathered_heads = []
    for part in attended:
        gathered_heads.append(weave(part, core_swap(part), hops_of(part)))
    heads = [gathered_heads[p][d] for d in range(count) for p in range(pairs)]

    proj_blocks = weave(proj_own, proj_core, [tie(item, after) for item in proj_hops])
    grad_blocks = weave(grad_own, grad_core, [tie(item, after) for item in grad_hops])
    w_all, in_all, w_cat, low_t = whole_call(
        functools.partial(join_body, count),
        [low1_near, low1_far, push, weight_three] + proj_blocks,
        [shape((wide, wide), BF), shape((ranks, wide), BF), shape((wide, 3 * width), BF), shape((ranks, rows), BF)],
        "join",
    )

    def block_call(ids, gate, name):
        size = len(ids) * own
        extra = [shape((own, ranks), BF), shape((own, wide), F32)] if 0 in ids else []
        keep = mask if gate is None else tie(mask, gate)
        return whole_call(
            functools.partial(block_body, ids, count, pairs, min(256, hid)),
            [keep, w_all, in_all, c_proj_out, row(proj_bias), row(norm2_gain), row(norm2_shift), c_up_in, up_weight,
             row(up_bias), c_up_out, down_weight, c_down_in, c_down_out]
            + [token_blocks[i] for i in ids] + [grad_blocks[i] for i in ids] + heads,
            [shape((size, wide), BF), shape((size, wide), BF), shape((size, ranks), BF), shape((size, ranks), BF),
             shape((size, ranks), BF), shape((size, hid), BF), shape((size, hid), BF), shape((size, ranks), BF)]
            + extra,
            name,
            scratch=[pltpu.VMEM((size, wide), BF), pltpu.VMEM((size, wide), BF), pltpu.VMEM((size, wide), F32)],
            long=gate is not None,
        )

    odd = block_call(odd_ids, None, "block_odd")
    odd_moved = core_swap(odd[0])
    even = block_call(even_ids, odd[3], "block_even")
    up_joined = join(even[0], odd_moved, "up_join")
    up_hops = send_far(up_joined)
    mine = block_call(near_ids, up_joined, "block_near")
    up_swap = core_swap(mine[0][own:])
    groups = (mine, even, odd)
    order_ids = (near_ids, even_ids, odd_ids)
    pack_hidden, p_up_in, p_down_out = whole_call(
        functools.partial(hidden_grads_body, 3, tuple(len(i) for i in order_ids)),
        [pick] + [g[k] for k in (2, 6, 4, 5, 3, 1, 7) for g in groups]
        + [grad_blocks[i] for ids in order_ids for i in ids],
        [shape((ranks, 2 * hid + cols), BF), shape((ranks, wide), F32), shape((ranks, wide), F32)],
        "hidden_grads",
    )
    up_hops = [tie(item, p_up_in) for item in up_hops]
    proj_low, mid = mine[8:]
    back = whole_call(
        functools.partial(mid_back_body, (2 + len(up_hops), count)),
        [mask, cotangent, mid, row(norm2_gain), c_proj_out, w_all, in_all, mine[0], up_swap] + up_hops,
        [shape((own, wide), F32), shape((own, wide), BF), shape((own, ranks), BF)]
        + [shape((own, width), BF)] * count,
        "mid_back",
        long=True,
    )
    grad_mid, grad_attn, grad_proj_low = back[:3]
    grad_att = exchange(back[3:])
    hidden_moved = dp_swap(tie(pack_hidden, grad_proj_low), top)

    messages = whole_call(
        functools.partial(message_body, count, pairs),
        [p_up_in, p_down_out, proj_low, grad_attn, grad_proj_low] + heads,
        [shape((4 * ranks, width), BF)] * count,
        "message",
        smem=[place],
        scratch=[pltpu.VMEM((ranks, wide), F32)],
        long=True,
    )
    down_parts = whole_call(
        functools.partial(down_body, 3),
        [tie(down_weight, messages[0]), c_down_out] + [g[5] for g in groups] + [g[7] for g in groups],
        [shape(g[0].shape, BF) for g in groups],
        "down",
        long=True,
    )
    down_mine, down_even, down_odd = down_parts
    grad_att = [grad_att[0]] + [tie(item, down_mine) for item in grad_att[1:]]
    wide_messages = exchange([tie(item, *grad_att[1:]) for item in messages])
    down_moved = core_swap(tie(down_odd, *grad_att[1:]))
    down_swap = core_swap(tie(down_mine[own:], *grad_att[1:]))

    back_pieces = []
    grad_seq = None
    for pair in range(pairs):
        last = pair == pairs - 1
        inputs = [qkv_seq, sums[pair]]
        outs = [shape((PAIR, rows), BF), shape((rows, PAIR), BF), shape((rows, PAIR), BF)]
        scratch = []
        if pair == 0:
            inputs += [pull_near, pull_far] + grad_att
        else:
            inputs += [grad_seq]
        if last:
            inputs += [push, low_t, n1_near, n1_far, c_qkv_out] + back_pieces
            outs = [shape((width, rows), BF), shape((rows, width), BF), shape((rows, width), BF),
                    shape((ranks, rows), BF), shape((ranks, 3 * width), BF)] + [shape((ranks, width), BF)] * count
        if pair == 0:
            if last:
                scratch += [pltpu.VMEM((rows, width), BF)]
            else:
                outs += [shape((rows, width), BF)]
            scratch += [pltpu.VMEM((rows, width), BF)]
        if last:
            scratch += [pltpu.VMEM((ranks, rows), BF), pltpu.VMEM((ranks, wide), F32)]
        results = whole_call(
            functools.partial(attend_back_body, pair, pairs, count, seq_len),
            inputs,
            outs,
            f"attend_back{pair}",
            smem=[place] if last else [],
            scratch=scratch,
            long=True,
        )
        if pair == 0:
            passed = results[0]
            wide_messages = [wide_messages[0]] + [tie(item, passed) for item in wide_messages[1:]]
            (pack_wide,) = whole_call(
                functools.partial(pack_body, count, 0),
                [pick] + wide_messages,
                [shape((ranks, 4 * width + cols), BF)],
                "pack_wide",
            )
            hidden_half = double(pack_hidden, tie(hidden_moved, passed, *wide_messages))
            hidden_moved = dp_swap(hidden_half, top // 2)
            hidden_first = dp_swap(hidden_half, top // 4)
            wide_moved = dp_swap(pack_wide, top)
            down_joined = join(down_even, tie(down_moved, passed, *wide_messages), "down_join")
            down_first = send_half(down_joined, 0)
        if not last:
            back_pieces += list(results[:3])
            grad_seq = tie(results[3], pack_wide, hidden_half, down_joined)
    grad_q, grad_k, grad_v, part_t, g_qkv_out = results[:5]
    down_first = [tie(item, part_t) for item in down_first]
    hidden_moved = tie(hidden_moved, part_t)
    hidden_first = tie(hidden_first, part_t)
    late_messages = exchange(results[5:])
    wide_moved_first = tie(wide_moved, part_t)
    wide_found = double(pack_wide, wide_moved_first)
    wide_moved = dp_swap(wide_found, top // 2)

    def unproject(ids, gates, name):
        size = len(ids) * own
        return whole_call(
            functools.partial(qkv_back_body, ids),
            [push, w_cat, c_qkv_in, grad_q, grad_k, grad_v, tie(part_t, *gates)],
            [shape((size, wide), BF)],
            name,
            scratch=[pltpu.VMEM((size, 3 * width), BF)],
            long=True,
        )[0]

    odd_part = unproject(odd_ids, [wide_moved_first, hidden_moved, hidden_first, *down_first], "qkv_back_odd")
    odd_moved = core_swap(odd_part)
    even_part = unproject(even_ids, [odd_part], "qkv_back_even")
    qkv_joined = join(even_part, tie(odd_moved, *late_messages[1:]), "qkv_join")
    qkv_first = send_half(qkv_joined, 0)
    late_messages = [late_messages[0]] + [tie(item, qkv_joined) for item in late_messages[1:]]
    (pack_late,) = whole_call(
        functools.partial(pack_body, count, 1),
        [pick, g_qkv_out] + late_messages,
        [shape((ranks, 4 * width + cols), BF)],
        "pack_late",
    )
    late_moved = dp_swap(pack_late, top)
    near_part = unproject(near_ids, [qkv_joined, pack_late], "qkv_back_near")
    qkv_swap = core_swap(near_part[own:])
    qkv_first = [tie(item, near_part) for item in qkv_first]
    wide_found = double(wide_found, tie(wide_moved, *qkv_first))
    wide_moved = dp_swap(wide_found, top // 4)
    qkv_second = send_half(tie(qkv_joined, *qkv_first), 1)
    late_found = double(pack_late, tie(late_moved, near_part, *qkv_first))
    late_moved = dp_swap(late_found, top // 2)
    late_moved = tie(late_moved, *qkv_second)
    wide_found = widen(double(wide_found, tie(wide_moved, late_moved)), top // 8)
    proj_in_full, wide_part = whole_call(
        functools.partial(spread_wide_body, width),
        [wide_found],
        [shape((width, cols), F32), shape((3 * cols, width), BF)],
        "spread_wide",
        final=(0,),
    )
    wide_blocks = weave(wide_part, core_swap(wide_part), hops_of(wide_part))
    late_found = double(late_found, late_moved)
    late_moved = dp_swap(late_found, top // 4)
    down_second = send_half(tie(down_joined, *qkv_second), 1)
    (grad_input,) = whole_call(
        input_back_body,
        [tokens, grad_mid, row(norm1_gain), near_part, qkv_swap, *qkv_first, *qkv_second],
        [shape((own, wide), F32)],
        "input_back",
        final=(0,),
    )
    hidden_second = dp_swap(tie(hidden_moved, grad_input), top // 4)
    up_in_full, down_out_full, proj_out_full = whole_call(
        functools.partial(place_wide_body, count),
        [tie(wide_blocks[0], grad_input)] + wide_blocks[1:],
        [shape((wide, cols), F32), shape((cols, wide), F32), shape((cols, wide), F32)],
        "place_wide",
        smem=[place],
        final=(0, 1, 2),
    )
    late_found = widen(double(late_found, tie(late_moved, grad_input)), top // 8)
    qkv_out_full, late_part = whole_call(
        functools.partial(spread_late_body, width),
        [late_found],
        [shape((3, cols, width), F32), shape((cols, width), BF)],
        "spread_late",
        final=(0,),
    )
    late_blocks = weave(late_part, core_swap(late_part), hops_of(late_part))
    (result,) = whole_call(
        result_body,
        [mid, row(down_bias), down_mine, down_swap, *down_first, *[tie(item, late_part) for item in down_second]],
        [shape((own, wide), F32)],
        "result",
        final=(0,),
    )
    hidden_found = jnp.concatenate([hidden_half, hidden_moved, hidden_first, tie(hidden_second, result)], 0)
    up_out_full, down_in_full = whole_call(
        functools.partial(spread_hidden_body, hid),
        [widen(hidden_found, top // 8)],
        [shape((cols, hid), F32), shape((hid, cols), F32)],
        "spread_hidden",
        final=(0, 1),
    )
    (qkv_in_full,) = whole_call(
        functools.partial(place_late_body, count),
        [late_blocks[0]] + [tie(item, up_out_full) for item in late_blocks[1:]],
        [shape((wide, cols), F32)],
        "place_late",
        smem=[place],
        final=(0,),
    )
    return (
        result,
        grad_input,
        qkv_in_full,
        jnp.transpose(qkv_out_full, (1, 0, 2)),
        proj_in_full,
        proj_out_full,
        up_in_full,
        up_out_full,
        down_in_full,
        down_out_full,
    )


def solution(mesh):
    in_specs = (
        P(("dp", "tensor"), None),
        P(("dp", "tensor"), None),
        P("dp", None),
        P("dp", None),
        P("dp", None),
        P(),
        P(),
        P(None, None, "tensor"),
        P(None, "tensor"),
        P("tensor", None),
        P(),
        P(),
        P(),
        P(None, "tensor"),
        P("tensor"),
        P("tensor", None),
        P(),
        P(),
        P(None, None, "tensor"),
        P("tensor", None),
        P(),
        P(),
        P(None, "tensor"),
        P("tensor", None),
        P(),
    )
    out_specs = (
        P(("dp", "tensor"), None),
        P(("dp", "tensor"), None),
        P(),
        P(None, None, "tensor"),
        P("tensor", None),
        P(),
        P(),
        P(None, "tensor"),
        P("tensor", None),
        P(),
    )
    run = functools.partial(body, mesh.shape["tensor"], mesh.shape["dp"])
    return jax.shard_map(run, mesh=mesh, in_specs=in_specs, out_specs=out_specs, check_vma=False)
```

```python
import functools
import math

import jax
import jax.numpy as jnp
from jax import lax
from jax.experimental import pallas as pl
from jax.experimental.pallas import tpu as pltpu
from jax.sharding import PartitionSpec as P

HD = 64
RANK = 16
PAIR = 2 * HD
EPSILON = 1e-05
NEGATIVE = -1000000000.0
BF = jnp.bfloat16
F32 = jnp.float32
LIMIT = 10 * 1024 * 1024
GELU_A = math.sqrt(2.0 / math.pi)
GELU_B = 0.044715


def dot(left, right):
    return jnp.dot(left, right, preferred_element_type=F32)


def dot_back(left, right):
    return lax.dot_general(left, right, (((1,), (1,)), ((), ())), preferred_element_type=F32)


def dot_over(left, right):
    return lax.dot_general(left, right, (((0,), (0,)), ((), ())), preferred_element_type=F32)


def shape(dims, kind):
    return jax.ShapeDtypeStruct(tuple(dims), kind)


def whole_call(body, inputs, outs, name, smem=(), scratch=(), final=(), loose=(), long=False):
    smem_spec = pl.BlockSpec(memory_space=pltpu.SMEM)
    vmem_spec = pl.BlockSpec(memory_space=pltpu.VMEM)
    held = [
        pltpu.with_memory_space_constraint(x, pltpu.HBM if i in loose else pltpu.VMEM) for i, x in enumerate(inputs)
    ]
    kinds = [o if i in final else pltpu.VMEM(o.shape, o.dtype) for i, o in enumerate(outs)]
    return pl.pallas_call(
        body,
        out_shape=kinds,
        in_specs=[smem_spec] * len(smem) + [vmem_spec] * len(inputs),
        out_specs=[vmem_spec] * len(outs),
        scratch_shapes=list(scratch),
        compiler_params=pltpu.CompilerParams(vmem_limit_bytes=LIMIT),
        name=name,
    )(*smem, *held)


def norm_parts(values):
    centre = values - jnp.mean(values, -1, keepdims=True)
    spread = jnp.mean(centre * centre, -1, keepdims=True)
    inv = lax.rsqrt(spread + EPSILON)
    return centre * inv, inv


def norm_back(normed, inv, upstream):
    return inv * (
        upstream
        - jnp.mean(upstream, -1, keepdims=True)
        - normed * jnp.mean(upstream * normed, -1, keepdims=True)
    )


def owner_of(me, d, count):
    return (((me // 2) + count // 2 - d // 2) % (count // 2)) * 2 + ((me % 2 + d % 2) % 2)


def prep_body(
    seq_len, own, count, me, dp_at, lengths, ids, order, proj_w, qkv_in, qkv_out, proj_in, proj_out, up_in, up_out,
    down_in, down_out, *outs
):
    o_qkv_in, o_qkv_out, o_proj, o_proj_out, o_up_in, o_up_out, o_down_in, o_down_out = outs[:8]
    pull_near, pull_far, push, mask, pick, limit, o_half = outs[8:]
    rank_at = lax.broadcasted_iota(jnp.int32, pick.shape, 0)
    col_at = lax.broadcasted_iota(jnp.int32, pick.shape, 1)
    wanted = rank_at + ids[0, 0] * RANK
    slot = lax.broadcasted_iota(jnp.int32, limit.shape, 1)
    bound = jnp.minimum(slot + 1, lengths[0, 0])
    for s in range(1, lengths.shape[1]):
        wanted = jnp.where(rank_at >= s * RANK, rank_at - s * RANK + ids[0, s] * RANK, wanted)
        bound = jnp.where(slot >= s * seq_len, jnp.minimum(slot - s * seq_len + 1, lengths[0, s]), bound)
    limit[...] = bound
    chosen = jnp.where(col_at == wanted, 1.0, 0.0).astype(BF)
    pick[...] = chosen
    width = proj_w.shape[0]
    fold = pick.shape[0] // count
    o_proj[pl.ds(0, width), :] = proj_w[...]
    o_proj[pl.ds(width, 16), :] = jnp.zeros((16, o_proj.shape[1]), BF)
    chosen_in = dot_back(chosen, proj_in[...])
    for j in range(count):
        o_proj[pl.ds(width, fold), j * width : (j + 1) * width] = chosen_in[j * fold : (j + 1) * fold].astype(BF)
    half = width // 2
    o_half[pl.ds(0, half), :] = proj_w[pl.ds(pl.multiple_of(dp_at[0] % 2 * half, half), half), :]
    o_half[pl.ds(half, 16), :] = o_proj[pl.ds(width, 16), :]
    o_qkv_in[...] = dot_back(chosen, qkv_in[...]).astype(BF)
    for k in range(3):
        o_qkv_out[k] = dot(chosen, qkv_out[k]).astype(BF)
    o_proj_out[...] = dot(chosen, proj_out[...]).astype(BF)
    o_up_in[...] = dot_back(chosen, up_in[...]).astype(BF)
    o_up_out[...] = dot(chosen, up_out[...]).astype(BF)
    o_down_in[...] = dot_back(chosen, down_in[...]).astype(BF)
    o_down_out[...] = dot(chosen, down_out[...]).astype(BF)
    stored = order[...]
    relative = stored
    for d in range(count):
        start = owner_of(me[0], d, count) * own
        relative = jnp.where((stored >= start) & (stored < start + own), stored - start + d * own, relative)
    near = pull_near.shape[1]
    rows = push.shape[0]
    tall = jnp.broadcast_to(relative.astype(F32), (8, rows)).T[:, :1].astype(jnp.int32)
    for ref, start in ((pull_near, 0), (pull_far, near)):
        at = lax.broadcasted_iota(jnp.int32, ref.shape, 1) + start
        ref[...] = jnp.where(at == tall, 1.0, 0.0).astype(BF)
    at = lax.broadcasted_iota(jnp.int32, (rows, rows), 0)
    push[...] = jnp.where(at == relative, 1.0, 0.0).astype(BF)
    seq_at = lax.broadcasted_iota(jnp.int32, mask.shape, 0) // seq_len
    lane_at = lax.broadcasted_iota(jnp.int32, mask.shape, 1) // RANK
    mask[...] = dot(push[...], jnp.where(seq_at == lane_at, 1.0, 0.0).astype(BF))


def qkv_body(ids, last, mask, gain, shift, weight, bias, low_in, low_out, pull, *refs):
    count = len(ids)
    blocks = refs[:count]
    rest = refs[count:]
    earlier = None
    if last:
        earlier, rest = rest[0], rest[1:]
    normed_ref, low_ref, moved_ref, joined = rest
    rows = blocks[0].shape[0]
    width = weight.shape[2]
    for i in range(count):
        part = pl.ds(i * rows, rows)
        unit, _ = norm_parts(blocks[i][...].astype(F32))
        normed = (unit * gain[...] + shift[...]).astype(BF)
        normed_ref[part, :] = normed
        low = (dot_back(normed, low_in[...]) * mask[pl.ds(ids[i] * rows, rows), :]).astype(BF)
        low_ref[part, :] = low
        for k in range(3):
            value = dot(normed, weight[k]) + dot(low, low_out[k])
            if k != 1:
                value = value + bias[k // 2 : k // 2 + 1, :]
            joined[part, k * width : (k + 1) * width] = value.astype(BF)
    total = moved_ref.shape[0]
    step = min(256, total)
    for i in range(total // step):
        part = pl.ds(i * step, step)
        moved = dot(pull[part, :], joined[...])
        if last:
            moved = moved + earlier[part, :]
            moved_ref[part, :width] = (moved[:, :width] * (1.0 / math.sqrt(HD))).astype(BF)
            moved_ref[part, width:] = moved[:, width:].astype(BF)
        else:
            moved_ref[part, :] = moved


def head_lanes(values, head):
    lane = lax.broadcasted_iota(jnp.int32, values.shape, 1)
    return jnp.where((lane // HD) == head, values, jnp.zeros_like(values))


def attend_body(seq_len, pair, limit, seq, push, out, kept, turned):
    rows = seq.shape[0]
    width = seq.shape[1] // 3
    step = min(256, seq_len)

    def one_sequence(s):
        base = s * seq_len
        keys = seq[pl.ds(base, seq_len), pl.ds(width + pair * PAIR, PAIR)]
        values = seq[pl.ds(base, seq_len), pl.ds(2 * width + pair * PAIR, PAIR)]
        values_t = values.astype(F32).T.astype(BF)
        for q in range(seq_len // step):
            span = pl.ds(base + q * step, step)
            queries = seq[span, pl.ds(pair * PAIR, PAIR)]
            seen = (q + 1) * step
            allowed = lax.broadcasted_iota(jnp.int32, (seen, step), 0) < limit[:, span]
            for h in range(2):
                scores = dot_back(keys[:seen], head_lanes(queries, h))
                scores = jnp.where(allowed, scores, NEGATIVE)
                weights = jnp.exp(scores - jnp.max(scores, 0, keepdims=True))
                total = jnp.sum(weights, 0, keepdims=True)
                probs = (weights * (1.0 / total)).astype(BF)
                kept[s, h, :seen, q * step : (q + 1) * step] = probs
                turned[pl.ds(h * HD, HD), span] = dot(values_t[h * HD : (h + 1) * HD, :seen], probs).astype(BF)

    for s in range(rows // seq_len):
        one_sequence(s)
    out[...] = dot_back(push[...], turned[...]).astype(BF)


def join_body(count, dp_at, low_near, low_far, push, weight, *refs):
    proj = refs[:2]
    parts = refs[2 : 2 + 2 * (count - 2)]
    w_all, in_all, w_cat, low_t = refs[2 + 2 * (count - 2) :]
    width = in_all.shape[1] // count
    half = width // 2
    fold = in_all.shape[0] // count
    near = low_near.shape[0]
    for d in range(count):
        if d < 2:
            source, at = proj[d], width
            w_all[pl.ds(d * width, width), :] = source[pl.ds(0, width), :]
        else:
            source, at = parts[2 * (d - 2)], half
            start = pl.multiple_of(dp_at[0] % 2 * half, half)
            w_all[pl.ds(d * width + start, half), :] = source[pl.ds(0, half), :]
            start = pl.multiple_of((dp_at[0] + 1) % 2 * half, half)
            w_all[pl.ds(d * width + start, half), :] = parts[2 * (d - 2) + 1][...]
        for j in range(count):
            part = source[pl.ds(at, fold), j * width : (j + 1) * width]
            in_all[pl.ds(j * fold, fold), d * width : (d + 1) * width] = part
    for k in range(3):
        w_cat[:, k * width : (k + 1) * width] = weight[k]
    rows = push.shape[0]
    low_t[...] = (
        dot_over(low_near[...], push[pl.ds(0, near), :]) + dot_over(low_far[...], push[pl.ds(near, rows - near), :])
    ).astype(BF)


def place_of(block, sender, chips):
    return ((block // 2 - sender // 2) % chips) * 2 + ((block % 2) ^ (sender % 2))


def block_body(
    ids, count, pairs, chunk, mask, w_all, in_all, proj_out, proj_bias, gain, shift, up_in, up_w, up_b, up_out,
    down_w, down_in, down_out, *refs
):
    size = len(ids)
    tokens = refs[:size]
    grads = refs[size : 2 * size]
    attended = refs[2 * size : 2 * size + count * pairs]
    rest = refs[2 * size + count * pairs :]
    outs = rest[: len(rest) - 3]
    heads, grad_all, acc = rest[len(rest) - 3 :]
    part_ref, normed_ref, low_ref, low_part, grad_down_low, act_ref, gup_ref, down_low = outs[:8]
    block = tokens[0].shape[0]
    width = in_all.shape[1] // count
    for i in range(size):
        part = pl.ds(i * block, block)
        for d in range(count):
            spot = place_of(ids[i], d, count // 2) * block
            for p in range(pairs):
                at = d * width + p * PAIR
                heads[part, at : at + PAIR] = attended[d * pairs + p][pl.ds(spot, block), :]
        keep = mask[pl.ds(ids[i] * block, block), :]
        grad = grads[i][...]
        grad_all[part, :] = grad
        grad_down_low[part, :] = (dot_back(grad, down_out[...]) * keep).astype(BF)
        rows = heads[part, :]
        low = (dot_back(rows, in_all[...]) * keep).astype(BF)
        mid = dot(rows, w_all[...]) + dot(low, proj_out[...]) + proj_bias[...] + tokens[i][...].astype(F32)
        unit, _ = norm_parts(mid)
        normed = (unit * gain[...] + shift[...]).astype(BF)
        normed_ref[part, :] = normed
        low_ref[part, :] = (dot_back(normed, up_in[...]) * keep).astype(BF)
        if len(outs) > 8 and i == 0:
            outs[8][...] = low
            outs[9][...] = mid
    low_sum = None
    down_sum = None
    hid = up_w.shape[1]
    for j in range(hid // chunk):
        cut = pl.ds(j * chunk, chunk)
        upper = dot(normed_ref[...], up_w[:, cut]) + dot(low_ref[...], up_out[:, cut]) + up_b[:, cut]
        grad = dot_back(grad_all[...], down_w[cut, :]) + dot(grad_down_low[...], down_in[:, cut])
        square = upper * upper
        curve = jnp.tanh(GELU_A * upper * (1.0 + GELU_B * square))
        half = 0.5 * (1.0 + curve)
        active = (upper * half).astype(BF)
        act_ref[:, cut] = active
        slope = half + 0.5 * upper * (1.0 - curve * curve) * (GELU_A * (1.0 + 3.0 * GELU_B * square))
        grad_upper = (grad * slope).astype(BF)
        gup_ref[:, cut] = grad_upper
        part = dot_back(grad_upper, up_w[:, cut])
        low = dot_back(grad_upper, up_out[:, cut])
        down = dot_back(active, down_in[:, cut])
        acc[...] = part if j == 0 else acc[...] + part
        low_sum = low if j == 0 else low_sum + low
        down_sum = down if j == 0 else down_sum + down
    for i in range(size):
        cut = slice(i * block, (i + 1) * block)
        part = pl.ds(i * block, block)
        keep = mask[pl.ds(ids[i] * block, block), :]
        low = (low_sum[cut] * keep).astype(BF)
        low_part[part, :] = low
        down_low[part, :] = (down_sum[cut] * keep).astype(BF)
        part_ref[part, :] = (acc[part, :] + dot(low, up_in[...])).astype(BF)


def down_body(groups, down_w, down_out, *refs):
    for g in range(groups):
        act, low, out = refs[g], refs[groups + g], refs[2 * groups + g]
        out[...] = (dot(act[...], down_w[...]) + dot(low[...], down_out[...])).astype(BF)


def hidden_grads_body(groups, sizes, pick, *refs):
    low2 = refs[:groups]
    gup = refs[groups : 2 * groups]
    gdl = refs[2 * groups : 3 * groups]
    act = refs[3 * groups : 4 * groups]
    part = refs[4 * groups : 5 * groups]
    normed = refs[5 * groups : 6 * groups]
    down = refs[6 * groups : 7 * groups]
    rest = refs[7 * groups :]
    total = sum(sizes)
    grads = rest[:total]
    pack, up_in, down_out = rest[total:]
    hid = gup[0].shape[1]
    block = grads[0].shape[0]
    add = lambda left, right: sum([dot_over(a[...], b[...]) for a, b in zip(left[1:], right[1:])], dot_over(left[0][...], right[0][...]))
    pack[:, :hid] = add(low2, gup).astype(BF)
    pack[:, hid : 2 * hid] = add(gdl, act).astype(BF)
    pack[:, 2 * hid :] = pick[...]
    up_in[...] = add(part, normed)
    at = 0
    out = None
    for g in range(groups):
        for i in range(sizes[g]):
            term = dot_over(down[g][pl.ds(i * block, block), :], grads[at][...])
            out = term if out is None else out + term
            at += 1
    down_out[...] = out


def add_body(left, right, out):
    out[...] = (left[...].astype(F32) + right[...].astype(F32)).astype(BF)


def mid_back_body(count, mask, cotangent, mid, gain, proj_out, w_all, in_all, *refs):
    pieces = refs[: count[0]]
    grad_mid, grad_attn, grad_low = refs[count[0] : count[0] + 3]
    outs = refs[count[0] + 3 :]
    block = mid.shape[0]
    upstream = pieces[0][pl.ds(0, block), :].astype(F32)
    for piece in pieces[1:]:
        upstream = upstream + piece[...].astype(F32)
    unit, inv = norm_parts(mid[...])
    total = cotangent[...] + norm_back(unit, inv, upstream * gain[...])
    grad_mid[...] = total
    attn = total.astype(BF)
    grad_attn[...] = attn
    low = (dot_back(attn, proj_out[...]) * mask[pl.ds(0, block), :]).astype(BF)
    grad_low[...] = low
    value = (dot_back(attn, w_all[...]) + dot(low, in_all[...])).astype(BF)
    width = outs[0].shape[1]
    for d in range(count[1]):
        outs[d][...] = value[:, d * width : (d + 1) * width]


def message_body(count, pairs, me, up_in, down_out, proj_low, grad_attn, grad_low, *refs):
    attended = refs[: count * pairs]
    outs = refs[count * pairs : count * pairs + count]
    proj_out = refs[count * pairs + count]
    rank = up_in.shape[0]
    block = grad_low.shape[0]
    width = outs[0].shape[1]
    proj_out[...] = dot_over(proj_low[...], grad_attn[...])
    for d in range(count):
        spot = place_of(0, d, count // 2) * block
        lanes = pl.ds(pl.multiple_of(owner_of(me[0], d, count) * width, width), width)
        outs[d][pl.ds(0, rank), :] = up_in[:, lanes].astype(BF)
        outs[d][pl.ds(rank, rank), :] = down_out[:, lanes].astype(BF)
        outs[d][pl.ds(2 * rank, rank), :] = proj_out[:, lanes].astype(BF)
        for p in range(pairs):
            outs[d][pl.ds(3 * rank, rank), p * PAIR : (p + 1) * PAIR] = dot_over(
                grad_low[...], attended[d * pairs + p][pl.ds(spot, block), :]
            ).astype(BF)


def pack_body(count, plain, pick, *refs):
    fixed = refs[:plain]
    messages = refs[plain : plain + count]
    out = refs[plain + count]
    rank = pick.shape[0]
    at = 0
    for ref in fixed:
        out[:, at : at + ref.shape[1]] = ref[...]
        at += ref.shape[1]
    width = messages[0].shape[1]
    for k in range(messages[0].shape[0] // rank):
        total = messages[0][pl.ds(k * rank, rank), :].astype(F32)
        for d in range(1, count):
            total = total + messages[d][pl.ds(k * rank, rank), :].astype(F32)
        out[:, at : at + width] = total.astype(BF)
        at += width
    out[:, at : at + pick.shape[1]] = pick[...]


def attend_back_body(pair, pairs, count, seq_len, *refs):
    first, last = pair == 0, pair == pairs - 1
    at = 0

    def take(number):
        nonlocal at
        at += number
        return refs[at - number : at]

    if last:
        (me,) = take(1)
    seq, kept = take(2)
    if first:
        pull_near, pull_far = take(2)
        grads = take(count)
    else:
        (grad_seq,) = take(1)
    if last:
        push, low_t, n1_near, n1_far, low_out = take(5)
        earlier = take(3 * (pairs - 1))
    grad_q, grad_k, grad_v = take(3)
    if last:
        part_t, qkv_out = take(2)
        messages = take(count)
    if first:
        grad_seq, grad_all = take(2)
    if last:
        part_seq, total_in = take(2)
    rows = seq.shape[0]
    width = seq.shape[1] // 3
    step = min(256, seq_len)
    scale = 1.0 / math.sqrt(HD)
    if first:
        block = grads[0].shape[0]
        near = pull_near.shape[1]
        for i in range(count):
            grad_all[pl.ds(i * block, block), :] = grads[i][...]
        grad_seq[...] = (
            dot(pull_near[...], grad_all[pl.ds(0, near), :])
            + dot(pull_far[...], grad_all[pl.ds(near, rows - near), :])
        ).astype(BF)
    if last:
        for p in range(pairs - 1):
            span = slice(p * PAIR, (p + 1) * PAIR)
            grad_q[span, :] = earlier[3 * p][...]
            grad_k[:, span] = earlier[3 * p + 1][...]
            grad_v[:, span] = earlier[3 * p + 2][...]
    base_row = pair * PAIR if last else 0

    def one_sequence(s):
        base = s * seq_len
        lanes = pl.ds(pair * PAIR, PAIR)
        keys = seq[pl.ds(base, seq_len), pl.ds(width + pair * PAIR, PAIR)]
        values = seq[pl.ds(base, seq_len), pl.ds(2 * width + pair * PAIR, PAIR)]
        keys_t = keys.astype(F32).T.astype(BF)
        steps = seq_len // step
        sums_k = [None] * steps
        sums_v = [None] * steps
        for q in range(steps):
            span = pl.ds(base + q * step, step)
            queries = seq[span, lanes]
            grad = grad_seq[span, lanes]
            seen = (q + 1) * step
            for h in range(2):
                own_q = head_lanes(queries, h)
                own_g = head_lanes(grad, h)
                probs = kept[s, h, :seen, q * step : (q + 1) * step]
                wide_probs = probs.astype(F32)
                mixed = wide_probs * dot_back(values[:seen], own_g)
                centre = jnp.sum(mixed, 0, keepdims=True)
                raw = (mixed - wide_probs * centre).astype(BF)
                grad_q[pl.ds(base_row + h * HD, HD), span] = (
                    dot(keys_t[h * HD : (h + 1) * HD, :seen], raw) * scale
                ).astype(BF)
                to_k = dot(raw, own_q)
                to_v = dot(probs, own_g)
                for b in range(q + 1):
                    cut = slice(b * step, (b + 1) * step)
                    sums_k[b] = to_k[cut] if sums_k[b] is None else sums_k[b] + to_k[cut]
                    sums_v[b] = to_v[cut] if sums_v[b] is None else sums_v[b] + to_v[cut]
        for b in range(steps):
            span = pl.ds(base + b * step, step)
            grad_k[span, pl.ds(base_row, PAIR)] = sums_k[b].astype(BF)
            grad_v[span, pl.ds(base_row, PAIR)] = sums_v[b].astype(BF)

    for s in range(rows // seq_len):
        one_sequence(s)
    if not last:
        return
    near = n1_near.shape[0]
    part = dot(low_out[0], grad_q[...]) + dot_back(low_out[1], grad_k[...]) + dot_back(low_out[2], grad_v[...])
    lane_at = lax.broadcasted_iota(jnp.int32, part.shape, 1) // seq_len
    rank_at = lax.broadcasted_iota(jnp.int32, part.shape, 0) // RANK
    part_seq[...] = jnp.where(lane_at == rank_at, part, 0.0).astype(BF)
    part_t[...] = dot_back(part_seq[...], push[...]).astype(BF)
    total_in[...] = dot(part_t[:, :near], n1_near[...]) + dot(part_t[:, near:], n1_far[...])
    qkv_out[:, :width] = dot_back(low_t[...], grad_q[...]).astype(BF)
    qkv_out[:, width : 2 * width] = dot(low_t[...], grad_k[...]).astype(BF)
    qkv_out[:, 2 * width :] = dot(low_t[...], grad_v[...]).astype(BF)
    for d in range(count):
        lanes = pl.ds(pl.multiple_of(owner_of(me[0], d, count) * width, width), width)
        messages[d][...] = total_in[:, lanes].astype(BF)


def qkv_back_body(ids, push, w_cat, low_in, grad_q, grad_k, grad_v, part_t, out, joined):
    block = out.shape[0] // len(ids)
    width = grad_k.shape[1]
    for i, at in enumerate(ids):
        rows = pl.ds(i * block, block)
        place = push[pl.ds(at * block, block), :]
        joined[rows, :width] = dot_back(place, grad_q[...]).astype(BF)
        joined[rows, width : 2 * width] = dot(place, grad_k[...]).astype(BF)
        joined[rows, 2 * width :] = dot(place, grad_v[...]).astype(BF)
    for i, at in enumerate(ids):
        rows = pl.ds(i * block, block)
        low = dot_over(part_t[:, at * block : (at + 1) * block], low_in[...])
        out[rows, :] = (dot_back(joined[rows, :], w_cat[...]) + low).astype(BF)


def add_pieces(total, pieces, block):
    total = total + pieces[0][pl.ds(0, block), :].astype(F32) + pieces[1][...].astype(F32)
    halves = pieces[2:]
    number = len(halves) // 2
    for i in range(number):
        total = total + jnp.concatenate(
            [halves[i][...].astype(F32), halves[number + i][...].astype(F32)], 0
        )
    return total


def input_back_body(tokens, grad_mid, gain, *refs):
    out = refs[-1]
    upstream = add_pieces(0.0, refs[:-1], tokens.shape[0])
    unit, inv = norm_parts(tokens[...].astype(F32))
    out[...] = grad_mid[...] + norm_back(unit, inv, upstream * gain[...])


def result_body(mid, bias, *refs):
    refs[-1][...] = add_pieces(mid[...] + bias[...], refs[:-1], mid.shape[0])


def spread_hidden_body(hid, found, up_out, down_in):
    pick = found[:, 2 * hid :]
    up_out[...] = dot_over(pick, found[:, :hid])
    down_in[...] = dot_over(found[:, hid : 2 * hid], pick)


def spread_wide_body(width, found, proj_in, wide):
    pick = found[:, 4 * width :]
    for k in range(3):
        wide[pl.ds(k * 128, 128), :] = dot_over(pick, found[:, k * width : (k + 1) * width]).astype(BF)
    proj_in[...] = dot_over(found[:, 3 * width : 4 * width], pick)


def spread_late_body(width, found, qkv_out, wide):
    pick = found[:, 4 * width :]
    for k in range(3):
        qkv_out[k] = dot_over(pick, found[:, k * width : (k + 1) * width])
    wide[...] = dot_over(pick, found[:, 3 * width : 4 * width]).astype(BF)


def place_wide_body(count, me, *refs):
    messages = refs[:count]
    up_in, down_out, proj_out = refs[count:]
    width = messages[0].shape[1]
    for d in range(count):
        span = pl.ds(pl.multiple_of(owner_of(me[0], d, count) * width, width), width)
        up_in[span, :] = messages[d][pl.ds(0, 128), :].astype(F32).T
        down_out[:, span] = messages[d][pl.ds(128, 128), :].astype(F32)
        proj_out[:, span] = messages[d][pl.ds(256, 128), :].astype(F32)


def place_late_body(count, me, *refs):
    messages = refs[:count]
    qkv_in = refs[count]
    width = messages[0].shape[1]
    for d in range(count):
        qkv_in[pl.ds(pl.multiple_of(owner_of(me[0], d, count) * width, width), width), :] = messages[d][...].astype(F32).T


def tie(value, *others):
    return lax.optimization_barrier((value, *others))[0]


def body(
    tensor_size,
    dp_size,
    tokens,
    cotangent,
    lengths,
    order,
    adapter_ids,
    norm1_gain,
    norm1_shift,
    qkv_weight,
    qv_bias,
    proj_weight,
    proj_bias,
    norm2_gain,
    norm2_shift,
    up_weight,
    up_bias,
    down_weight,
    down_bias,
    adapt_qkv_in,
    adapt_qkv_out,
    adapt_proj_in,
    adapt_proj_out,
    adapt_up_in,
    adapt_up_out,
    adapt_down_in,
    adapt_down_out,
):
    count = tensor_size
    chips = count // 2
    own, wide = tokens.shape
    width = qkv_weight.shape[2]
    pairs = width // PAIR
    hid = up_weight.shape[1]
    rows = order.shape[1]
    seqs = lengths.shape[1]
    seq_len = rows // seqs
    ranks = seqs * RANK
    near = 2 * own
    far = rows - near
    cols = adapt_qkv_in.shape[1]
    near_ids = (0, 1)
    even_ids = tuple(range(2, count, 2))
    odd_ids = tuple(range(3, count, 2))
    me = lax.axis_index("tensor")

    core_perm = [(t, t ^ 1) for t in range(count)]

    def core_swap(value):
        return lax.ppermute(value, "tensor", core_perm)

    def chip_hop(value, k):
        return lax.ppermute(value, "tensor", [(t, ((t // 2 + k) % chips) * 2 + t % 2) for t in range(count)])

    def hops_of(value):
        return [chip_hop(value, k) for k in range(1, chips)]

    def weave(value, swapped, moved):
        found = [value, swapped]
        for item in moved:
            found += [item, core_swap(item)]
        return found

    def exchange(messages):
        out = [messages[0], core_swap(messages[1])] + [None] * (count - 2)
        for k in range(1, chips):
            flat = [(t, ((t // 2 - k) % chips) * 2 + t % 2) for t in range(count)]
            cross = [(t, ((t // 2 - k) % chips) * 2 + (t % 2 ^ 1)) for t in range(count)]
            out[2 * (chips - k)] = lax.ppermute(messages[2 * k], "tensor", flat)
            out[2 * (chips - k) + 1] = lax.ppermute(messages[2 * k + 1], "tensor", cross)
        return out

    def join(left, right, name):
        return whole_call(add_body, [left, right], [shape(left.shape, BF)], name)[0]

    def send_far(joined):
        return [chip_hop(joined[(k - 1) * own : k * own] if chips > 2 else joined, -k) for k in range(1, chips)]

    def send_half(joined, part):
        half = own // 2
        return [
            chip_hop(joined[(k - 1) * own + part * half : (k - 1) * own + (part + 1) * half], -k)
            for k in range(1, chips)
        ]

    def dp_swap(value, stride):
        return lax.ppermute(value, "dp", [(i, i ^ stride) for i in range(dp_size)])

    def double(value, moved):
        return jnp.concatenate([value, moved], 0)

    def widen(value, stride):
        while stride:
            value = double(value, dp_swap(value, stride))
            stride //= 2
        return value

    place = me.reshape(1)
    dp_at = lax.axis_index("dp").reshape(1)
    weight_three = jnp.transpose(qkv_weight, (1, 0, 2))
    out_three = jnp.transpose(adapt_qkv_out, (1, 0, 2))
    row = lambda v: v.reshape(1, -1)

    top = dp_size // 2
    token_core = core_swap(tokens)
    token_hops = hops_of(tokens)
    grad_own = tie(cotangent, token_core).astype(BF)
    grad_core = core_swap(grad_own)

    prepared = whole_call(
        functools.partial(prep_body, seq_len, own, count),
        [order, proj_weight, adapt_qkv_in, out_three, adapt_proj_in, adapt_proj_out, adapt_up_in, adapt_up_out, adapt_down_in,
         adapt_down_out],
        [shape((ranks, wide), BF), shape((3, ranks, width), BF), shape((width + 16, wide), BF),
         shape((ranks, wide), BF), shape((ranks, wide), BF), shape((ranks, hid), BF),
         shape((ranks, hid), BF), shape((ranks, wide), BF), shape((rows, near), BF), shape((rows, far), BF),
         shape((rows, rows), BF), shape((rows, ranks), F32), shape((ranks, cols), BF), shape((1, rows), jnp.int32),
         shape((width // 2 + 16, wide), BF)],
        "prep",
        smem=[place, dp_at, lengths, adapter_ids],
        loose=tuple(range(10)),
    )
    c_qkv_in, c_qkv_out, proj_own, c_proj_out, c_up_in, c_up_out, c_down_in, c_down_out = prepared[:8]
    pull_near, pull_far, push, mask, pick, limit, proj_half = prepared[8:]
    proj_core = core_swap(proj_own)
    proj_hops = hops_of(proj_half)

    norm1 = [row(norm1_gain), row(norm1_shift), weight_three, qv_bias, c_qkv_in, c_qkv_out]
    n1_near, low1_near, moved_near = whole_call(
        functools.partial(qkv_body, near_ids, False),
        [mask] + norm1 + [pull_near, tokens, token_core],
        [shape((near, wide), BF), shape((near, ranks), BF), shape((rows, 3 * width), F32)],
        "qkv_near",
        loose=(1, 2, 3, 4, 8, 9),
        long=True,
        scratch=[pltpu.VMEM((near, 3 * width), BF)],
    )
    token_hops = [tie(item, low1_near) for item in token_hops]
    token_blocks = weave(tokens, token_core, token_hops)
    n1_far, low1_far, qkv_seq = whole_call(
        functools.partial(qkv_body, tuple(range(2, count)), True),
        [mask] + norm1 + [pull_far] + token_blocks[2:] + [moved_near],
        [shape((far, wide), BF), shape((far, ranks), BF), shape((rows, 3 * width), BF)],
        "qkv_far",
        scratch=[pltpu.VMEM((far, 3 * width), BF)],
    )

    grad_hops = hops_of(tie(grad_own, low1_far))
    sums = []
    attended = []
    seq_in = qkv_seq
    for pair in range(pairs):
        part, kept = whole_call(
            functools.partial(attend_body, seq_len, pair),
            [limit, seq_in, push],
            [shape((rows, PAIR), BF), shape((seqs, 2, seq_len, seq_len), BF)],
            f"attend{pair}",
            scratch=[pltpu.VMEM((PAIR, rows), BF)],
        )
        sums.append(kept)
        attended.append(part)
        if pair == 0:
            seq_in = tie(qkv_seq, part)
    after = attended[-1]
    gathered_heads = []
    for part in attended:
        gathered_heads.append(weave(part, core_swap(part), hops_of(part)))
    heads = [gathered_heads[p][d] for d in range(count) for p in range(pairs)]

    proj_parts = []
    for item in proj_hops:
        item = tie(item, after)
        other = dp_swap(item[: width // 2], 1)
        proj_parts += [item, other, core_swap(item), core_swap(other)]
    grad_blocks = weave(grad_own, grad_core, [tie(item, after) for item in grad_hops])
    w_all, in_all, w_cat, low_t = whole_call(
        functools.partial(join_body, count),
        [low1_near, low1_far, push, weight_three, proj_own, proj_core] + proj_parts,
        [shape((wide, wide), BF), shape((ranks, wide), BF), shape((wide, 3 * width), BF), shape((ranks, rows), BF)],
        "join",
        smem=[dp_at],
    )

    def block_call(ids, gate, name):
        size = len(ids) * own
        extra = [shape((own, ranks), BF), shape((own, wide), F32)] if 0 in ids else []
        keep = mask if gate is None else tie(mask, gate)
        return whole_call(
            functools.partial(block_body, ids, count, pairs, min(512, hid)),
            [keep, w_all, in_all, c_proj_out, row(proj_bias), row(norm2_gain), row(norm2_shift), c_up_in, up_weight,
             row(up_bias), c_up_out, down_weight, c_down_in, c_down_out]
            + [token_blocks[i] for i in ids] + [grad_blocks[i] for i in ids] + heads,
            [shape((size, wide), BF), shape((size, wide), BF), shape((size, ranks), BF), shape((size, ranks), BF),
             shape((size, ranks), BF), shape((size, hid), BF), shape((size, hid), BF), shape((size, ranks), BF)]
            + extra,
            name,
            scratch=[pltpu.VMEM((size, wide), BF), pltpu.VMEM((size, wide), BF), pltpu.VMEM((size, wide), F32)],
            long=gate is not None,
        )

    odd = block_call(odd_ids, None, "block_odd")
    odd_moved = core_swap(odd[0])
    even = block_call(even_ids, odd[3], "block_even")
    up_joined = join(even[0], odd_moved, "up_join")
    up_hops = send_far(up_joined)
    mine = block_call(near_ids, up_joined, "block_near")
    up_swap = core_swap(mine[0][own:])
    groups = (mine, even, odd)
    order_ids = (near_ids, even_ids, odd_ids)
    pack_hidden, p_up_in, p_down_out = whole_call(
        functools.partial(hidden_grads_body, 3, tuple(len(i) for i in order_ids)),
        [pick] + [g[k] for k in (2, 6, 4, 5, 3, 1, 7) for g in groups]
        + [grad_blocks[i] for ids in order_ids for i in ids],
        [shape((ranks, 2 * hid + cols), BF), shape((ranks, wide), F32), shape((ranks, wide), F32)],
        "hidden_grads",
    )
    up_hops = [tie(item, p_up_in) for item in up_hops]
    proj_low, mid = mine[8:]
    back = whole_call(
        functools.partial(mid_back_body, (2 + len(up_hops), count)),
        [mask, cotangent, mid, row(norm2_gain), c_proj_out, w_all, in_all, mine[0], up_swap] + up_hops,
        [shape((own, wide), F32), shape((own, wide), BF), shape((own, ranks), BF)]
        + [shape((own, width), BF)] * count,
        "mid_back",
        long=True,
    )
    grad_mid, grad_attn, grad_proj_low = back[:3]
    grad_att = exchange(back[3:])
    hidden_moved = dp_swap(tie(pack_hidden, grad_proj_low), top)

    messages = whole_call(
        functools.partial(message_body, count, pairs),
        [p_up_in, p_down_out, proj_low, grad_attn, grad_proj_low] + heads,
        [shape((4 * ranks, width), BF)] * count,
        "message",
        smem=[place],
        scratch=[pltpu.VMEM((ranks, wide), F32)],
        long=True,
    )
    down_parts = whole_call(
        functools.partial(down_body, 3),
        [tie(down_weight, messages[0]), c_down_out] + [g[5] for g in groups] + [g[7] for g in groups],
        [shape(g[0].shape, BF) for g in groups],
        "down",
        long=True,
    )
    down_mine, down_even, down_odd = down_parts
    grad_att = [grad_att[0]] + [tie(item, down_mine) for item in grad_att[1:]]
    wide_messages = exchange([tie(item, *grad_att[1:]) for item in messages])
    down_moved = core_swap(tie(down_odd, *grad_att[1:]))
    down_swap = core_swap(tie(down_mine[own:], *grad_att[1:]))

    back_pieces = []
    grad_seq = None
    for pair in range(pairs):
        last = pair == pairs - 1
        inputs = [qkv_seq, sums[pair]]
        outs = [shape((PAIR, rows), BF), shape((rows, PAIR), BF), shape((rows, PAIR), BF)]
        scratch = []
        if pair == 0:
            inputs += [pull_near, pull_far] + grad_att
        else:
            inputs += [grad_seq]
        if last:
            inputs += [push, low_t, n1_near, n1_far, c_qkv_out] + back_pieces
            outs = [shape((width, rows), BF), shape((rows, width), BF), shape((rows, width), BF),
                    shape((ranks, rows), BF), shape((ranks, 3 * width), BF)] + [shape((ranks, width), BF)] * count
        if pair == 0:
            if last:
                scratch += [pltpu.VMEM((rows, width), BF)]
            else:
                outs += [shape((rows, width), BF)]
            scratch += [pltpu.VMEM((rows, width), BF)]
        if last:
            scratch += [pltpu.VMEM((ranks, rows), BF), pltpu.VMEM((ranks, wide), F32)]
        results = whole_call(
            functools.partial(attend_back_body, pair, pairs, count, seq_len),
            inputs,
            outs,
            f"attend_back{pair}",
            smem=[place] if last else [],
            scratch=scratch,
            long=True,
        )
        if pair == 0:
            passed = results[0]
            wide_messages = [wide_messages[0]] + [tie(item, passed) for item in wide_messages[1:]]
            (pack_wide,) = whole_call(
                functools.partial(pack_body, count, 0),
                [pick] + wide_messages,
                [shape((ranks, 4 * width + cols), BF)],
                "pack_wide",
            )
            hidden_half = double(pack_hidden, tie(hidden_moved, passed, *wide_messages))
            hidden_moved = dp_swap(hidden_half, top // 2)
            hidden_first = dp_swap(hidden_half, top // 4)
            wide_moved = dp_swap(pack_wide, top)
            down_joined = join(down_even, tie(down_moved, passed, *wide_messages), "down_join")
            down_first = send_half(down_joined, 0)
        if not last:
            back_pieces += list(results[:3])
            grad_seq = tie(results[3], pack_wide, hidden_half, down_joined)
    grad_q, grad_k, grad_v, part_t, g_qkv_out = results[:5]
    down_first = [tie(item, part_t) for item in down_first]
    hidden_moved = tie(hidden_moved, part_t)
    hidden_first = tie(hidden_first, part_t)
    late_messages = exchange(results[5:])
    hidden_second = dp_swap(hidden_moved, top // 4)
    wide_moved_first = tie(wide_moved, part_t)
    wide_found = double(pack_wide, wide_moved_first)
    wide_moved = dp_swap(wide_found, top // 2)

    def unproject(ids, gates, name):
        size = len(ids) * own
        return whole_call(
            functools.partial(qkv_back_body, ids),
            [push, w_cat, c_qkv_in, grad_q, grad_k, grad_v, tie(part_t, *gates)],
            [shape((size, wide), BF)],
            name,
            scratch=[pltpu.VMEM((size, 3 * width), BF)],
            long=True,
        )[0]

    odd_part = unproject(odd_ids, [wide_moved_first, hidden_moved, hidden_first, *down_first], "qkv_back_odd")
    odd_moved = core_swap(odd_part)
    even_part = unproject(even_ids, [odd_part], "qkv_back_even")
    qkv_joined = join(even_part, tie(odd_moved, *late_messages[1:], wide_moved), "qkv_join")
    qkv_first = send_half(qkv_joined, 0)
    late_messages = [late_messages[0]] + [tie(item, qkv_joined) for item in late_messages[1:]]
    (pack_late,) = whole_call(
        functools.partial(pack_body, count, 1),
        [pick, g_qkv_out] + late_messages,
        [shape((ranks, 4 * width + cols), BF)],
        "pack_late",
    )
    late_moved = dp_swap(pack_late, top)
    wide_found = double(wide_found, wide_moved)
    wide_moved = dp_swap(wide_found, top // 4)
    near_part = unproject(near_ids, [qkv_joined, pack_late, hidden_second], "qkv_back_near")
    qkv_swap = core_swap(near_part[own:])
    qkv_first = [tie(item, near_part) for item in qkv_first]
    qkv_second = send_half(tie(qkv_joined, *qkv_first), 1)
    late_found = double(pack_late, tie(late_moved, near_part, *qkv_first))
    late_moved = dp_swap(late_found, top // 2)
    late_moved = tie(late_moved, *qkv_second)
    wide_found = widen(double(wide_found, tie(wide_moved, late_moved)), top // 8)
    proj_in_full, wide_part = whole_call(
        functools.partial(spread_wide_body, width),
        [wide_found],
        [shape((width, cols), F32), shape((3 * cols, width), BF)],
        "spread_wide",
        final=(0,),
    )
    wide_blocks = weave(wide_part, core_swap(wide_part), hops_of(wide_part))
    late_found = double(late_found, late_moved)
    late_moved = dp_swap(late_found, top // 4)
    down_second = send_half(tie(down_joined, *qkv_second), 1)
    (grad_input,) = whole_call(
        input_back_body,
        [tokens, grad_mid, row(norm1_gain), near_part, qkv_swap, *qkv_first, *qkv_second],
        [shape((own, wide), F32)],
        "input_back",
        final=(0,),
    )
    up_in_full, down_out_full, proj_out_full = whole_call(
        functools.partial(place_wide_body, count),
        [tie(wide_blocks[0], grad_input)] + wide_blocks[1:],
        [shape((wide, cols), F32), shape((cols, wide), F32), shape((cols, wide), F32)],
        "place_wide",
        smem=[place],
        final=(0, 1, 2),
    )
    late_found = widen(double(late_found, tie(late_moved, grad_input)), top // 8)
    qkv_out_full, late_part = whole_call(
        functools.partial(spread_late_body, width),
        [late_found],
        [shape((3, cols, width), F32), shape((cols, width), BF)],
        "spread_late",
        final=(0,),
    )
    late_blocks = weave(late_part, core_swap(late_part), hops_of(late_part))
    (result,) = whole_call(
        result_body,
        [mid, row(down_bias), down_mine, down_swap, *down_first, *[tie(item, late_part) for item in down_second]],
        [shape((own, wide), F32)],
        "result",
        final=(0,),
    )
    hidden_found = jnp.concatenate([hidden_half, hidden_moved, hidden_first, tie(hidden_second, result)], 0)
    up_out_full, down_in_full = whole_call(
        functools.partial(spread_hidden_body, hid),
        [widen(hidden_found, top // 8)],
        [shape((cols, hid), F32), shape((hid, cols), F32)],
        "spread_hidden",
        final=(0, 1),
    )
    (qkv_in_full,) = whole_call(
        functools.partial(place_late_body, count),
        [late_blocks[0]] + [tie(item, up_out_full) for item in late_blocks[1:]],
        [shape((wide, cols), F32)],
        "place_late",
        smem=[place],
        final=(0,),
    )
    return (
        result,
        grad_input,
        qkv_in_full,
        jnp.transpose(qkv_out_full, (1, 0, 2)),
        proj_in_full,
        proj_out_full,
        up_in_full,
        up_out_full,
        down_in_full,
        down_out_full,
    )


def solution(mesh):
    in_specs = (
        P(("dp", "tensor"), None),
        P(("dp", "tensor"), None),
        P("dp", None),
        P("dp", None),
        P("dp", None),
        P(),
        P(),
        P(None, None, "tensor"),
        P(None, "tensor"),
        P("tensor", None),
        P(),
        P(),
        P(),
        P(None, "tensor"),
        P("tensor"),
        P("tensor", None),
        P(),
        P(),
        P(None, None, "tensor"),
        P("tensor", None),
        P(),
        P(),
        P(None, "tensor"),
        P("tensor", None),
        P(),
    )
    out_specs = (
        P(("dp", "tensor"), None),
        P(("dp", "tensor"), None),
        P(),
        P(None, None, "tensor"),
        P("tensor", None),
        P(),
        P(),
        P(None, "tensor"),
        P("tensor", None),
        P(),
    )
    run = functools.partial(body, mesh.shape["tensor"], mesh.shape["dp"])
    return jax.shard_map(run, mesh=mesh, in_specs=in_specs, out_specs=out_specs, check_vma=False)
```

```python
import functools
import math

import jax
import jax.numpy as jnp
from jax import lax
from jax.experimental import pallas as pl
from jax.experimental.pallas import tpu as pltpu
from jax.sharding import PartitionSpec as P

HD = 64
RANK = 16
PAIR = 2 * HD
EPSILON = 1e-05
NEGATIVE = -1000000000.0
BF = jnp.bfloat16
F32 = jnp.float32
LIMIT = 10 * 1024 * 1024
GELU_A = math.sqrt(2.0 / math.pi)
GELU_B = 0.044715


def dot(left, right):
    return jnp.dot(left, right, preferred_element_type=F32)


def dot_back(left, right):
    return lax.dot_general(left, right, (((1,), (1,)), ((), ())), preferred_element_type=F32)


def dot_over(left, right):
    return lax.dot_general(left, right, (((0,), (0,)), ((), ())), preferred_element_type=F32)


def shape(dims, kind):
    return jax.ShapeDtypeStruct(tuple(dims), kind)


def whole_call(body, inputs, outs, name, smem=(), scratch=(), final=(), loose=(), long=False):
    smem_spec = pl.BlockSpec(memory_space=pltpu.SMEM)
    vmem_spec = pl.BlockSpec(memory_space=pltpu.VMEM)
    held = [
        pltpu.with_memory_space_constraint(x, pltpu.HBM if i in loose else pltpu.VMEM) for i, x in enumerate(inputs)
    ]
    kinds = [o if i in final else pltpu.VMEM(o.shape, o.dtype) for i, o in enumerate(outs)]
    return pl.pallas_call(
        body,
        out_shape=kinds,
        in_specs=[smem_spec] * len(smem) + [vmem_spec] * len(inputs),
        out_specs=[vmem_spec] * len(outs),
        scratch_shapes=list(scratch),
        compiler_params=pltpu.CompilerParams(vmem_limit_bytes=LIMIT),
        name=name,
    )(*smem, *held)


def norm_parts(values):
    centre = values - jnp.mean(values, -1, keepdims=True)
    spread = jnp.mean(centre * centre, -1, keepdims=True)
    inv = lax.rsqrt(spread + EPSILON)
    return centre * inv, inv


def norm_back(normed, inv, upstream):
    return inv * (
        upstream
        - jnp.mean(upstream, -1, keepdims=True)
        - normed * jnp.mean(upstream * normed, -1, keepdims=True)
    )


def rows_at(i, size):
    return pl.ds(pl.multiple_of(i * size, size), size)


def repeat(count, step):
    if count == 1:
        step(0)
    else:
        lax.fori_loop(0, count, lambda i, carry: (step(i), carry)[1], 0)


def owner_of(me, d, count):
    return (((me // 2) + count // 2 - d // 2) % (count // 2)) * 2 + ((me % 2 + d % 2) % 2)


def prep_body(
    seq_len, own, count, me, dp_at, lengths, ids, order, proj_w, qkv_in, qkv_out, proj_in, proj_out, up_in, up_out,
    down_in, down_out, *outs
):
    o_qkv_in, o_qkv_out, o_proj, o_proj_out, o_up_in, o_up_out, o_down_in, o_down_out = outs[:8]
    pull_near, pull_far, push, mask, pick, limit, o_half, tall_ref = outs[8:]
    rank_at = lax.broadcasted_iota(jnp.int32, pick.shape, 0)
    col_at = lax.broadcasted_iota(jnp.int32, pick.shape, 1)
    wanted = rank_at + ids[0, 0] * RANK
    slot = lax.broadcasted_iota(jnp.int32, limit.shape, 1)
    bound = jnp.minimum(slot + 1, lengths[0, 0])
    for s in range(1, lengths.shape[1]):
        wanted = jnp.where(rank_at >= s * RANK, rank_at - s * RANK + ids[0, s] * RANK, wanted)
        bound = jnp.where(slot >= s * seq_len, jnp.minimum(slot - s * seq_len + 1, lengths[0, s]), bound)
    limit[...] = bound
    chosen = jnp.where(col_at == wanted, 1.0, 0.0).astype(BF)
    pick[...] = chosen
    width = proj_w.shape[0]
    fold = pick.shape[0] // count
    o_proj[pl.ds(0, width), :] = proj_w[...]
    o_proj[pl.ds(width, 16), :] = jnp.zeros((16, o_proj.shape[1]), BF)
    chosen_in = dot_back(chosen, proj_in[...])
    for j in range(count):
        o_proj[pl.ds(width, fold), j * width : (j + 1) * width] = chosen_in[j * fold : (j + 1) * fold].astype(BF)
    half = width // 2
    o_half[pl.ds(0, half), :] = proj_w[pl.ds(pl.multiple_of(dp_at[0] % 2 * half, half), half), :]
    o_half[pl.ds(half, 16), :] = o_proj[pl.ds(width, 16), :]
    o_qkv_in[...] = dot_back(chosen, qkv_in[...]).astype(BF)
    for k in range(3):
        o_qkv_out[k] = dot(chosen, qkv_out[k]).astype(BF)
    o_proj_out[...] = dot(chosen, proj_out[...]).astype(BF)
    o_up_in[...] = dot_back(chosen, up_in[...]).astype(BF)
    o_up_out[...] = dot(chosen, up_out[...]).astype(BF)
    o_down_in[...] = dot_back(chosen, down_in[...]).astype(BF)
    o_down_out[...] = dot(chosen, down_out[...]).astype(BF)
    stored = order[...]
    relative = stored
    for d in range(count):
        start = owner_of(me[0], d, count) * own
        relative = jnp.where((stored >= start) & (stored < start + own), stored - start + d * own, relative)
    near = pull_near.shape[1]
    rows = push.shape[0]
    tall = jnp.broadcast_to(relative.astype(F32), (8, rows)).T[:, :1].astype(jnp.int32)
    tall_ref[...] = tall

    def one_hot(i):
        part = rows_at(i, own)
        for ref, start in ((pull_near, 0), (pull_far, near)):
            at = lax.broadcasted_iota(jnp.int32, (own, ref.shape[1]), 1) + start
            ref[part, :] = jnp.where(at == tall_ref[part, :], 1.0, 0.0).astype(BF)
        at = lax.broadcasted_iota(jnp.int32, (own, rows), 0) + i * own
        push[part, :] = jnp.where(at == relative, 1.0, 0.0).astype(BF)

    repeat(rows // own, one_hot)
    seq_at = lax.broadcasted_iota(jnp.int32, mask.shape, 0) // seq_len
    lane_at = lax.broadcasted_iota(jnp.int32, mask.shape, 1) // RANK
    mask[...] = dot(push[...], jnp.where(seq_at == lane_at, 1.0, 0.0).astype(BF))


def qkv_body(ids, last, mask, gain, shift, weight, bias, low_in, low_out, pull, *refs):
    count = len(ids)
    blocks = refs[:count]
    rest = refs[count:]
    earlier = None
    if last:
        earlier, rest = rest[0], rest[1:]
    normed_ref, low_ref, moved_ref, joined, tokens, keep = rest
    rows = blocks[0].shape[0]
    width = weight.shape[2]
    for i in range(count):
        tokens[pl.ds(i * rows, rows), :] = blocks[i][...]
        keep[pl.ds(i * rows, rows), :] = mask[pl.ds(ids[i] * rows, rows), :]

    def project(i):
        part = rows_at(i, rows)
        unit, _ = norm_parts(tokens[part, :].astype(F32))
        normed = (unit * gain[...] + shift[...]).astype(BF)
        normed_ref[part, :] = normed
        low = (dot_back(normed, low_in[...]) * keep[part, :]).astype(BF)
        low_ref[part, :] = low
        for k in range(3):
            value = dot(normed, weight[k]) + dot(low, low_out[k])
            if k != 1:
                value = value + bias[k // 2 : k // 2 + 1, :]
            joined[part, k * width : (k + 1) * width] = value.astype(BF)

    repeat(count, project)
    total = moved_ref.shape[0]
    step = min(256, total)

    def move(i):
        part = rows_at(i, step)
        moved = dot(pull[part, :], joined[...])
        if last:
            moved = moved + earlier[part, :]
            moved_ref[part, :width] = (moved[:, :width] * (1.0 / math.sqrt(HD))).astype(BF)
            moved_ref[part, width:] = moved[:, width:].astype(BF)
        else:
            moved_ref[part, :] = moved

    repeat(total // step, move)


def head_lanes(values, head):
    lane = lax.broadcasted_iota(jnp.int32, values.shape, 1)
    return jnp.where((lane // HD) == head, values, jnp.zeros_like(values))


def attend_body(seq_len, pair, limit, seq, push, out, kept, turned):
    rows = seq.shape[0]
    width = seq.shape[1] // 3
    step = min(256, seq_len)

    def one(s):
        base = s * seq_len
        all_rows = rows_at(s, seq_len)
        keys = seq[all_rows, pl.ds(width + pair * PAIR, PAIR)]
        values = seq[all_rows, pl.ds(2 * width + pair * PAIR, PAIR)]
        values_t = values.astype(F32).T.astype(BF)
        for q in range(seq_len // step):
            span = pl.ds(pl.multiple_of(base + q * step, step), step)
            queries = seq[span, pl.ds(pair * PAIR, PAIR)]
            seen = (q + 1) * step
            allowed = lax.broadcasted_iota(jnp.int32, (seen, step), 0) < limit[:, span]
            for h in range(2):
                scores = dot_back(keys[:seen], head_lanes(queries, h))
                scores = jnp.where(allowed, scores, NEGATIVE)
                weights = jnp.exp(scores - jnp.max(scores, 0, keepdims=True))
                total = jnp.sum(weights, 0, keepdims=True)
                probs = (weights * (1.0 / total)).astype(BF)
                kept[s, h, :seen, q * step : (q + 1) * step] = probs
                turned[pl.ds(h * HD, HD), span] = dot(values_t[h * HD : (h + 1) * HD, :seen], probs).astype(BF)

    repeat(rows // seq_len, one)
    out[...] = dot_back(push[...], turned[...]).astype(BF)


def join_body(count, dp_at, low_near, low_far, push, weight, *refs):
    proj = refs[:2]
    parts = refs[2 : 2 + 2 * (count - 2)]
    w_all, in_all, w_cat, low_t = refs[2 + 2 * (count - 2) :]
    width = in_all.shape[1] // count
    half = width // 2
    fold = in_all.shape[0] // count
    near = low_near.shape[0]
    for d in range(count):
        if d < 2:
            source, at = proj[d], width
            w_all[pl.ds(d * width, width), :] = source[pl.ds(0, width), :]
        else:
            source, at = parts[2 * (d - 2)], half
            start = pl.multiple_of(dp_at[0] % 2 * half, half)
            w_all[pl.ds(d * width + start, half), :] = source[pl.ds(0, half), :]
            start = pl.multiple_of((dp_at[0] + 1) % 2 * half, half)
            w_all[pl.ds(d * width + start, half), :] = parts[2 * (d - 2) + 1][...]
        for j in range(count):
            part = source[pl.ds(at, fold), j * width : (j + 1) * width]
            in_all[pl.ds(j * fold, fold), d * width : (d + 1) * width] = part
    for k in range(3):
        w_cat[:, k * width : (k + 1) * width] = weight[k]
    rows = push.shape[0]
    low_t[...] = (
        dot_over(low_near[...], push[pl.ds(0, near), :]) + dot_over(low_far[...], push[pl.ds(near, rows - near), :])
    ).astype(BF)


def place_of(block, sender, chips):
    return ((block // 2 - sender // 2) % chips) * 2 + ((block % 2) ^ (sender % 2))


def block_body(
    ids, count, pairs, chunk, mask, w_all, in_all, proj_out, proj_bias, gain, shift, up_in, up_w, up_b, up_out,
    down_w, down_in, down_out, *refs
):
    size = len(ids)
    tokens = refs[:size]
    grads = refs[size : 2 * size]
    attended = refs[2 * size : 2 * size + count * pairs]
    rest = refs[2 * size + count * pairs :]
    outs = rest[: len(rest) - 7]
    heads, grad_all, token_all, keep_all, acc, low_acc, down_acc = rest[len(rest) - 7 :]
    part_ref, normed_ref, low_ref, low_part, grad_down_low, act_ref, gup_ref, down_low = outs[:8]
    block = tokens[0].shape[0]
    width = in_all.shape[1] // count
    for i in range(size):
        part = pl.ds(i * block, block)
        for d in range(count):
            spot = place_of(ids[i], d, count // 2) * block
            for p in range(pairs):
                at = d * width + p * PAIR
                heads[part, at : at + PAIR] = attended[d * pairs + p][pl.ds(spot, block), :]
        keep_all[part, :] = mask[pl.ds(ids[i] * block, block), :]
        grad_all[part, :] = grads[i][...]
        token_all[part, :] = tokens[i][...]

    def one(i):
        part = rows_at(i, block)
        keep = keep_all[part, :]
        grad = grad_all[part, :]
        grad_low = (dot_back(grad, down_out[...]) * keep).astype(BF)
        grad_down_low[part, :] = grad_low
        rows = heads[part, :]
        low = (dot_back(rows, in_all[...]) * keep).astype(BF)
        mid = dot(rows, w_all[...]) + dot(low, proj_out[...]) + proj_bias[...] + token_all[part, :].astype(F32)
        unit, _ = norm_parts(mid)
        normed = (unit * gain[...] + shift[...]).astype(BF)
        normed_ref[part, :] = normed
        low2 = (dot_back(normed, up_in[...]) * keep).astype(BF)
        low_ref[part, :] = low2
        if len(outs) > 8:
            outs[8][part, :] = low
            outs[9][part, :] = mid
        acc[...] = jnp.zeros_like(acc)
        low_acc[...] = jnp.zeros_like(low_acc)
        down_acc[...] = jnp.zeros_like(down_acc)

        def one_chunk(j):
            cut = rows_at(j, chunk)
            upper = dot(normed, up_w[:, cut]) + dot(low2, up_out[:, cut]) + up_b[:, cut]
            grad_act = dot_back(grad, down_w[cut, :]) + dot(grad_low, down_in[:, cut])
            square = upper * upper
            curve = jnp.tanh(GELU_A * upper * (1.0 + GELU_B * square))
            half = 0.5 * (1.0 + curve)
            active = (upper * half).astype(BF)
            act_ref[part, cut] = active
            slope = half + 0.5 * upper * (1.0 - curve * curve) * (GELU_A * (1.0 + 3.0 * GELU_B * square))
            grad_upper = (grad_act * slope).astype(BF)
            gup_ref[part, cut] = grad_upper
            acc[...] += dot_back(grad_upper, up_w[:, cut])
            low_acc[...] += dot_back(grad_upper, up_out[:, cut])
            down_acc[...] += dot_back(active, down_in[:, cut])

        repeat(up_w.shape[1] // chunk, one_chunk)
        low = (low_acc[...] * keep).astype(BF)
        low_part[part, :] = low
        down_low[part, :] = (down_acc[...] * keep).astype(BF)
        part_ref[part, :] = (acc[...] + dot(low, up_in[...])).astype(BF)

    repeat(size, one)


def down_body(groups, block, down_w, down_out, *refs):
    for g in range(groups):
        act, low, out = refs[g], refs[groups + g], refs[2 * groups + g]

        def one(i, act=act, low=low, out=out):
            part = rows_at(i, block)
            out[part, :] = (dot(act[part, :], down_w[...]) + dot(low[part, :], down_out[...])).astype(BF)

        repeat(act.shape[0] // block, one)


def hidden_grads_body(groups, sizes, pick, *refs):
    low2 = refs[:groups]
    gup = refs[groups : 2 * groups]
    gdl = refs[2 * groups : 3 * groups]
    act = refs[3 * groups : 4 * groups]
    part = refs[4 * groups : 5 * groups]
    normed = refs[5 * groups : 6 * groups]
    down = refs[6 * groups : 7 * groups]
    rest = refs[7 * groups :]
    total = sum(sizes)
    grads = rest[:total]
    pack, up_in, down_out = rest[total:]
    hid = gup[0].shape[1]
    block = grads[0].shape[0]
    add = lambda left, right: sum([dot_over(a[...], b[...]) for a, b in zip(left[1:], right[1:])], dot_over(left[0][...], right[0][...]))
    pack[:, :hid] = add(low2, gup).astype(BF)
    pack[:, hid : 2 * hid] = add(gdl, act).astype(BF)
    pack[:, 2 * hid :] = pick[...]
    up_in[...] = add(part, normed)
    at = 0
    out = None
    for g in range(groups):
        for i in range(sizes[g]):
            term = dot_over(down[g][pl.ds(i * block, block), :], grads[at][...])
            out = term if out is None else out + term
            at += 1
    down_out[...] = out


def add_body(left, right, out):
    out[...] = (left[...].astype(F32) + right[...].astype(F32)).astype(BF)


def mid_back_body(count, mask, cotangent, mid, gain, proj_out, w_all, in_all, *refs):
    pieces = refs[: count[0]]
    grad_mid, grad_attn, grad_low = refs[count[0] : count[0] + 3]
    outs = refs[count[0] + 3 :]
    width = outs[0].shape[1]
    half = cotangent.shape[0] // 2

    def one(i):
        part = rows_at(i, half)
        upstream = pieces[0][part, :].astype(F32)
        for piece in pieces[1:]:
            upstream = upstream + piece[part, :].astype(F32)
        unit, inv = norm_parts(mid[part, :])
        total = cotangent[part, :] + norm_back(unit, inv, upstream * gain[...])
        grad_mid[part, :] = total
        attn = total.astype(BF)
        grad_attn[part, :] = attn
        low = (dot_back(attn, proj_out[...]) * mask[part, :]).astype(BF)
        grad_low[part, :] = low
        value = (dot_back(attn, w_all[...]) + dot(low, in_all[...])).astype(BF)
        for d in range(count[1]):
            outs[d][part, :] = value[:, d * width : (d + 1) * width]

    repeat(2, one)


def message_body(count, pairs, me, up_in, down_out, proj_low, grad_attn, grad_low, *refs):
    attended = refs[: count * pairs]
    outs = refs[count * pairs : count * pairs + count]
    proj_out = refs[count * pairs + count]
    rank = up_in.shape[0]
    block = grad_low.shape[0]
    width = outs[0].shape[1]
    proj_out[...] = dot_over(proj_low[pl.ds(0, grad_low.shape[0]), :], grad_attn[...])
    for d in range(count):
        spot = place_of(0, d, count // 2) * block
        lanes = pl.ds(pl.multiple_of(owner_of(me[0], d, count) * width, width), width)
        outs[d][pl.ds(0, rank), :] = up_in[:, lanes].astype(BF)
        outs[d][pl.ds(rank, rank), :] = down_out[:, lanes].astype(BF)
        outs[d][pl.ds(2 * rank, rank), :] = proj_out[:, lanes].astype(BF)
        for p in range(pairs):
            outs[d][pl.ds(3 * rank, rank), p * PAIR : (p + 1) * PAIR] = dot_over(
                grad_low[...], attended[d * pairs + p][pl.ds(spot, block), :]
            ).astype(BF)


def pack_body(count, plain, pick, *refs):
    fixed = refs[:plain]
    messages = refs[plain : plain + count]
    out = refs[plain + count]
    rank = pick.shape[0]
    at = 0
    for ref in fixed:
        out[:, at : at + ref.shape[1]] = ref[...]
        at += ref.shape[1]
    width = messages[0].shape[1]
    for k in range(messages[0].shape[0] // rank):
        total = messages[0][pl.ds(k * rank, rank), :].astype(F32)
        for d in range(1, count):
            total = total + messages[d][pl.ds(k * rank, rank), :].astype(F32)
        out[:, at : at + width] = total.astype(BF)
        at += width
    out[:, at : at + pick.shape[1]] = pick[...]


def attend_back_body(pair, pairs, count, seq_len, *refs):
    first, last = pair == 0, pair == pairs - 1
    at = 0

    def take(number):
        nonlocal at
        at += number
        return refs[at - number : at]

    if last:
        (me,) = take(1)
    seq, kept = take(2)
    if first:
        pull_near, pull_far = take(2)
        grads = take(count)
    else:
        (grad_seq,) = take(1)
    if last:
        push, low_t, n1_near, n1_far, low_out = take(5)
        earlier = take(3 * (pairs - 1))
    grad_q, grad_k, grad_v = take(3)
    if last:
        part_t, qkv_out = take(2)
        messages = take(count)
    if first:
        grad_seq, grad_all = take(2)
    if last:
        part_seq, total_in = take(2)
    rows = seq.shape[0]
    width = seq.shape[1] // 3
    step = min(256, seq_len)
    scale = 1.0 / math.sqrt(HD)
    if first:
        block = grads[0].shape[0]
        near = pull_near.shape[1]
        for i in range(count):
            grad_all[pl.ds(i * block, block), :] = grads[i][...]
        grad_seq[...] = (
            dot(pull_near[...], grad_all[pl.ds(0, near), :])
            + dot(pull_far[...], grad_all[pl.ds(near, rows - near), :])
        ).astype(BF)
    if last:
        for p in range(pairs - 1):
            span = slice(p * PAIR, (p + 1) * PAIR)
            grad_q[span, :] = earlier[3 * p][...]
            grad_k[:, span] = earlier[3 * p + 1][...]
            grad_v[:, span] = earlier[3 * p + 2][...]
    base_row = pair * PAIR if last else 0

    def one_sequence(s):
        base = s * seq_len
        all_rows = rows_at(s, seq_len)
        lanes = pl.ds(pair * PAIR, PAIR)
        keys = seq[all_rows, pl.ds(width + pair * PAIR, PAIR)]
        values = seq[all_rows, pl.ds(2 * width + pair * PAIR, PAIR)]
        keys_t = keys.astype(F32).T.astype(BF)
        steps = seq_len // step
        sums_k = [None] * steps
        sums_v = [None] * steps
        for q in range(steps):
            span = pl.ds(pl.multiple_of(base + q * step, step), step)
            queries = seq[span, lanes]
            grad = grad_seq[span, lanes]
            seen = (q + 1) * step
            for h in range(2):
                own_q = head_lanes(queries, h)
                own_g = head_lanes(grad, h)
                probs = kept[s, h, :seen, q * step : (q + 1) * step]
                wide_probs = probs.astype(F32)
                mixed = wide_probs * dot_back(values[:seen], own_g)
                centre = jnp.sum(mixed, 0, keepdims=True)
                raw = (mixed - wide_probs * centre).astype(BF)
                grad_q[pl.ds(base_row + h * HD, HD), span] = (
                    dot(keys_t[h * HD : (h + 1) * HD, :seen], raw) * scale
                ).astype(BF)
                to_k = dot(raw, own_q)
                to_v = dot(probs, own_g)
                for b in range(q + 1):
                    cut = slice(b * step, (b + 1) * step)
                    sums_k[b] = to_k[cut] if sums_k[b] is None else sums_k[b] + to_k[cut]
                    sums_v[b] = to_v[cut] if sums_v[b] is None else sums_v[b] + to_v[cut]
        for b in range(steps):
            span = pl.ds(pl.multiple_of(base + b * step, step), step)
            grad_k[span, pl.ds(base_row, PAIR)] = sums_k[b].astype(BF)
            grad_v[span, pl.ds(base_row, PAIR)] = sums_v[b].astype(BF)

    repeat(rows // seq_len, one_sequence)
    if not last:
        return
    near = n1_near.shape[0]
    part = dot(low_out[0], grad_q[...]) + dot_back(low_out[1], grad_k[...]) + dot_back(low_out[2], grad_v[...])
    lane_at = lax.broadcasted_iota(jnp.int32, part.shape, 1) // seq_len
    rank_at = lax.broadcasted_iota(jnp.int32, part.shape, 0) // RANK
    part_seq[...] = jnp.where(lane_at == rank_at, part, 0.0).astype(BF)
    part_t[...] = dot_back(part_seq[...], push[...]).astype(BF)
    total_in[...] = dot(part_t[:, :near], n1_near[...]) + dot(part_t[:, near:], n1_far[...])
    qkv_out[:, :width] = dot_back(low_t[...], grad_q[...]).astype(BF)
    qkv_out[:, width : 2 * width] = dot(low_t[...], grad_k[...]).astype(BF)
    qkv_out[:, 2 * width :] = dot(low_t[...], grad_v[...]).astype(BF)
    for d in range(count):
        lanes = pl.ds(pl.multiple_of(owner_of(me[0], d, count) * width, width), width)
        messages[d][...] = total_in[:, lanes].astype(BF)


def qkv_back_body(ids, push, w_cat, low_in, grad_q, grad_k, grad_v, part_t, out, joined):
    block = out.shape[0] // len(ids)
    width = grad_k.shape[1]

    def one(i, at):
        rows = rows_at(i, block)
        place = push[rows_at(at, block), :]
        joined[:, :width] = dot_back(place, grad_q[...]).astype(BF)
        joined[:, width : 2 * width] = dot(place, grad_k[...]).astype(BF)
        joined[:, 2 * width :] = dot(place, grad_v[...]).astype(BF)
        low = dot_over(part_t[:, rows_at(at, block)], low_in[...])
        out[rows, :] = (dot_back(joined[...], w_cat[...]) + low).astype(BF)

    if ids == tuple(range(len(ids))):
        repeat(len(ids), lambda i: one(i, i))
    else:
        for i, at in enumerate(ids):
            one(i, at)


def add_pieces(total, pieces, i, half):
    part = rows_at(i, half)
    total = total + pieces[0][part, :].astype(F32) + pieces[1][part, :].astype(F32)
    halves = pieces[2:]
    number = len(halves) // 2
    for k in range(number):
        total = total + halves[i * number + k][...].astype(F32)
    return total


def input_back_body(tokens, grad_mid, gain, *refs):
    out, upstream = refs[-2:]
    half = tokens.shape[0] // 2
    for i in range(2):
        upstream[pl.ds(i * half, half), :] = add_pieces(0.0, refs[:-2], i, half)

    def one(i):
        part = rows_at(i, half)
        unit, inv = norm_parts(tokens[part, :].astype(F32))
        out[part, :] = grad_mid[part, :] + norm_back(unit, inv, upstream[part, :] * gain[...])

    repeat(2, one)


def result_body(mid, bias, *refs):
    out = refs[-1]
    half = out.shape[0] // 2
    for i in range(2):
        part = pl.ds(i * half, half)
        out[part, :] = add_pieces(mid[part, :] + bias[...], refs[:-1], i, half)


def spread_hidden_body(hid, found, up_out, down_in):
    pick = found[:, 2 * hid :]
    up_out[...] = dot_over(pick, found[:, :hid])
    down_in[...] = dot_over(found[:, hid : 2 * hid], pick)


def spread_wide_body(width, found, proj_in, wide):
    pick = found[:, 4 * width :]
    for k in range(3):
        wide[pl.ds(k * 128, 128), :] = dot_over(pick, found[:, k * width : (k + 1) * width]).astype(BF)
    proj_in[...] = dot_over(found[:, 3 * width : 4 * width], pick)


def spread_late_body(width, found, qkv_out, wide):
    pick = found[:, 4 * width :]
    for k in range(3):
        qkv_out[k] = dot_over(pick, found[:, k * width : (k + 1) * width])
    wide[...] = dot_over(pick, found[:, 3 * width : 4 * width]).astype(BF)


def place_wide_body(count, me, *refs):
    messages = refs[:count]
    up_in, down_out, proj_out = refs[count:]
    width = messages[0].shape[1]
    for d in range(count):
        span = pl.ds(pl.multiple_of(owner_of(me[0], d, count) * width, width), width)
        up_in[span, :] = messages[d][pl.ds(0, 128), :].astype(F32).T
        down_out[:, span] = messages[d][pl.ds(128, 128), :].astype(F32)
        proj_out[:, span] = messages[d][pl.ds(256, 128), :].astype(F32)


def place_late_body(count, me, *refs):
    messages = refs[:count]
    qkv_in = refs[count]
    width = messages[0].shape[1]
    for d in range(count):
        qkv_in[pl.ds(pl.multiple_of(owner_of(me[0], d, count) * width, width), width), :] = messages[d][...].astype(F32).T


def tie(value, *others):
    return lax.optimization_barrier((value, *others))[0]


def body(
    tensor_size,
    dp_size,
    tokens,
    cotangent,
    lengths,
    order,
    adapter_ids,
    norm1_gain,
    norm1_shift,
    qkv_weight,
    qv_bias,
    proj_weight,
    proj_bias,
    norm2_gain,
    norm2_shift,
    up_weight,
    up_bias,
    down_weight,
    down_bias,
    adapt_qkv_in,
    adapt_qkv_out,
    adapt_proj_in,
    adapt_proj_out,
    adapt_up_in,
    adapt_up_out,
    adapt_down_in,
    adapt_down_out,
):
    count = tensor_size
    chips = count // 2
    own, wide = tokens.shape
    width = qkv_weight.shape[2]
    pairs = width // PAIR
    hid = up_weight.shape[1]
    rows = order.shape[1]
    seqs = lengths.shape[1]
    seq_len = rows // seqs
    ranks = seqs * RANK
    near = 2 * own
    far = rows - near
    cols = adapt_qkv_in.shape[1]
    near_ids = (0, 1)
    even_ids = tuple(range(2, count, 2))
    odd_ids = tuple(range(3, count, 2))
    me = lax.axis_index("tensor")

    core_perm = [(t, t ^ 1) for t in range(count)]

    def core_swap(value):
        return lax.ppermute(value, "tensor", core_perm)

    def chip_hop(value, k):
        return lax.ppermute(value, "tensor", [(t, ((t // 2 + k) % chips) * 2 + t % 2) for t in range(count)])

    def hops_of(value):
        return [chip_hop(value, k) for k in range(1, chips)]

    def weave(value, swapped, moved):
        found = [value, swapped]
        for item in moved:
            found += [item, core_swap(item)]
        return found

    def exchange(messages):
        out = [messages[0], core_swap(messages[1])] + [None] * (count - 2)
        for k in range(1, chips):
            flat = [(t, ((t // 2 - k) % chips) * 2 + t % 2) for t in range(count)]
            cross = [(t, ((t // 2 - k) % chips) * 2 + (t % 2 ^ 1)) for t in range(count)]
            out[2 * (chips - k)] = lax.ppermute(messages[2 * k], "tensor", flat)
            out[2 * (chips - k) + 1] = lax.ppermute(messages[2 * k + 1], "tensor", cross)
        return out

    def join(left, right, name):
        return whole_call(add_body, [left, right], [shape(left.shape, BF)], name)[0]

    def send_far(joined):
        return [chip_hop(joined[(k - 1) * own : k * own] if chips > 2 else joined, -k) for k in range(1, chips)]

    def send_half(joined, part):
        half = own // 2
        return [
            chip_hop(joined[(k - 1) * own + part * half : (k - 1) * own + (part + 1) * half], -k)
            for k in range(1, chips)
        ]

    def dp_swap(value, stride):
        return lax.ppermute(value, "dp", [(i, i ^ stride) for i in range(dp_size)])

    def double(value, moved):
        return jnp.concatenate([value, moved], 0)

    def widen(value, stride):
        while stride:
            value = double(value, dp_swap(value, stride))
            stride //= 2
        return value

    place = me.reshape(1)
    dp_at = lax.axis_index("dp").reshape(1)
    weight_three = jnp.transpose(qkv_weight, (1, 0, 2))
    out_three = jnp.transpose(adapt_qkv_out, (1, 0, 2))
    row = lambda v: v.reshape(1, -1)

    top = dp_size // 2
    token_core = core_swap(tokens)
    token_hops = hops_of(tokens)
    grad_own = tie(cotangent, token_core).astype(BF)
    grad_core = core_swap(grad_own)

    prepared = whole_call(
        functools.partial(prep_body, seq_len, own, count),
        [order, proj_weight, adapt_qkv_in, out_three, adapt_proj_in, adapt_proj_out, adapt_up_in, adapt_up_out, adapt_down_in,
         adapt_down_out],
        [shape((ranks, wide), BF), shape((3, ranks, width), BF), shape((width + 16, wide), BF),
         shape((ranks, wide), BF), shape((ranks, wide), BF), shape((ranks, hid), BF),
         shape((ranks, hid), BF), shape((ranks, wide), BF), shape((rows, near), BF), shape((rows, far), BF),
         shape((rows, rows), BF), shape((rows, ranks), F32), shape((ranks, cols), BF), shape((1, rows), jnp.int32),
         shape((width // 2 + 16, wide), BF)],
        "prep",
        smem=[place, dp_at, lengths, adapter_ids],
        loose=tuple(range(10)),
        scratch=[pltpu.VMEM((rows, 1), jnp.int32)],
    )
    c_qkv_in, c_qkv_out, proj_own, c_proj_out, c_up_in, c_up_out, c_down_in, c_down_out = prepared[:8]
    pull_near, pull_far, push, mask, pick, limit, proj_half = prepared[8:]
    proj_core = core_swap(proj_own)
    proj_hops = hops_of(proj_half)

    norm1 = [row(norm1_gain), row(norm1_shift), weight_three, qv_bias, c_qkv_in, c_qkv_out]
    n1_near, low1_near, moved_near = whole_call(
        functools.partial(qkv_body, near_ids, False),
        [mask] + norm1 + [pull_near, tokens, token_core],
        [shape((near, wide), BF), shape((near, ranks), BF), shape((rows, 3 * width), F32)],
        "qkv_near",
        loose=(1, 2, 3, 4, 8, 9),
        long=True,
        scratch=[pltpu.VMEM((near, 3 * width), BF), pltpu.VMEM((near, wide), BF), pltpu.VMEM((near, ranks), F32)],
    )
    token_hops = [tie(item, low1_near) for item in token_hops]
    token_blocks = weave(tokens, token_core, token_hops)
    n1_far, low1_far, qkv_seq = whole_call(
        functools.partial(qkv_body, tuple(range(2, count)), True),
        [mask] + norm1 + [pull_far] + token_blocks[2:] + [moved_near],
        [shape((far, wide), BF), shape((far, ranks), BF), shape((rows, 3 * width), BF)],
        "qkv_far",
        scratch=[pltpu.VMEM((far, 3 * width), BF), pltpu.VMEM((far, wide), BF), pltpu.VMEM((far, ranks), F32)],
    )

    grad_hops = hops_of(tie(grad_own, low1_far))
    sums = []
    attended = []
    seq_in = qkv_seq
    for pair in range(pairs):
        part, kept = whole_call(
            functools.partial(attend_body, seq_len, pair),
            [limit, seq_in, push],
            [shape((rows, PAIR), BF), shape((seqs, 2, seq_len, seq_len), BF)],
            f"attend{pair}",
            scratch=[pltpu.VMEM((PAIR, rows), BF)],
        )
        sums.append(kept)
        attended.append(part)
        if pair == 0:
            seq_in = tie(qkv_seq, part)
    after = attended[-1]
    gathered_heads = []
    for part in attended:
        gathered_heads.append(weave(part, core_swap(part), hops_of(part)))
    heads = [gathered_heads[p][d] for d in range(count) for p in range(pairs)]

    proj_parts = []
    for item in proj_hops:
        item = tie(item, after)
        other = dp_swap(item[: width // 2], 1)
        proj_parts += [item, other, core_swap(item), core_swap(other)]
    grad_blocks = weave(grad_own, grad_core, [tie(item, after) for item in grad_hops])
    w_all, in_all, w_cat, low_t = whole_call(
        functools.partial(join_body, count),
        [low1_near, low1_far, push, weight_three, proj_own, proj_core] + proj_parts,
        [shape((wide, wide), BF), shape((ranks, wide), BF), shape((wide, 3 * width), BF), shape((ranks, rows), BF)],
        "join",
        smem=[dp_at],
    )

    def block_call(ids, gate, name):
        size = len(ids) * own
        extra = [shape((size, ranks), BF), shape((size, wide), F32)] if 0 in ids else []
        keep = mask if gate is None else tie(mask, gate)
        return whole_call(
            functools.partial(block_body, ids, count, pairs, min(512, hid)),
            [keep, w_all, in_all, c_proj_out, row(proj_bias), row(norm2_gain), row(norm2_shift), c_up_in, up_weight,
             row(up_bias), c_up_out, down_weight, c_down_in, c_down_out]
            + [token_blocks[i] for i in ids] + [grad_blocks[i] for i in ids] + heads,
            [shape((size, wide), BF), shape((size, wide), BF), shape((size, ranks), BF), shape((size, ranks), BF),
             shape((size, ranks), BF), shape((size, hid), BF), shape((size, hid), BF), shape((size, ranks), BF)]
            + extra,
            name,
            scratch=[pltpu.VMEM((size, wide), BF)] * 3
            + [pltpu.VMEM((size, ranks), F32), pltpu.VMEM((own, wide), F32)] + [pltpu.VMEM((own, ranks), F32)] * 2,
            long=gate is not None,
        )

    odd = block_call(odd_ids, None, "block_odd")
    odd_moved = core_swap(odd[0])
    even = block_call(even_ids, odd[3], "block_even")
    up_joined = join(even[0], odd_moved, "up_join")
    up_hops = send_far(up_joined)
    mine = block_call(near_ids, up_joined, "block_near")
    up_swap = core_swap(mine[0][own:])
    groups = (mine, even, odd)
    order_ids = (near_ids, even_ids, odd_ids)
    pack_hidden, p_up_in, p_down_out = whole_call(
        functools.partial(hidden_grads_body, 3, tuple(len(i) for i in order_ids)),
        [pick] + [g[k] for k in (2, 6, 4, 5, 3, 1, 7) for g in groups]
        + [grad_blocks[i] for ids in order_ids for i in ids],
        [shape((ranks, 2 * hid + cols), BF), shape((ranks, wide), F32), shape((ranks, wide), F32)],
        "hidden_grads",
    )
    up_hops = [tie(item, p_up_in) for item in up_hops]
    proj_low, mid = mine[8:]
    back = whole_call(
        functools.partial(mid_back_body, (2 + len(up_hops), count)),
        [mask, cotangent, mid, row(norm2_gain), c_proj_out, w_all, in_all, mine[0], up_swap] + up_hops,
        [shape((own, wide), F32), shape((own, wide), BF), shape((own, ranks), BF)]
        + [shape((own, width), BF)] * count,
        "mid_back",
        long=True,
    )
    grad_mid, grad_attn, grad_proj_low = back[:3]
    grad_att = exchange(back[3:])
    hidden_moved = dp_swap(tie(pack_hidden, grad_proj_low), top)

    messages = whole_call(
        functools.partial(message_body, count, pairs),
        [p_up_in, p_down_out, proj_low, grad_attn, grad_proj_low] + heads,
        [shape((4 * ranks, width), BF)] * count,
        "message",
        smem=[place],
        scratch=[pltpu.VMEM((ranks, wide), F32)],
        long=True,
    )
    down_parts = whole_call(
        functools.partial(down_body, 3, own),
        [tie(down_weight, messages[0]), c_down_out] + [g[5] for g in groups] + [g[7] for g in groups],
        [shape(g[0].shape, BF) for g in groups],
        "down",
        long=True,
    )
    down_mine, down_even, down_odd = down_parts
    grad_att = [grad_att[0]] + [tie(item, down_mine) for item in grad_att[1:]]
    wide_messages = exchange([tie(item, *grad_att[1:]) for item in messages])
    down_moved = core_swap(tie(down_odd, *grad_att[1:]))
    down_swap = core_swap(tie(down_mine[own:], *grad_att[1:]))

    back_pieces = []
    grad_seq = None
    for pair in range(pairs):
        last = pair == pairs - 1
        inputs = [qkv_seq, sums[pair]]
        outs = [shape((PAIR, rows), BF), shape((rows, PAIR), BF), shape((rows, PAIR), BF)]
        scratch = []
        if pair == 0:
            inputs += [pull_near, pull_far] + grad_att
        else:
            inputs += [grad_seq]
        if last:
            inputs += [push, low_t, n1_near, n1_far, c_qkv_out] + back_pieces
            outs = [shape((width, rows), BF), shape((rows, width), BF), shape((rows, width), BF),
                    shape((ranks, rows), BF), shape((ranks, 3 * width), BF)] + [shape((ranks, width), BF)] * count
        if pair == 0:
            if last:
                scratch += [pltpu.VMEM((rows, width), BF)]
            else:
                outs += [shape((rows, width), BF)]
            scratch += [pltpu.VMEM((rows, width), BF)]
        if last:
            scratch += [pltpu.VMEM((ranks, rows), BF), pltpu.VMEM((ranks, wide), F32)]
        results = whole_call(
            functools.partial(attend_back_body, pair, pairs, count, seq_len),
            inputs,
            outs,
            f"attend_back{pair}",
            smem=[place] if last else [],
            scratch=scratch,
            long=True,
        )
        if pair == 0:
            passed = results[0]
            wide_messages = [wide_messages[0]] + [tie(item, passed) for item in wide_messages[1:]]
            (pack_wide,) = whole_call(
                functools.partial(pack_body, count, 0),
                [pick] + wide_messages,
                [shape((ranks, 4 * width + cols), BF)],
                "pack_wide",
            )
            hidden_half = double(pack_hidden, tie(hidden_moved, passed, *wide_messages))
            hidden_moved = dp_swap(hidden_half, top // 2)
            hidden_first = dp_swap(hidden_half, top // 4)
            wide_moved = dp_swap(pack_wide, top)
            down_joined = join(down_even, tie(down_moved, passed, *wide_messages), "down_join")
            down_first = send_half(down_joined, 0)
        if not last:
            back_pieces += list(results[:3])
            grad_seq = tie(results[3], pack_wide, hidden_half, down_joined)
    grad_q, grad_k, grad_v, part_t, g_qkv_out = results[:5]
    down_first = [tie(item, part_t) for item in down_first]
    hidden_moved = tie(hidden_moved, part_t)
    hidden_first = tie(hidden_first, part_t)
    late_messages = exchange(results[5:])
    hidden_second = dp_swap(hidden_moved, top // 4)
    wide_moved_first = tie(wide_moved, part_t)
    wide_found = double(pack_wide, wide_moved_first)
    wide_moved = dp_swap(wide_found, top // 2)

    def unproject(ids, gates, name):
        size = len(ids) * own
        return whole_call(
            functools.partial(qkv_back_body, ids),
            [push, w_cat, c_qkv_in, grad_q, grad_k, grad_v, tie(part_t, *gates)],
            [shape((size, wide), BF)],
            name,
            scratch=[pltpu.VMEM((own, 3 * width), BF)],
            long=True,
        )[0]

    odd_part = unproject(odd_ids, [wide_moved_first, hidden_moved, hidden_first, *down_first], "qkv_back_odd")
    odd_moved = core_swap(odd_part)
    even_part = unproject(even_ids, [odd_part], "qkv_back_even")
    qkv_joined = join(even_part, tie(odd_moved, *late_messages[1:], wide_moved), "qkv_join")
    qkv_first = send_half(qkv_joined, 0)
    late_messages = [late_messages[0]] + [tie(item, qkv_joined) for item in late_messages[1:]]
    (pack_late,) = whole_call(
        functools.partial(pack_body, count, 1),
        [pick, g_qkv_out] + late_messages,
        [shape((ranks, 4 * width + cols), BF)],
        "pack_late",
    )
    late_moved = dp_swap(pack_late, top)
    wide_found = double(wide_found, wide_moved)
    wide_moved = dp_swap(wide_found, top // 4)
    near_part = unproject(near_ids, [qkv_joined, pack_late, hidden_second], "qkv_back_near")
    qkv_swap = core_swap(near_part[own:])
    qkv_first = [tie(item, near_part) for item in qkv_first]
    qkv_second = send_half(tie(qkv_joined, *qkv_first), 1)
    late_found = double(pack_late, tie(late_moved, near_part, *qkv_first))
    late_moved = dp_swap(late_found, top // 2)
    late_moved = tie(late_moved, *qkv_second)
    wide_found = widen(double(wide_found, tie(wide_moved, late_moved)), top // 8)
    proj_in_full, wide_part = whole_call(
        functools.partial(spread_wide_body, width),
        [wide_found],
        [shape((width, cols), F32), shape((3 * cols, width), BF)],
        "spread_wide",
        final=(0,),
    )
    wide_blocks = weave(wide_part, core_swap(wide_part), hops_of(wide_part))
    late_found = double(late_found, late_moved)
    late_moved = dp_swap(late_found, top // 4)
    down_second = send_half(tie(down_joined, *qkv_second), 1)
    (grad_input,) = whole_call(
        input_back_body,
        [tokens, grad_mid, row(norm1_gain), near_part, qkv_swap, *qkv_first, *qkv_second],
        [shape((own, wide), F32)],
        "input_back",
        scratch=[pltpu.VMEM((own, wide), F32)],
        final=(0,),
    )
    up_in_full, down_out_full, proj_out_full = whole_call(
        functools.partial(place_wide_body, count),
        [tie(wide_blocks[0], grad_input)] + wide_blocks[1:],
        [shape((wide, cols), F32), shape((cols, wide), F32), shape((cols, wide), F32)],
        "place_wide",
        smem=[place],
        final=(0, 1, 2),
    )
    late_found = widen(double(late_found, tie(late_moved, grad_input)), top // 8)
    qkv_out_full, late_part = whole_call(
        functools.partial(spread_late_body, width),
        [late_found],
        [shape((3, cols, width), F32), shape((cols, width), BF)],
        "spread_late",
        final=(0,),
    )
    late_blocks = weave(late_part, core_swap(late_part), hops_of(late_part))
    (result,) = whole_call(
        result_body,
        [mid, row(down_bias), down_mine, down_swap, *down_first, *[tie(item, late_part) for item in down_second]],
        [shape((own, wide), F32)],
        "result",
        final=(0,),
    )
    hidden_found = jnp.concatenate([hidden_half, hidden_moved, hidden_first, tie(hidden_second, result)], 0)
    up_out_full, down_in_full = whole_call(
        functools.partial(spread_hidden_body, hid),
        [widen(hidden_found, top // 8)],
        [shape((cols, hid), F32), shape((hid, cols), F32)],
        "spread_hidden",
        final=(0, 1),
    )
    (qkv_in_full,) = whole_call(
        functools.partial(place_late_body, count),
        [late_blocks[0]] + [tie(item, up_out_full) for item in late_blocks[1:]],
        [shape((wide, cols), F32)],
        "place_late",
        smem=[place],
        final=(0,),
    )
    return (
        result,
        grad_input,
        qkv_in_full,
        jnp.transpose(qkv_out_full, (1, 0, 2)),
        proj_in_full,
        proj_out_full,
        up_in_full,
        up_out_full,
        down_in_full,
        down_out_full,
    )


def solution(mesh):
    in_specs = (
        P(("dp", "tensor"), None),
        P(("dp", "tensor"), None),
        P("dp", None),
        P("dp", None),
        P("dp", None),
        P(),
        P(),
        P(None, None, "tensor"),
        P(None, "tensor"),
        P("tensor", None),
        P(),
        P(),
        P(),
        P(None, "tensor"),
        P("tensor"),
        P("tensor", None),
        P(),
        P(),
        P(None, None, "tensor"),
        P("tensor", None),
        P(),
        P(),
        P(None, "tensor"),
        P("tensor", None),
        P(),
    )
    out_specs = (
        P(("dp", "tensor"), None),
        P(("dp", "tensor"), None),
        P(),
        P(None, None, "tensor"),
        P("tensor", None),
        P(),
        P(),
        P(None, "tensor"),
        P("tensor", None),
        P(),
    )
    run = functools.partial(body, mesh.shape["tensor"], mesh.shape["dp"])
    return jax.shard_map(run, mesh=mesh, in_specs=in_specs, out_specs=out_specs, check_vma=False)
```

```python
import functools
import math

import jax
import jax.numpy as jnp
from jax import lax
from jax.experimental import pallas as pl
from jax.experimental.pallas import tpu as pltpu
from jax.sharding import PartitionSpec as P

HD = 64
RANK = 16
PAIR = 2 * HD
EPSILON = 1e-05
NEGATIVE = -1000000000.0
BF = jnp.bfloat16
F32 = jnp.float32
LIMIT = 10 * 1024 * 1024
GELU_A = math.sqrt(2.0 / math.pi)
GELU_B = 0.044715


def dot(left, right):
    return jnp.dot(left, right, preferred_element_type=F32)


def dot_back(left, right):
    return lax.dot_general(left, right, (((1,), (1,)), ((), ())), preferred_element_type=F32)


def dot_over(left, right):
    return lax.dot_general(left, right, (((0,), (0,)), ((), ())), preferred_element_type=F32)


def shape(dims, kind):
    return jax.ShapeDtypeStruct(tuple(dims), kind)


def whole_call(body, inputs, outs, name, smem=(), scratch=(), final=(), loose=(), long=False):
    smem_spec = pl.BlockSpec(memory_space=pltpu.SMEM)
    vmem_spec = pl.BlockSpec(memory_space=pltpu.VMEM)
    held = [
        pltpu.with_memory_space_constraint(x, pltpu.HBM if i in loose else pltpu.VMEM) for i, x in enumerate(inputs)
    ]
    kinds = [o if i in final else pltpu.VMEM(o.shape, o.dtype) for i, o in enumerate(outs)]
    return pl.pallas_call(
        body,
        out_shape=kinds,
        in_specs=[smem_spec] * len(smem) + [vmem_spec] * len(inputs),
        out_specs=[vmem_spec] * len(outs),
        scratch_shapes=list(scratch),
        compiler_params=pltpu.CompilerParams(vmem_limit_bytes=LIMIT),
        name=name,
    )(*smem, *held)


def norm_parts(values):
    centre = values - jnp.mean(values, -1, keepdims=True)
    spread = jnp.mean(centre * centre, -1, keepdims=True)
    inv = lax.rsqrt(spread + EPSILON)
    return centre * inv, inv


def norm_back(normed, inv, upstream):
    return inv * (
        upstream
        - jnp.mean(upstream, -1, keepdims=True)
        - normed * jnp.mean(upstream * normed, -1, keepdims=True)
    )


def rows_at(i, size):
    return pl.ds(pl.multiple_of(i * size, size), size)


def repeat(count, step):
    if count == 1:
        step(0)
    else:
        lax.fori_loop(0, count, lambda i, carry: (step(i), carry)[1], 0)


def owner_of(me, d, count):
    return (((me // 2) + count // 2 - d // 2) % (count // 2)) * 2 + ((me % 2 + d % 2) % 2)


def prep_body(
    seq_len, own, count, me, dp_at, lengths, ids, order, proj_w, qkv_in, qkv_out, proj_in, proj_out, up_in, up_out,
    down_in, down_out, *outs
):
    o_qkv_in, o_qkv_out, o_proj, o_proj_out, o_up_in, o_up_out, o_down_in, o_down_out = outs[:8]
    pull_near, pull_far, push, mask, pick, limit, o_half, tall_ref = outs[8:]
    rank_at = lax.broadcasted_iota(jnp.int32, pick.shape, 0)
    col_at = lax.broadcasted_iota(jnp.int32, pick.shape, 1)
    wanted = rank_at + ids[0, 0] * RANK
    slot = lax.broadcasted_iota(jnp.int32, limit.shape, 1)
    bound = jnp.minimum(slot + 1, lengths[0, 0])
    for s in range(1, lengths.shape[1]):
        wanted = jnp.where(rank_at >= s * RANK, rank_at - s * RANK + ids[0, s] * RANK, wanted)
        bound = jnp.where(slot >= s * seq_len, jnp.minimum(slot - s * seq_len + 1, lengths[0, s]), bound)
    limit[...] = bound
    chosen = jnp.where(col_at == wanted, 1.0, 0.0).astype(BF)
    pick[...] = chosen
    width = proj_w.shape[0]
    fold = pick.shape[0] // count
    o_proj[pl.ds(0, width), :] = proj_w[...]
    o_proj[pl.ds(width, 16), :] = jnp.zeros((16, o_proj.shape[1]), BF)
    chosen_in = dot_back(chosen, proj_in[...])
    for j in range(count):
        o_proj[pl.ds(width, fold), j * width : (j + 1) * width] = chosen_in[j * fold : (j + 1) * fold].astype(BF)
    half = width // 2
    o_half[pl.ds(0, half), :] = proj_w[pl.ds(pl.multiple_of(dp_at[0] % 2 * half, half), half), :]
    o_half[pl.ds(half, 16), :] = o_proj[pl.ds(width, 16), :]
    o_qkv_in[...] = dot_back(chosen, qkv_in[...]).astype(BF)
    for k in range(3):
        o_qkv_out[k] = dot(chosen, qkv_out[k]).astype(BF)
    o_proj_out[...] = dot(chosen, proj_out[...]).astype(BF)
    o_up_in[...] = dot_back(chosen, up_in[...]).astype(BF)
    o_up_out[...] = dot(chosen, up_out[...]).astype(BF)
    o_down_in[...] = dot_back(chosen, down_in[...]).astype(BF)
    o_down_out[...] = dot(chosen, down_out[...]).astype(BF)
    stored = order[...]
    relative = stored
    for d in range(count):
        start = owner_of(me[0], d, count) * own
        relative = jnp.where((stored >= start) & (stored < start + own), stored - start + d * own, relative)
    near = pull_near.shape[1]
    rows = push.shape[0]
    tall = jnp.broadcast_to(relative.astype(F32), (8, rows)).T[:, :1].astype(jnp.int32)
    tall_ref[...] = tall

    def one_hot(i):
        part = rows_at(i, own)
        for ref, start in ((pull_near, 0), (pull_far, near)):
            at = lax.broadcasted_iota(jnp.int32, (own, ref.shape[1]), 1) + start
            ref[part, :] = jnp.where(at == tall_ref[part, :], 1.0, 0.0).astype(BF)
        at = lax.broadcasted_iota(jnp.int32, (own, rows), 0) + i * own
        push[part, :] = jnp.where(at == relative, 1.0, 0.0).astype(BF)

    repeat(rows // own, one_hot)
    seq_at = lax.broadcasted_iota(jnp.int32, mask.shape, 0) // seq_len
    lane_at = lax.broadcasted_iota(jnp.int32, mask.shape, 1) // RANK
    mask[...] = dot(push[...], jnp.where(seq_at == lane_at, 1.0, 0.0).astype(BF))


def qkv_body(ids, last, mask, gain, shift, weight, bias, low_in, low_out, pull, *refs):
    count = len(ids)
    blocks = refs[:count]
    rest = refs[count:]
    earlier = None
    if last:
        earlier, rest = rest[0], rest[1:]
    normed_ref, low_ref, moved_ref, joined, tokens, keep = rest
    rows = blocks[0].shape[0]
    width = weight.shape[2]
    for i in range(count):
        tokens[pl.ds(i * rows, rows), :] = blocks[i][...]
        keep[pl.ds(i * rows, rows), :] = mask[pl.ds(ids[i] * rows, rows), :]

    def project(i):
        part = rows_at(i, rows)
        unit, _ = norm_parts(tokens[part, :].astype(F32))
        normed = (unit * gain[...] + shift[...]).astype(BF)
        normed_ref[part, :] = normed
        low = (dot_back(normed, low_in[...]) * keep[part, :]).astype(BF)
        low_ref[part, :] = low
        for k in range(3):
            value = dot(normed, weight[k]) + dot(low, low_out[k])
            if k != 1:
                value = value + bias[k // 2 : k // 2 + 1, :]
            joined[part, k * width : (k + 1) * width] = value.astype(BF)

    repeat(count, project)
    total = moved_ref.shape[0]
    step = min(256, total)

    def move(i):
        part = rows_at(i, step)
        moved = dot(pull[part, :], joined[...])
        if last:
            moved = moved + earlier[part, :]
            moved_ref[part, :width] = (moved[:, :width] * (1.0 / math.sqrt(HD))).astype(BF)
            moved_ref[part, width:] = moved[:, width:].astype(BF)
        else:
            moved_ref[part, :] = moved

    repeat(total // step, move)


def head_lanes(values, head):
    lane = lax.broadcasted_iota(jnp.int32, values.shape, 1)
    return jnp.where((lane // HD) == head, values, jnp.zeros_like(values))


def attend_body(seq_len, pair, limit, seq, push, out, kept, turned):
    rows = seq.shape[0]
    width = seq.shape[1] // 3
    step = min(256, seq_len)

    def one(s):
        base = s * seq_len
        all_rows = rows_at(s, seq_len)
        keys = seq[all_rows, pl.ds(width + pair * PAIR, PAIR)]
        values = seq[all_rows, pl.ds(2 * width + pair * PAIR, PAIR)]
        values_t = values.astype(F32).T.astype(BF)
        for q in range(seq_len // step):
            span = pl.ds(pl.multiple_of(base + q * step, step), step)
            queries = seq[span, pl.ds(pair * PAIR, PAIR)]
            seen = (q + 1) * step
            allowed = lax.broadcasted_iota(jnp.int32, (seen, step), 0) < limit[:, span]
            for h in range(2):
                scores = dot_back(keys[:seen], head_lanes(queries, h))
                scores = jnp.where(allowed, scores, NEGATIVE)
                weights = jnp.exp(scores - jnp.max(scores, 0, keepdims=True))
                total = jnp.sum(weights, 0, keepdims=True)
                probs = (weights * (1.0 / total)).astype(BF)
                kept[s, h, :seen, q * step : (q + 1) * step] = probs
                turned[pl.ds(h * HD, HD), span] = dot(values_t[h * HD : (h + 1) * HD, :seen], probs).astype(BF)

    repeat(rows // seq_len, one)
    out[...] = dot_back(push[...], turned[...]).astype(BF)


def join_body(count, dp_at, low_near, low_far, push, weight, *refs):
    proj = refs[:2]
    parts = refs[2 : 2 + 2 * (count - 2)]
    w_all, in_all, w_cat, low_t = refs[2 + 2 * (count - 2) :]
    width = in_all.shape[1] // count
    half = width // 2
    fold = in_all.shape[0] // count
    near = low_near.shape[0]
    for d in range(count):
        if d < 2:
            source, at = proj[d], width
            w_all[pl.ds(d * width, width), :] = source[pl.ds(0, width), :]
        else:
            source, at = parts[2 * (d - 2)], half
            start = pl.multiple_of(dp_at[0] % 2 * half, half)
            w_all[pl.ds(d * width + start, half), :] = source[pl.ds(0, half), :]
            start = pl.multiple_of((dp_at[0] + 1) % 2 * half, half)
            w_all[pl.ds(d * width + start, half), :] = parts[2 * (d - 2) + 1][...]
        for j in range(count):
            part = source[pl.ds(at, fold), j * width : (j + 1) * width]
            in_all[pl.ds(j * fold, fold), d * width : (d + 1) * width] = part
    for k in range(3):
        w_cat[:, k * width : (k + 1) * width] = weight[k]
    rows = push.shape[0]
    low_t[...] = (
        dot_over(low_near[...], push[pl.ds(0, near), :]) + dot_over(low_far[...], push[pl.ds(near, rows - near), :])
    ).astype(BF)


def place_of(block, sender, chips):
    return ((block // 2 - sender // 2) % chips) * 2 + ((block % 2) ^ (sender % 2))


def block_body(
    ids, count, pairs, chunk, mask, w_all, in_all, proj_out, proj_bias, gain, shift, up_in, up_w, up_b, up_out,
    down_w, down_in, down_out, *refs
):
    size = len(ids)
    tokens = refs[:size]
    grads = refs[size : 2 * size]
    attended = refs[2 * size : 2 * size + count * pairs]
    rest = refs[2 * size + count * pairs :]
    outs = rest[: len(rest) - 7]
    heads, grad_all, token_all, keep_all, acc, low_acc, down_acc = rest[len(rest) - 7 :]
    part_ref, normed_ref, low_ref, low_part, grad_down_low, act_ref, gup_ref, down_low = outs[:8]
    block = tokens[0].shape[0]
    width = in_all.shape[1] // count
    for i in range(size):
        part = pl.ds(i * block, block)
        for d in range(count):
            spot = place_of(ids[i], d, count // 2) * block
            for p in range(pairs):
                at = d * width + p * PAIR
                heads[part, at : at + PAIR] = attended[d * pairs + p][pl.ds(spot, block), :]
        keep_all[part, :] = mask[pl.ds(ids[i] * block, block), :]
        grad_all[part, :] = grads[i][...]
        token_all[part, :] = tokens[i][...]

    def one(i):
        part = rows_at(i, block)
        keep = keep_all[part, :]
        grad = grad_all[part, :]
        grad_low = (dot_back(grad, down_out[...]) * keep).astype(BF)
        grad_down_low[part, :] = grad_low
        rows = heads[part, :]
        low = (dot_back(rows, in_all[...]) * keep).astype(BF)
        mid = dot(rows, w_all[...]) + dot(low, proj_out[...]) + proj_bias[...] + token_all[part, :].astype(F32)
        unit, _ = norm_parts(mid)
        normed = (unit * gain[...] + shift[...]).astype(BF)
        normed_ref[part, :] = normed
        low2 = (dot_back(normed, up_in[...]) * keep).astype(BF)
        low_ref[part, :] = low2
        if len(outs) > 8:
            outs[8][part, :] = low
            outs[9][part, :] = mid
        acc[...] = jnp.zeros_like(acc)
        low_acc[...] = jnp.zeros_like(low_acc)
        down_acc[...] = jnp.zeros_like(down_acc)

        def one_chunk(j):
            cut = rows_at(j, chunk)
            upper = dot(normed, up_w[:, cut]) + dot(low2, up_out[:, cut]) + up_b[:, cut]
            grad_act = dot_back(grad, down_w[cut, :]) + dot(grad_low, down_in[:, cut])
            square = upper * upper
            curve = jnp.tanh(GELU_A * upper * (1.0 + GELU_B * square))
            half = 0.5 * (1.0 + curve)
            active = (upper * half).astype(BF)
            act_ref[part, cut] = active
            slope = half + 0.5 * upper * (1.0 - curve * curve) * (GELU_A * (1.0 + 3.0 * GELU_B * square))
            grad_upper = (grad_act * slope).astype(BF)
            gup_ref[part, cut] = grad_upper
            acc[...] += dot_back(grad_upper, up_w[:, cut])
            low_acc[...] += dot_back(grad_upper, up_out[:, cut])
            down_acc[...] += dot_back(active, down_in[:, cut])

        repeat(up_w.shape[1] // chunk, one_chunk)
        low = (low_acc[...] * keep).astype(BF)
        low_part[part, :] = low
        down_low[part, :] = (down_acc[...] * keep).astype(BF)
        part_ref[part, :] = (acc[...] + dot(low, up_in[...])).astype(BF)

    repeat(size, one)


def down_body(groups, block, down_w, down_out, *refs):
    for g in range(groups):
        act, low, out = refs[g], refs[groups + g], refs[2 * groups + g]

        def one(i, act=act, low=low, out=out):
            part = rows_at(i, block)
            out[part, :] = (dot(act[part, :], down_w[...]) + dot(low[part, :], down_out[...])).astype(BF)

        repeat(act.shape[0] // block, one)


def hidden_grads_body(groups, sizes, pick, *refs):
    low2 = refs[:groups]
    gup = refs[groups : 2 * groups]
    gdl = refs[2 * groups : 3 * groups]
    act = refs[3 * groups : 4 * groups]
    part = refs[4 * groups : 5 * groups]
    normed = refs[5 * groups : 6 * groups]
    down = refs[6 * groups : 7 * groups]
    rest = refs[7 * groups :]
    total = sum(sizes)
    grads = rest[:total]
    pack, up_in, down_out = rest[total:]
    hid = gup[0].shape[1]
    block = grads[0].shape[0]
    add = lambda left, right: sum([dot_over(a[...], b[...]) for a, b in zip(left[1:], right[1:])], dot_over(left[0][...], right[0][...]))
    pack[:, :hid] = add(low2, gup).astype(BF)
    pack[:, hid : 2 * hid] = add(gdl, act).astype(BF)
    pack[:, 2 * hid :] = pick[...]
    up_in[...] = add(part, normed)
    at = 0
    out = None
    for g in range(groups):
        for i in range(sizes[g]):
            term = dot_over(down[g][pl.ds(i * block, block), :], grads[at][...])
            out = term if out is None else out + term
            at += 1
    down_out[...] = out


def add_body(left, right, out):
    out[...] = (left[...].astype(F32) + right[...].astype(F32)).astype(BF)


def mid_back_body(count, mask, cotangent, mid, gain, proj_out, w_all, in_all, *refs):
    pieces = refs[: count[0]]
    grad_mid, grad_attn, grad_low = refs[count[0] : count[0] + 3]
    outs = refs[count[0] + 3 :]
    width = outs[0].shape[1]
    half = cotangent.shape[0] // 2

    def one(i):
        part = rows_at(i, half)
        upstream = pieces[0][part, :].astype(F32)
        for piece in pieces[1:]:
            upstream = upstream + piece[part, :].astype(F32)
        unit, inv = norm_parts(mid[part, :])
        total = cotangent[part, :] + norm_back(unit, inv, upstream * gain[...])
        grad_mid[part, :] = total
        attn = total.astype(BF)
        grad_attn[part, :] = attn

    repeat(2, one)
    attn = grad_attn[...]
    low = (dot_back(attn, proj_out[...]) * mask[pl.ds(0, 2 * half), :]).astype(BF)
    grad_low[...] = low
    value = (dot_back(attn, w_all[...]) + dot(low, in_all[...])).astype(BF)
    for d in range(count[1]):
        outs[d][...] = value[:, d * width : (d + 1) * width]


def message_body(count, pairs, me, up_in, down_out, proj_low, grad_attn, grad_low, *refs):
    attended = refs[: count * pairs]
    outs = refs[count * pairs : count * pairs + count]
    proj_out = refs[count * pairs + count]
    rank = up_in.shape[0]
    block = grad_low.shape[0]
    width = outs[0].shape[1]
    proj_out[...] = dot_over(proj_low[pl.ds(0, grad_low.shape[0]), :], grad_attn[...])
    for d in range(count):
        spot = place_of(0, d, count // 2) * block
        lanes = pl.ds(pl.multiple_of(owner_of(me[0], d, count) * width, width), width)
        outs[d][pl.ds(0, rank), :] = up_in[:, lanes].astype(BF)
        outs[d][pl.ds(rank, rank), :] = down_out[:, lanes].astype(BF)
        outs[d][pl.ds(2 * rank, rank), :] = proj_out[:, lanes].astype(BF)
        for p in range(pairs):
            outs[d][pl.ds(3 * rank, rank), p * PAIR : (p + 1) * PAIR] = dot_over(
                grad_low[...], attended[d * pairs + p][pl.ds(spot, block), :]
            ).astype(BF)


def pack_body(count, plain, pick, *refs):
    fixed = refs[:plain]
    messages = refs[plain : plain + count]
    out = refs[plain + count]
    rank = pick.shape[0]
    at = 0
    for ref in fixed:
        out[:, at : at + ref.shape[1]] = ref[...]
        at += ref.shape[1]
    width = messages[0].shape[1]
    for k in range(messages[0].shape[0] // rank):
        total = messages[0][pl.ds(k * rank, rank), :].astype(F32)
        for d in range(1, count):
            total = total + messages[d][pl.ds(k * rank, rank), :].astype(F32)
        out[:, at : at + width] = total.astype(BF)
        at += width
    out[:, at : at + pick.shape[1]] = pick[...]


def attend_back_body(pair, pairs, count, seq_len, *refs):
    first, last = pair == 0, pair == pairs - 1
    at = 0

    def take(number):
        nonlocal at
        at += number
        return refs[at - number : at]

    if last:
        (me,) = take(1)
    seq, kept = take(2)
    if first:
        pull_near, pull_far = take(2)
        grads = take(count)
    else:
        (grad_seq,) = take(1)
    if last:
        push, low_t, n1_near, n1_far, low_out = take(5)
        earlier = take(3 * (pairs - 1))
    grad_q, grad_k, grad_v = take(3)
    if last:
        part_t, qkv_out = take(2)
        messages = take(count)
    if first:
        grad_seq, grad_all = take(2)
    if last:
        part_seq, total_in = take(2)
    rows = seq.shape[0]
    width = seq.shape[1] // 3
    step = min(256, seq_len)
    scale = 1.0 / math.sqrt(HD)
    if first:
        block = grads[0].shape[0]
        near = pull_near.shape[1]
        for i in range(count):
            grad_all[pl.ds(i * block, block), :] = grads[i][...]
        grad_seq[...] = (
            dot(pull_near[...], grad_all[pl.ds(0, near), :])
            + dot(pull_far[...], grad_all[pl.ds(near, rows - near), :])
        ).astype(BF)
    if last:
        for p in range(pairs - 1):
            span = slice(p * PAIR, (p + 1) * PAIR)
            grad_q[span, :] = earlier[3 * p][...]
            grad_k[:, span] = earlier[3 * p + 1][...]
            grad_v[:, span] = earlier[3 * p + 2][...]
    base_row = pair * PAIR if last else 0

    def one_sequence(s):
        base = s * seq_len
        all_rows = rows_at(s, seq_len)
        lanes = pl.ds(pair * PAIR, PAIR)
        keys = seq[all_rows, pl.ds(width + pair * PAIR, PAIR)]
        values = seq[all_rows, pl.ds(2 * width + pair * PAIR, PAIR)]
        keys_t = keys.astype(F32).T.astype(BF)
        steps = seq_len // step
        sums_k = [None] * steps
        sums_v = [None] * steps
        for q in range(steps):
            span = pl.ds(pl.multiple_of(base + q * step, step), step)
            queries = seq[span, lanes]
            grad = grad_seq[span, lanes]
            seen = (q + 1) * step
            for h in range(2):
                own_q = head_lanes(queries, h)
                own_g = head_lanes(grad, h)
                probs = kept[s, h, :seen, q * step : (q + 1) * step]
                wide_probs = probs.astype(F32)
                mixed = wide_probs * dot_back(values[:seen], own_g)
                centre = jnp.sum(mixed, 0, keepdims=True)
                raw = (mixed - wide_probs * centre).astype(BF)
                grad_q[pl.ds(base_row + h * HD, HD), span] = (
                    dot(keys_t[h * HD : (h + 1) * HD, :seen], raw) * scale
                ).astype(BF)
                to_k = dot(raw, own_q)
                to_v = dot(probs, own_g)
                for b in range(q + 1):
                    cut = slice(b * step, (b + 1) * step)
                    sums_k[b] = to_k[cut] if sums_k[b] is None else sums_k[b] + to_k[cut]
                    sums_v[b] = to_v[cut] if sums_v[b] is None else sums_v[b] + to_v[cut]
        for b in range(steps):
            span = pl.ds(pl.multiple_of(base + b * step, step), step)
            grad_k[span, pl.ds(base_row, PAIR)] = sums_k[b].astype(BF)
            grad_v[span, pl.ds(base_row, PAIR)] = sums_v[b].astype(BF)

    repeat(rows // seq_len, one_sequence)
    if not last:
        return
    near = n1_near.shape[0]
    part = dot(low_out[0], grad_q[...]) + dot_back(low_out[1], grad_k[...]) + dot_back(low_out[2], grad_v[...])
    lane_at = lax.broadcasted_iota(jnp.int32, part.shape, 1) // seq_len
    rank_at = lax.broadcasted_iota(jnp.int32, part.shape, 0) // RANK
    part_seq[...] = jnp.where(lane_at == rank_at, part, 0.0).astype(BF)
    part_t[...] = dot_back(part_seq[...], push[...]).astype(BF)
    total_in[...] = dot(part_t[:, :near], n1_near[...]) + dot(part_t[:, near:], n1_far[...])
    qkv_out[:, :width] = dot_back(low_t[...], grad_q[...]).astype(BF)
    qkv_out[:, width : 2 * width] = dot(low_t[...], grad_k[...]).astype(BF)
    qkv_out[:, 2 * width :] = dot(low_t[...], grad_v[...]).astype(BF)
    for d in range(count):
        lanes = pl.ds(pl.multiple_of(owner_of(me[0], d, count) * width, width), width)
        messages[d][...] = total_in[:, lanes].astype(BF)


def qkv_back_body(ids, push, w_cat, low_in, grad_q, grad_k, grad_v, part_t, out, joined):
    block = out.shape[0] // len(ids)
    width = grad_k.shape[1]

    def one(i, at):
        rows = rows_at(i, block)
        place = push[rows_at(at, block), :]
        joined[:, :width] = dot_back(place, grad_q[...]).astype(BF)
        joined[:, width : 2 * width] = dot(place, grad_k[...]).astype(BF)
        joined[:, 2 * width :] = dot(place, grad_v[...]).astype(BF)
        low = dot_over(part_t[:, rows_at(at, block)], low_in[...])
        out[rows, :] = (dot_back(joined[...], w_cat[...]) + low).astype(BF)

    if ids == tuple(range(len(ids))):
        repeat(len(ids), lambda i: one(i, i))
    else:
        for i, at in enumerate(ids):
            one(i, at)


def add_pieces(total, pieces, i, half):
    part = rows_at(i, half)
    total = total + pieces[0][part, :].astype(F32) + pieces[1][part, :].astype(F32)
    halves = pieces[2:]
    number = len(halves) // 2
    for k in range(number):
        total = total + halves[i * number + k][...].astype(F32)
    return total


def input_back_body(tokens, grad_mid, gain, *refs):
    out, upstream = refs[-2:]
    half = tokens.shape[0] // 2
    for i in range(2):
        upstream[pl.ds(i * half, half), :] = add_pieces(0.0, refs[:-2], i, half)

    def one(i):
        part = rows_at(i, half)
        unit, inv = norm_parts(tokens[part, :].astype(F32))
        out[part, :] = grad_mid[part, :] + norm_back(unit, inv, upstream[part, :] * gain[...])

    repeat(2, one)


def result_body(mid, bias, *refs):
    out = refs[-1]
    half = out.shape[0] // 2
    for i in range(2):
        part = pl.ds(i * half, half)
        out[part, :] = add_pieces(mid[part, :] + bias[...], refs[:-1], i, half)


def spread_hidden_body(hid, found, up_out, down_in):
    pick = found[:, 2 * hid :]
    up_out[...] = dot_over(pick, found[:, :hid])
    down_in[...] = dot_over(found[:, hid : 2 * hid], pick)


def spread_wide_body(width, found, proj_in, wide):
    pick = found[:, 4 * width :]
    for k in range(3):
        wide[pl.ds(k * 128, 128), :] = dot_over(pick, found[:, k * width : (k + 1) * width]).astype(BF)
    proj_in[...] = dot_over(found[:, 3 * width : 4 * width], pick)


def spread_late_body(width, found, qkv_out, wide):
    pick = found[:, 4 * width :]
    for k in range(3):
        qkv_out[k] = dot_over(pick, found[:, k * width : (k + 1) * width])
    wide[...] = dot_over(pick, found[:, 3 * width : 4 * width]).astype(BF)


def place_wide_body(count, me, *refs):
    messages = refs[:count]
    up_in, down_out, proj_out = refs[count:]
    width = messages[0].shape[1]
    for d in range(count):
        span = pl.ds(pl.multiple_of(owner_of(me[0], d, count) * width, width), width)
        up_in[span, :] = messages[d][pl.ds(0, 128), :].astype(F32).T
        down_out[:, span] = messages[d][pl.ds(128, 128), :].astype(F32)
        proj_out[:, span] = messages[d][pl.ds(256, 128), :].astype(F32)


def place_late_body(count, me, *refs):
    messages = refs[:count]
    qkv_in = refs[count]
    width = messages[0].shape[1]
    for d in range(count):
        qkv_in[pl.ds(pl.multiple_of(owner_of(me[0], d, count) * width, width), width), :] = messages[d][...].astype(F32).T


def tie(value, *others):
    return lax.optimization_barrier((value, *others))[0]


def body(
    tensor_size,
    dp_size,
    tokens,
    cotangent,
    lengths,
    order,
    adapter_ids,
    norm1_gain,
    norm1_shift,
    qkv_weight,
    qv_bias,
    proj_weight,
    proj_bias,
    norm2_gain,
    norm2_shift,
    up_weight,
    up_bias,
    down_weight,
    down_bias,
    adapt_qkv_in,
    adapt_qkv_out,
    adapt_proj_in,
    adapt_proj_out,
    adapt_up_in,
    adapt_up_out,
    adapt_down_in,
    adapt_down_out,
):
    count = tensor_size
    chips = count // 2
    own, wide = tokens.shape
    width = qkv_weight.shape[2]
    pairs = width // PAIR
    hid = up_weight.shape[1]
    rows = order.shape[1]
    seqs = lengths.shape[1]
    seq_len = rows // seqs
    ranks = seqs * RANK
    near = 2 * own
    far = rows - near
    cols = adapt_qkv_in.shape[1]
    near_ids = (0, 1)
    even_ids = tuple(range(2, count, 2))
    odd_ids = tuple(range(3, count, 2))
    me = lax.axis_index("tensor")

    core_perm = [(t, t ^ 1) for t in range(count)]

    def core_swap(value):
        return lax.ppermute(value, "tensor", core_perm)

    def chip_hop(value, k):
        return lax.ppermute(value, "tensor", [(t, ((t // 2 + k) % chips) * 2 + t % 2) for t in range(count)])

    def hops_of(value):
        return [chip_hop(value, k) for k in range(1, chips)]

    def weave(value, swapped, moved):
        found = [value, swapped]
        for item in moved:
            found += [item, core_swap(item)]
        return found

    def exchange(messages):
        out = [messages[0], core_swap(messages[1])] + [None] * (count - 2)
        for k in range(1, chips):
            flat = [(t, ((t // 2 - k) % chips) * 2 + t % 2) for t in range(count)]
            cross = [(t, ((t // 2 - k) % chips) * 2 + (t % 2 ^ 1)) for t in range(count)]
            out[2 * (chips - k)] = lax.ppermute(messages[2 * k], "tensor", flat)
            out[2 * (chips - k) + 1] = lax.ppermute(messages[2 * k + 1], "tensor", cross)
        return out

    def join(left, right, name):
        return whole_call(add_body, [left, right], [shape(left.shape, BF)], name)[0]

    def send_far(joined):
        return [chip_hop(joined[(k - 1) * own : k * own] if chips > 2 else joined, -k) for k in range(1, chips)]

    def send_half(joined, part):
        half = own // 2
        return [
            chip_hop(joined[(k - 1) * own + part * half : (k - 1) * own + (part + 1) * half], -k)
            for k in range(1, chips)
        ]

    def dp_swap(value, stride):
        return lax.ppermute(value, "dp", [(i, i ^ stride) for i in range(dp_size)])

    def double(value, moved):
        return jnp.concatenate([value, moved], 0)

    def widen(value, stride):
        while stride:
            value = double(value, dp_swap(value, stride))
            stride //= 2
        return value

    place = me.reshape(1)
    dp_at = lax.axis_index("dp").reshape(1)
    weight_three = jnp.transpose(qkv_weight, (1, 0, 2))
    out_three = jnp.transpose(adapt_qkv_out, (1, 0, 2))
    row = lambda v: v.reshape(1, -1)

    top = dp_size // 2
    token_core = core_swap(tokens)
    token_hops = hops_of(tokens)
    grad_own = tie(cotangent, token_core).astype(BF)
    grad_core = core_swap(grad_own)

    prepared = whole_call(
        functools.partial(prep_body, seq_len, own, count),
        [order, proj_weight, adapt_qkv_in, out_three, adapt_proj_in, adapt_proj_out, adapt_up_in, adapt_up_out, adapt_down_in,
         adapt_down_out],
        [shape((ranks, wide), BF), shape((3, ranks, width), BF), shape((width + 16, wide), BF),
         shape((ranks, wide), BF), shape((ranks, wide), BF), shape((ranks, hid), BF),
         shape((ranks, hid), BF), shape((ranks, wide), BF), shape((rows, near), BF), shape((rows, far), BF),
         shape((rows, rows), BF), shape((rows, ranks), F32), shape((ranks, cols), BF), shape((1, rows), jnp.int32),
         shape((width // 2 + 16, wide), BF)],
        "prep",
        smem=[place, dp_at, lengths, adapter_ids],
        loose=tuple(range(10)),
        scratch=[pltpu.VMEM((rows, 1), jnp.int32)],
    )
    c_qkv_in, c_qkv_out, proj_own, c_proj_out, c_up_in, c_up_out, c_down_in, c_down_out = prepared[:8]
    pull_near, pull_far, push, mask, pick, limit, proj_half = prepared[8:]
    proj_core = core_swap(proj_own)
    proj_hops = hops_of(proj_half)

    norm1 = [row(norm1_gain), row(norm1_shift), weight_three, qv_bias, c_qkv_in, c_qkv_out]
    n1_near, low1_near, moved_near = whole_call(
        functools.partial(qkv_body, near_ids, False),
        [mask] + norm1 + [pull_near, tokens, token_core],
        [shape((near, wide), BF), shape((near, ranks), BF), shape((rows, 3 * width), F32)],
        "qkv_near",
        loose=(1, 2, 3, 4, 8, 9),
        long=True,
        scratch=[pltpu.VMEM((near, 3 * width), BF), pltpu.VMEM((near, wide), BF), pltpu.VMEM((near, ranks), F32)],
    )
    token_hops = [tie(item, low1_near) for item in token_hops]
    token_blocks = weave(tokens, token_core, token_hops)
    n1_far, low1_far, qkv_seq = whole_call(
        functools.partial(qkv_body, tuple(range(2, count)), True),
        [mask] + norm1 + [pull_far] + token_blocks[2:] + [moved_near],
        [shape((far, wide), BF), shape((far, ranks), BF), shape((rows, 3 * width), BF)],
        "qkv_far",
        scratch=[pltpu.VMEM((far, 3 * width), BF), pltpu.VMEM((far, wide), BF), pltpu.VMEM((far, ranks), F32)],
    )

    grad_hops = hops_of(tie(grad_own, low1_far))
    sums = []
    attended = []
    seq_in = qkv_seq
    for pair in range(pairs):
        part, kept = whole_call(
            functools.partial(attend_body, seq_len, pair),
            [limit, seq_in, push],
            [shape((rows, PAIR), BF), shape((seqs, 2, seq_len, seq_len), BF)],
            f"attend{pair}",
            scratch=[pltpu.VMEM((PAIR, rows), BF)],
        )
        sums.append(kept)
        attended.append(part)
        if pair == 0:
            seq_in = tie(qkv_seq, part)
    after = attended[-1]
    gathered_heads = []
    for part in attended:
        gathered_heads.append(weave(part, core_swap(part), hops_of(part)))
    heads = [gathered_heads[p][d] for d in range(count) for p in range(pairs)]

    proj_parts = []
    for item in proj_hops:
        item = tie(item, after)
        other = dp_swap(item[: width // 2], 1)
        proj_parts += [item, other, core_swap(item), core_swap(other)]
    grad_blocks = weave(grad_own, grad_core, [tie(item, after) for item in grad_hops])
    w_all, in_all, w_cat, low_t = whole_call(
        functools.partial(join_body, count),
        [low1_near, low1_far, push, weight_three, proj_own, proj_core] + proj_parts,
        [shape((wide, wide), BF), shape((ranks, wide), BF), shape((wide, 3 * width), BF), shape((ranks, rows), BF)],
        "join",
        smem=[dp_at],
    )

    def block_call(ids, gate, name):
        size = len(ids) * own
        extra = [shape((size, ranks), BF), shape((size, wide), F32)] if 0 in ids else []
        keep = mask if gate is None else tie(mask, gate)
        return whole_call(
            functools.partial(block_body, ids, count, pairs, min(512, hid)),
            [keep, w_all, in_all, c_proj_out, row(proj_bias), row(norm2_gain), row(norm2_shift), c_up_in, up_weight,
             row(up_bias), c_up_out, down_weight, c_down_in, c_down_out]
            + [token_blocks[i] for i in ids] + [grad_blocks[i] for i in ids] + heads,
            [shape((size, wide), BF), shape((size, wide), BF), shape((size, ranks), BF), shape((size, ranks), BF),
             shape((size, ranks), BF), shape((size, hid), BF), shape((size, hid), BF), shape((size, ranks), BF)]
            + extra,
            name,
            scratch=[pltpu.VMEM((size, wide), BF)] * 3
            + [pltpu.VMEM((size, ranks), F32), pltpu.VMEM((own, wide), F32)] + [pltpu.VMEM((own, ranks), F32)] * 2,
            long=gate is not None,
        )

    odd = block_call(odd_ids, None, "block_odd")
    odd_moved = core_swap(odd[0])
    even = block_call(even_ids, odd[3], "block_even")
    up_joined = join(even[0], odd_moved, "up_join")
    up_hops = send_far(up_joined)
    mine = block_call(near_ids, up_joined, "block_near")
    up_swap = core_swap(mine[0][own:])
    groups = (mine, even, odd)
    order_ids = (near_ids, even_ids, odd_ids)
    pack_hidden, p_up_in, p_down_out = whole_call(
        functools.partial(hidden_grads_body, 3, tuple(len(i) for i in order_ids)),
        [pick] + [g[k] for k in (2, 6, 4, 5, 3, 1, 7) for g in groups]
        + [grad_blocks[i] for ids in order_ids for i in ids],
        [shape((ranks, 2 * hid + cols), BF), shape((ranks, wide), F32), shape((ranks, wide), F32)],
        "hidden_grads",
    )
    up_hops = [tie(item, p_up_in) for item in up_hops]
    proj_low, mid = mine[8:]
    back = whole_call(
        functools.partial(mid_back_body, (2 + len(up_hops), count)),
        [mask, cotangent, mid, row(norm2_gain), c_proj_out, w_all, in_all, mine[0], up_swap] + up_hops,
        [shape((own, wide), F32), shape((own, wide), BF), shape((own, ranks), BF)]
        + [shape((own, width), BF)] * count,
        "mid_back",
        long=True,
    )
    grad_mid, grad_attn, grad_proj_low = back[:3]
    grad_att = exchange(back[3:])
    hidden_moved = dp_swap(tie(pack_hidden, grad_proj_low), top)

    messages = whole_call(
        functools.partial(message_body, count, pairs),
        [p_up_in, p_down_out, proj_low, grad_attn, grad_proj_low] + heads,
        [shape((4 * ranks, width), BF)] * count,
        "message",
        smem=[place],
        scratch=[pltpu.VMEM((ranks, wide), F32)],
        long=True,
    )
    down_parts = whole_call(
        functools.partial(down_body, 3, own),
        [tie(down_weight, messages[0]), c_down_out] + [g[5] for g in groups] + [g[7] for g in groups],
        [shape(g[0].shape, BF) for g in groups],
        "down",
        long=True,
    )
    down_mine, down_even, down_odd = down_parts
    grad_att = [grad_att[0]] + [tie(item, down_mine) for item in grad_att[1:]]
    wide_messages = exchange([tie(item, *grad_att[1:]) for item in messages])
    down_moved = core_swap(tie(down_odd, *grad_att[1:]))
    down_swap = core_swap(tie(down_mine[own:], *grad_att[1:]))

    back_pieces = []
    grad_seq = None
    for pair in range(pairs):
        last = pair == pairs - 1
        inputs = [qkv_seq, sums[pair]]
        outs = [shape((PAIR, rows), BF), shape((rows, PAIR), BF), shape((rows, PAIR), BF)]
        scratch = []
        if pair == 0:
            inputs += [pull_near, pull_far] + grad_att
        else:
            inputs += [grad_seq]
        if last:
            inputs += [push, low_t, n1_near, n1_far, c_qkv_out] + back_pieces
            outs = [shape((width, rows), BF), shape((rows, width), BF), shape((rows, width), BF),
                    shape((ranks, rows), BF), shape((ranks, 3 * width), BF)] + [shape((ranks, width), BF)] * count
        if pair == 0:
            if last:
                scratch += [pltpu.VMEM((rows, width), BF)]
            else:
                outs += [shape((rows, width), BF)]
            scratch += [pltpu.VMEM((rows, width), BF)]
        if last:
            scratch += [pltpu.VMEM((ranks, rows), BF), pltpu.VMEM((ranks, wide), F32)]
        results = whole_call(
            functools.partial(attend_back_body, pair, pairs, count, seq_len),
            inputs,
            outs,
            f"attend_back{pair}",
            smem=[place] if last else [],
            scratch=scratch,
            long=True,
        )
        if pair == 0:
            passed = results[0]
            wide_messages = [wide_messages[0]] + [tie(item, passed) for item in wide_messages[1:]]
            (pack_wide,) = whole_call(
                functools.partial(pack_body, count, 0),
                [pick] + wide_messages,
                [shape((ranks, 4 * width + cols), BF)],
                "pack_wide",
            )
            hidden_half = double(pack_hidden, tie(hidden_moved, passed, *wide_messages))
            hidden_moved = dp_swap(hidden_half, top // 2)
            hidden_first = dp_swap(hidden_half, top // 4)
            wide_moved = dp_swap(pack_wide, top)
            down_joined = join(down_even, tie(down_moved, passed, *wide_messages), "down_join")
            down_first = send_half(down_joined, 0)
        if not last:
            back_pieces += list(results[:3])
            grad_seq = tie(results[3], pack_wide, hidden_half, down_joined)
    grad_q, grad_k, grad_v, part_t, g_qkv_out = results[:5]
    down_first = [tie(item, part_t) for item in down_first]
    hidden_moved = tie(hidden_moved, part_t)
    hidden_first = tie(hidden_first, part_t)
    late_messages = exchange(results[5:])
    hidden_second = dp_swap(hidden_moved, top // 4)
    wide_moved_first = tie(wide_moved, part_t)
    wide_found = double(pack_wide, wide_moved_first)
    wide_moved = dp_swap(wide_found, top // 2)

    def unproject(ids, gates, name):
        size = len(ids) * own
        return whole_call(
            functools.partial(qkv_back_body, ids),
            [push, w_cat, c_qkv_in, grad_q, grad_k, grad_v, tie(part_t, *gates)],
            [shape((size, wide), BF)],
            name,
            scratch=[pltpu.VMEM((own, 3 * width), BF)],
            long=True,
        )[0]

    odd_part = unproject(odd_ids, [wide_moved_first, hidden_moved, hidden_first, *down_first], "qkv_back_odd")
    odd_moved = core_swap(odd_part)
    even_part = unproject(even_ids, [odd_part], "qkv_back_even")
    qkv_joined = join(even_part, tie(odd_moved, *late_messages[1:], wide_moved), "qkv_join")
    qkv_first = send_half(qkv_joined, 0)
    late_messages = [late_messages[0]] + [tie(item, qkv_joined) for item in late_messages[1:]]
    (pack_late,) = whole_call(
        functools.partial(pack_body, count, 1),
        [pick, g_qkv_out] + late_messages,
        [shape((ranks, 4 * width + cols), BF)],
        "pack_late",
    )
    late_moved = dp_swap(pack_late, top)
    wide_found = double(wide_found, wide_moved)
    wide_moved = dp_swap(wide_found, top // 4)
    near_part = unproject(near_ids, [qkv_joined, pack_late, hidden_second], "qkv_back_near")
    qkv_swap = core_swap(near_part[own:])
    qkv_first = [tie(item, near_part) for item in qkv_first]
    qkv_second = send_half(tie(qkv_joined, *qkv_first), 1)
    late_found = double(pack_late, tie(late_moved, near_part, *qkv_first))
    late_moved = dp_swap(late_found, top // 2)
    late_moved = tie(late_moved, *qkv_second)
    wide_found = widen(double(wide_found, tie(wide_moved, late_moved)), top // 8)
    proj_in_full, wide_part = whole_call(
        functools.partial(spread_wide_body, width),
        [wide_found],
        [shape((width, cols), F32), shape((3 * cols, width), BF)],
        "spread_wide",
        final=(0,),
    )
    wide_blocks = weave(wide_part, core_swap(wide_part), hops_of(wide_part))
    late_found = double(late_found, late_moved)
    late_moved = dp_swap(late_found, top // 4)
    down_second = send_half(tie(down_joined, *qkv_second), 1)
    (grad_input,) = whole_call(
        input_back_body,
        [tokens, grad_mid, row(norm1_gain), near_part, qkv_swap, *qkv_first, *qkv_second],
        [shape((own, wide), F32)],
        "input_back",
        scratch=[pltpu.VMEM((own, wide), F32)],
        final=(0,),
    )
    late_found = widen(double(late_found, tie(late_moved, grad_input)), top // 8)
    qkv_out_full, late_part = whole_call(
        functools.partial(spread_late_body, width),
        [late_found],
        [shape((3, cols, width), F32), shape((cols, width), BF)],
        "spread_late",
        final=(0,),
    )
    late_swap = core_swap(late_part)
    late_hops = hops_of(late_part)
    hidden_found = jnp.concatenate([hidden_half, hidden_moved, hidden_first, tie(hidden_second, late_part)], 0)
    up_out_full, down_in_full = whole_call(
        functools.partial(spread_hidden_body, hid),
        [widen(hidden_found, top // 8)],
        [shape((cols, hid), F32), shape((hid, cols), F32)],
        "spread_hidden",
        final=(0, 1),
    )
    up_in_full, down_out_full, proj_out_full = whole_call(
        functools.partial(place_wide_body, count),
        [tie(wide_blocks[0], up_out_full)] + wide_blocks[1:],
        [shape((wide, cols), F32), shape((cols, wide), F32), shape((cols, wide), F32)],
        "place_wide",
        smem=[place],
        final=(0, 1, 2),
    )
    late_blocks = weave(late_part, late_swap, [tie(item, up_in_full) for item in late_hops])
    (result,) = whole_call(
        result_body,
        [mid, row(down_bias), down_mine, down_swap, *down_first, *[tie(item, up_in_full) for item in down_second]],
        [shape((own, wide), F32)],
        "result",
        final=(0,),
    )
    (qkv_in_full,) = whole_call(
        functools.partial(place_late_body, count),
        late_blocks,
        [shape((wide, cols), F32)],
        "place_late",
        smem=[place],
        final=(0,),
    )
    return (
        result,
        grad_input,
        qkv_in_full,
        jnp.transpose(qkv_out_full, (1, 0, 2)),
        proj_in_full,
        proj_out_full,
        up_in_full,
        up_out_full,
        down_in_full,
        down_out_full,
    )


def solution(mesh):
    in_specs = (
        P(("dp", "tensor"), None),
        P(("dp", "tensor"), None),
        P("dp", None),
        P("dp", None),
        P("dp", None),
        P(),
        P(),
        P(None, None, "tensor"),
        P(None, "tensor"),
        P("tensor", None),
        P(),
        P(),
        P(),
        P(None, "tensor"),
        P("tensor"),
        P("tensor", None),
        P(),
        P(),
        P(None, None, "tensor"),
        P("tensor", None),
        P(),
        P(),
        P(None, "tensor"),
        P("tensor", None),
        P(),
    )
    out_specs = (
        P(("dp", "tensor"), None),
        P(("dp", "tensor"), None),
        P(),
        P(None, None, "tensor"),
        P("tensor", None),
        P(),
        P(),
        P(None, "tensor"),
        P("tensor", None),
        P(),
    )
    run = functools.partial(body, mesh.shape["tensor"], mesh.shape["dp"])
    return jax.shard_map(run, mesh=mesh, in_specs=in_specs, out_specs=out_specs, check_vma=False)
```

```python
import functools
import math

import jax
import jax.numpy as jnp
from jax import lax
from jax.experimental import pallas as pl
from jax.experimental.pallas import tpu as pltpu
from jax.sharding import PartitionSpec as P

HD = 64
RANK = 16
PAIR = 2 * HD
EPSILON = 1e-05
NEGATIVE = -1000000000.0
BF = jnp.bfloat16
F32 = jnp.float32
LIMIT = 10 * 1024 * 1024
GELU_A = math.sqrt(2.0 / math.pi)
GELU_B = 0.044715


def dot(left, right):
    return jnp.dot(left, right, preferred_element_type=F32)


def dot_back(left, right):
    return lax.dot_general(left, right, (((1,), (1,)), ((), ())), preferred_element_type=F32)


def dot_over(left, right):
    return lax.dot_general(left, right, (((0,), (0,)), ((), ())), preferred_element_type=F32)


def shape(dims, kind):
    return jax.ShapeDtypeStruct(tuple(dims), kind)


def whole_call(body, inputs, outs, name, smem=(), scratch=(), final=(), loose=(), long=False):
    smem_spec = pl.BlockSpec(memory_space=pltpu.SMEM)
    vmem_spec = pl.BlockSpec(memory_space=pltpu.VMEM)
    held = [
        pltpu.with_memory_space_constraint(x, pltpu.HBM if i in loose else pltpu.VMEM) for i, x in enumerate(inputs)
    ]
    kinds = [o if i in final else pltpu.VMEM(o.shape, o.dtype) for i, o in enumerate(outs)]
    return pl.pallas_call(
        body,
        out_shape=kinds,
        in_specs=[smem_spec] * len(smem) + [vmem_spec] * len(inputs),
        out_specs=[vmem_spec] * len(outs),
        scratch_shapes=list(scratch),
        compiler_params=pltpu.CompilerParams(vmem_limit_bytes=LIMIT),
        name=name,
    )(*smem, *held)


def norm_parts(values):
    centre = values - jnp.mean(values, -1, keepdims=True)
    spread = jnp.mean(centre * centre, -1, keepdims=True)
    inv = lax.rsqrt(spread + EPSILON)
    return centre * inv, inv


def norm_back(normed, inv, upstream):
    return inv * (
        upstream
        - jnp.mean(upstream, -1, keepdims=True)
        - normed * jnp.mean(upstream * normed, -1, keepdims=True)
    )


def rows_at(i, size):
    return pl.ds(pl.multiple_of(i * size, size), size)


def repeat(count, step):
    if count == 1:
        step(0)
    else:
        lax.fori_loop(0, count, lambda i, carry: (step(i), carry)[1], 0)


def owner_of(me, d, count):
    return (((me // 2) + count // 2 - d // 2) % (count // 2)) * 2 + ((me % 2 + d % 2) % 2)


def prep_body(
    seq_len, own, count, me, dp_at, lengths, ids, order, proj_w, qkv_in, qkv_out, proj_in, proj_out, up_in, up_out,
    down_in, down_out, *outs
):
    o_qkv_in, o_qkv_out, o_proj, o_proj_out, o_up_in, o_up_out, o_down_in, o_down_out = outs[:8]
    pull_near, pull_far, push, mask, pick, limit, o_half, tall_ref = outs[8:]
    rank_at = lax.broadcasted_iota(jnp.int32, pick.shape, 0)
    col_at = lax.broadcasted_iota(jnp.int32, pick.shape, 1)
    wanted = rank_at + ids[0, 0] * RANK
    slot = lax.broadcasted_iota(jnp.int32, limit.shape, 1)
    bound = jnp.minimum(slot + 1, lengths[0, 0])
    for s in range(1, lengths.shape[1]):
        wanted = jnp.where(rank_at >= s * RANK, rank_at - s * RANK + ids[0, s] * RANK, wanted)
        bound = jnp.where(slot >= s * seq_len, jnp.minimum(slot - s * seq_len + 1, lengths[0, s]), bound)
    limit[...] = bound
    chosen = jnp.where(col_at == wanted, 1.0, 0.0).astype(BF)
    pick[...] = chosen
    width = proj_w.shape[0]
    fold = pick.shape[0] // count
    o_proj[pl.ds(0, width), :] = proj_w[...]
    o_proj[pl.ds(width, 16), :] = jnp.zeros((16, o_proj.shape[1]), BF)
    chosen_in = dot_back(chosen, proj_in[...])
    for j in range(count):
        o_proj[pl.ds(width, fold), j * width : (j + 1) * width] = chosen_in[j * fold : (j + 1) * fold].astype(BF)
    half = width // 2
    o_half[pl.ds(0, half), :] = proj_w[pl.ds(pl.multiple_of(dp_at[0] % 2 * half, half), half), :]
    o_half[pl.ds(half, 16), :] = o_proj[pl.ds(width, 16), :]
    o_qkv_in[...] = dot_back(chosen, qkv_in[...]).astype(BF)
    for k in range(3):
        o_qkv_out[k] = dot(chosen, qkv_out[k]).astype(BF)
    o_proj_out[...] = dot(chosen, proj_out[...]).astype(BF)
    o_up_in[...] = dot_back(chosen, up_in[...]).astype(BF)
    o_up_out[...] = dot(chosen, up_out[...]).astype(BF)
    o_down_in[...] = dot_back(chosen, down_in[...]).astype(BF)
    o_down_out[...] = dot(chosen, down_out[...]).astype(BF)
    stored = order[...]
    relative = stored
    for d in range(count):
        start = owner_of(me[0], d, count) * own
        relative = jnp.where((stored >= start) & (stored < start + own), stored - start + d * own, relative)
    near = pull_near.shape[1]
    rows = push.shape[0]
    tall = jnp.broadcast_to(relative.astype(F32), (8, rows)).T[:, :1].astype(jnp.int32)
    tall_ref[...] = tall

    def one_hot(i):
        part = rows_at(i, own)
        for ref, start in ((pull_near, 0), (pull_far, near)):
            at = lax.broadcasted_iota(jnp.int32, (own, ref.shape[1]), 1) + start
            ref[part, :] = jnp.where(at == tall_ref[part, :], 1.0, 0.0).astype(BF)
        at = lax.broadcasted_iota(jnp.int32, (own, rows), 0) + i * own
        push[part, :] = jnp.where(at == relative, 1.0, 0.0).astype(BF)

    repeat(rows // own, one_hot)
    seq_at = lax.broadcasted_iota(jnp.int32, mask.shape, 0) // seq_len
    lane_at = lax.broadcasted_iota(jnp.int32, mask.shape, 1) // RANK
    mask[...] = dot(push[...], jnp.where(seq_at == lane_at, 1.0, 0.0).astype(BF))


def qkv_body(ids, last, mask, gain, shift, weight, bias, low_in, low_out, pull, *refs):
    count = len(ids)
    blocks = refs[:count]
    rest = refs[count:]
    earlier = None
    if last:
        earlier, rest = rest[0], rest[1:]
    normed_ref, low_ref, moved_ref, joined, tokens, keep = rest
    rows = blocks[0].shape[0]
    width = weight.shape[2]
    for i in range(count):
        tokens[pl.ds(i * rows, rows), :] = blocks[i][...]
        keep[pl.ds(i * rows, rows), :] = mask[pl.ds(ids[i] * rows, rows), :]

    def project(i):
        part = rows_at(i, rows)
        unit, _ = norm_parts(tokens[part, :].astype(F32))
        normed = (unit * gain[...] + shift[...]).astype(BF)
        normed_ref[part, :] = normed
        low = (dot_back(normed, low_in[...]) * keep[part, :]).astype(BF)
        low_ref[part, :] = low
        for k in range(3):
            value = dot(normed, weight[k]) + dot(low, low_out[k])
            if k != 1:
                value = value + bias[k // 2 : k // 2 + 1, :]
            joined[part, k * width : (k + 1) * width] = value.astype(BF)

    repeat(count, project)
    total = moved_ref.shape[0]
    step = min(256, total)

    def move(i):
        part = rows_at(i, step)
        moved = dot(pull[part, :], joined[...])
        if last:
            moved = moved + earlier[part, :]
            moved_ref[part, :width] = (moved[:, :width] * (1.0 / math.sqrt(HD))).astype(BF)
            moved_ref[part, width:] = moved[:, width:].astype(BF)
        else:
            moved_ref[part, :] = moved

    repeat(total // step, move)


def head_lanes(values, head):
    lane = lax.broadcasted_iota(jnp.int32, values.shape, 1)
    return jnp.where((lane // HD) == head, values, jnp.zeros_like(values))


def attend_body(seq_len, pair, limit, seq, push, out, kept, turned):
    rows = seq.shape[0]
    width = seq.shape[1] // 3
    step = min(256, seq_len)

    def one(s):
        base = s * seq_len
        all_rows = rows_at(s, seq_len)
        keys = seq[all_rows, pl.ds(width + pair * PAIR, PAIR)]
        values = seq[all_rows, pl.ds(2 * width + pair * PAIR, PAIR)]
        values_t = values.astype(F32).T.astype(BF)
        for q in range(seq_len // step):
            span = pl.ds(pl.multiple_of(base + q * step, step), step)
            queries = seq[span, pl.ds(pair * PAIR, PAIR)]
            seen = (q + 1) * step
            allowed = lax.broadcasted_iota(jnp.int32, (seen, step), 0) < limit[:, span]
            for h in range(2):
                scores = dot_back(keys[:seen], head_lanes(queries, h))
                scores = jnp.where(allowed, scores, NEGATIVE)
                weights = jnp.exp(scores - jnp.max(scores, 0, keepdims=True))
                total = jnp.sum(weights, 0, keepdims=True)
                probs = (weights * (1.0 / total)).astype(BF)
                kept[s, h, :seen, q * step : (q + 1) * step] = probs
                turned[pl.ds(h * HD, HD), span] = dot(values_t[h * HD : (h + 1) * HD, :seen], probs).astype(BF)

    repeat(rows // seq_len, one)
    out[...] = dot_back(push[...], turned[...]).astype(BF)


def join_body(count, dp_at, low_near, low_far, push, weight, *refs):
    proj = refs[:2]
    parts = refs[2 : 2 + 2 * (count - 2)]
    w_all, in_all, w_cat, low_t = refs[2 + 2 * (count - 2) :]
    width = in_all.shape[1] // count
    half = width // 2
    fold = in_all.shape[0] // count
    near = low_near.shape[0]
    for d in range(count):
        if d < 2:
            source, at = proj[d], width
            w_all[pl.ds(d * width, width), :] = source[pl.ds(0, width), :]
        else:
            source, at = parts[2 * (d - 2)], half
            start = pl.multiple_of(dp_at[0] % 2 * half, half)
            w_all[pl.ds(d * width + start, half), :] = source[pl.ds(0, half), :]
            start = pl.multiple_of((dp_at[0] + 1) % 2 * half, half)
            w_all[pl.ds(d * width + start, half), :] = parts[2 * (d - 2) + 1][...]
        for j in range(count):
            part = source[pl.ds(at, fold), j * width : (j + 1) * width]
            in_all[pl.ds(j * fold, fold), d * width : (d + 1) * width] = part
    for k in range(3):
        w_cat[:, k * width : (k + 1) * width] = weight[k]
    rows = push.shape[0]
    low_t[...] = (
        dot_over(low_near[...], push[pl.ds(0, near), :]) + dot_over(low_far[...], push[pl.ds(near, rows - near), :])
    ).astype(BF)


def place_of(block, sender, chips):
    return ((block // 2 - sender // 2) % chips) * 2 + ((block % 2) ^ (sender % 2))


def block_body(
    ids, count, pairs, chunk, mask, w_all, in_all, proj_out, proj_bias, gain, shift, up_in, up_w, up_b, up_out,
    down_w, down_in, down_out, *refs
):
    size = len(ids)
    tokens = refs[:size]
    grads = refs[size : 2 * size]
    attended = refs[2 * size : 2 * size + count * pairs]
    rest = refs[2 * size + count * pairs :]
    outs = rest[: len(rest) - 7]
    heads, grad_all, token_all, keep_all, acc, low_acc, down_acc = rest[len(rest) - 7 :]
    part_ref, normed_ref, low_ref, low_part, grad_down_low, act_ref, gup_ref, down_low = outs[:8]
    block = tokens[0].shape[0]
    width = in_all.shape[1] // count
    for i in range(size):
        part = pl.ds(i * block, block)
        for d in range(count):
            spot = place_of(ids[i], d, count // 2) * block
            for p in range(pairs):
                at = d * width + p * PAIR
                heads[part, at : at + PAIR] = attended[d * pairs + p][pl.ds(spot, block), :]
        keep_all[part, :] = mask[pl.ds(ids[i] * block, block), :]
        grad_all[part, :] = grads[i][...]
        token_all[part, :] = tokens[i][...]

    def one(i):
        part = rows_at(i, block)
        keep = keep_all[part, :]
        grad = grad_all[part, :]
        grad_low = (dot_back(grad, down_out[...]) * keep).astype(BF)
        grad_down_low[part, :] = grad_low
        rows = heads[part, :]
        low = (dot_back(rows, in_all[...]) * keep).astype(BF)
        mid = dot(rows, w_all[...]) + dot(low, proj_out[...]) + proj_bias[...] + token_all[part, :].astype(F32)
        unit, _ = norm_parts(mid)
        normed = (unit * gain[...] + shift[...]).astype(BF)
        normed_ref[part, :] = normed
        low2 = (dot_back(normed, up_in[...]) * keep).astype(BF)
        low_ref[part, :] = low2
        if len(outs) > 8:
            outs[8][part, :] = low
            outs[9][part, :] = mid
        acc[...] = jnp.zeros_like(acc)
        low_acc[...] = jnp.zeros_like(low_acc)
        down_acc[...] = jnp.zeros_like(down_acc)

        def one_chunk(j):
            cut = rows_at(j, chunk)
            upper = dot(normed, up_w[:, cut]) + dot(low2, up_out[:, cut]) + up_b[:, cut]
            grad_act = dot_back(grad, down_w[cut, :]) + dot(grad_low, down_in[:, cut])
            square = upper * upper
            curve = jnp.tanh(GELU_A * upper * (1.0 + GELU_B * square))
            half = 0.5 * (1.0 + curve)
            active = (upper * half).astype(BF)
            act_ref[part, cut] = active
            slope = half + 0.5 * upper * (1.0 - curve * curve) * (GELU_A * (1.0 + 3.0 * GELU_B * square))
            grad_upper = (grad_act * slope).astype(BF)
            gup_ref[part, cut] = grad_upper
            acc[...] += dot_back(grad_upper, up_w[:, cut])
            low_acc[...] += dot_back(grad_upper, up_out[:, cut])
            down_acc[...] += dot_back(active, down_in[:, cut])

        repeat(up_w.shape[1] // chunk, one_chunk)
        low = (low_acc[...] * keep).astype(BF)
        low_part[part, :] = low
        down_low[part, :] = (down_acc[...] * keep).astype(BF)
        part_ref[part, :] = (acc[...] + dot(low, up_in[...])).astype(BF)

    repeat(size, one)


def down_body(groups, block, down_w, down_out, *refs):
    for g in range(groups):
        act, low, out = refs[g], refs[groups + g], refs[2 * groups + g]

        def one(i, act=act, low=low, out=out):
            part = rows_at(i, block)
            out[part, :] = (dot(act[part, :], down_w[...]) + dot(low[part, :], down_out[...])).astype(BF)

        repeat(act.shape[0] // block, one)


def hidden_grads_body(groups, sizes, pick, *refs):
    low2 = refs[:groups]
    gup = refs[groups : 2 * groups]
    gdl = refs[2 * groups : 3 * groups]
    act = refs[3 * groups : 4 * groups]
    part = refs[4 * groups : 5 * groups]
    normed = refs[5 * groups : 6 * groups]
    down = refs[6 * groups : 7 * groups]
    rest = refs[7 * groups :]
    total = sum(sizes)
    grads = rest[:total]
    pack, up_in, down_out = rest[total:]
    hid = gup[0].shape[1]
    block = grads[0].shape[0]
    add = lambda left, right: sum([dot_over(a[...], b[...]) for a, b in zip(left[1:], right[1:])], dot_over(left[0][...], right[0][...]))
    pack[:, :hid] = add(low2, gup).astype(BF)
    pack[:, hid : 2 * hid] = add(gdl, act).astype(BF)
    pack[:, 2 * hid :] = pick[...]
    up_in[...] = add(part, normed)
    at = 0
    out = None
    for g in range(groups):
        for i in range(sizes[g]):
            term = dot_over(down[g][pl.ds(i * block, block), :], grads[at][...])
            out = term if out is None else out + term
            at += 1
    down_out[...] = out


def add_body(left, right, out):
    out[...] = (left[...].astype(F32) + right[...].astype(F32)).astype(BF)


def mid_back_body(count, mask, cotangent, mid, gain, proj_out, w_all, in_all, *refs):
    pieces = refs[: count[0]]
    grad_mid, grad_attn, grad_low = refs[count[0] : count[0] + 3]
    outs = refs[count[0] + 3 :]
    width = outs[0].shape[1]
    half = cotangent.shape[0] // 2

    def one(i):
        part = rows_at(i, half)
        upstream = pieces[0][part, :].astype(F32)
        for piece in pieces[1:]:
            upstream = upstream + piece[part, :].astype(F32)
        unit, inv = norm_parts(mid[part, :])
        total = cotangent[part, :] + norm_back(unit, inv, upstream * gain[...])
        grad_mid[part, :] = total
        attn = total.astype(BF)
        grad_attn[part, :] = attn

    repeat(2, one)
    attn = grad_attn[...]
    low = (dot_back(attn, proj_out[...]) * mask[pl.ds(0, 2 * half), :]).astype(BF)
    grad_low[...] = low
    value = (dot_back(attn, w_all[...]) + dot(low, in_all[...])).astype(BF)
    for d in range(count[1]):
        outs[d][...] = value[:, d * width : (d + 1) * width]


def message_body(count, pairs, me, up_in, down_out, proj_low, grad_attn, grad_low, *refs):
    attended = refs[: count * pairs]
    outs = refs[count * pairs : count * pairs + count]
    proj_out = refs[count * pairs + count]
    rank = up_in.shape[0]
    block = grad_low.shape[0]
    width = outs[0].shape[1]
    proj_out[...] = dot_over(proj_low[pl.ds(0, grad_low.shape[0]), :], grad_attn[...])
    for d in range(count):
        spot = place_of(0, d, count // 2) * block
        lanes = pl.ds(pl.multiple_of(owner_of(me[0], d, count) * width, width), width)
        outs[d][pl.ds(0, rank), :] = up_in[:, lanes].astype(BF)
        outs[d][pl.ds(rank, rank), :] = down_out[:, lanes].astype(BF)
        outs[d][pl.ds(2 * rank, rank), :] = proj_out[:, lanes].astype(BF)
        for p in range(pairs):
            outs[d][pl.ds(3 * rank, rank), p * PAIR : (p + 1) * PAIR] = dot_over(
                grad_low[...], attended[d * pairs + p][pl.ds(spot, block), :]
            ).astype(BF)


def pack_body(count, plain, pick, *refs):
    fixed = refs[:plain]
    messages = refs[plain : plain + count]
    out = refs[plain + count]
    rank = pick.shape[0]
    at = 0
    for ref in fixed:
        out[:, at : at + ref.shape[1]] = ref[...]
        at += ref.shape[1]
    width = messages[0].shape[1]
    for k in range(messages[0].shape[0] // rank):
        total = messages[0][pl.ds(k * rank, rank), :].astype(F32)
        for d in range(1, count):
            total = total + messages[d][pl.ds(k * rank, rank), :].astype(F32)
        out[:, at : at + width] = total.astype(BF)
        at += width
    out[:, at : at + pick.shape[1]] = pick[...]


def attend_back_body(pair, pairs, count, seq_len, *refs):
    first, last = pair == 0, pair == pairs - 1
    at = 0

    def take(number):
        nonlocal at
        at += number
        return refs[at - number : at]

    if last:
        (me,) = take(1)
    seq, kept = take(2)
    if first:
        pull_near, pull_far = take(2)
        grads = take(count)
    else:
        (grad_seq,) = take(1)
    if last:
        push, low_t, n1_near, n1_far, low_out = take(5)
        earlier = take(3 * (pairs - 1))
    grad_q, grad_k, grad_v = take(3)
    if last:
        part_t, qkv_out = take(2)
        messages = take(count)
    if first:
        grad_seq, grad_all = take(2)
    if last:
        part_seq, total_in = take(2)
    rows = seq.shape[0]
    width = seq.shape[1] // 3
    step = min(256, seq_len)
    scale = 1.0 / math.sqrt(HD)
    if first:
        block = grads[0].shape[0]
        near = pull_near.shape[1]
        for i in range(count):
            grad_all[pl.ds(i * block, block), :] = grads[i][...]
        grad_seq[...] = (
            dot(pull_near[...], grad_all[pl.ds(0, near), :])
            + dot(pull_far[...], grad_all[pl.ds(near, rows - near), :])
        ).astype(BF)
    if last:
        for p in range(pairs - 1):
            span = slice(p * PAIR, (p + 1) * PAIR)
            grad_q[span, :] = earlier[3 * p][...]
            grad_k[:, span] = earlier[3 * p + 1][...]
            grad_v[:, span] = earlier[3 * p + 2][...]
    base_row = pair * PAIR if last else 0

    def one_sequence(s):
        base = s * seq_len
        all_rows = rows_at(s, seq_len)
        lanes = pl.ds(pair * PAIR, PAIR)
        keys = seq[all_rows, pl.ds(width + pair * PAIR, PAIR)]
        values = seq[all_rows, pl.ds(2 * width + pair * PAIR, PAIR)]
        keys_t = keys.astype(F32).T.astype(BF)
        steps = seq_len // step
        sums_k = [None] * steps
        sums_v = [None] * steps
        for q in range(steps):
            span = pl.ds(pl.multiple_of(base + q * step, step), step)
            queries = seq[span, lanes]
            grad = grad_seq[span, lanes]
            seen = (q + 1) * step
            for h in range(2):
                own_q = head_lanes(queries, h)
                own_g = head_lanes(grad, h)
                probs = kept[s, h, :seen, q * step : (q + 1) * step]
                wide_probs = probs.astype(F32)
                mixed = wide_probs * dot_back(values[:seen], own_g)
                centre = jnp.sum(mixed, 0, keepdims=True)
                raw = (mixed - wide_probs * centre).astype(BF)
                grad_q[pl.ds(base_row + h * HD, HD), span] = (
                    dot(keys_t[h * HD : (h + 1) * HD, :seen], raw) * scale
                ).astype(BF)
                to_k = dot(raw, own_q)
                to_v = dot(probs, own_g)
                for b in range(q + 1):
                    cut = slice(b * step, (b + 1) * step)
                    sums_k[b] = to_k[cut] if sums_k[b] is None else sums_k[b] + to_k[cut]
                    sums_v[b] = to_v[cut] if sums_v[b] is None else sums_v[b] + to_v[cut]
        for b in range(steps):
            span = pl.ds(pl.multiple_of(base + b * step, step), step)
            grad_k[span, pl.ds(base_row, PAIR)] = sums_k[b].astype(BF)
            grad_v[span, pl.ds(base_row, PAIR)] = sums_v[b].astype(BF)

    repeat(rows // seq_len, one_sequence)
    if not last:
        return
    near = n1_near.shape[0]
    part = dot(low_out[0], grad_q[...]) + dot_back(low_out[1], grad_k[...]) + dot_back(low_out[2], grad_v[...])
    lane_at = lax.broadcasted_iota(jnp.int32, part.shape, 1) // seq_len
    rank_at = lax.broadcasted_iota(jnp.int32, part.shape, 0) // RANK
    part_seq[...] = jnp.where(lane_at == rank_at, part, 0.0).astype(BF)
    part_t[...] = dot_back(part_seq[...], push[...]).astype(BF)
    total_in[...] = dot(part_t[:, :near], n1_near[...]) + dot(part_t[:, near:], n1_far[...])
    qkv_out[:, :width] = dot_back(low_t[...], grad_q[...]).astype(BF)
    qkv_out[:, width : 2 * width] = dot(low_t[...], grad_k[...]).astype(BF)
    qkv_out[:, 2 * width :] = dot(low_t[...], grad_v[...]).astype(BF)
    for d in range(count):
        lanes = pl.ds(pl.multiple_of(owner_of(me[0], d, count) * width, width), width)
        messages[d][...] = total_in[:, lanes].astype(BF)


def qkv_back_body(ids, push, w_cat, low_in, grad_q, grad_k, grad_v, part_t, out, joined):
    block = out.shape[0] // len(ids)
    width = grad_k.shape[1]

    def one(i, at):
        rows = rows_at(i, block)
        place = push[rows_at(at, block), :]
        joined[:, :width] = dot_back(place, grad_q[...]).astype(BF)
        joined[:, width : 2 * width] = dot(place, grad_k[...]).astype(BF)
        joined[:, 2 * width :] = dot(place, grad_v[...]).astype(BF)
        low = dot_over(part_t[:, rows_at(at, block)], low_in[...])
        out[rows, :] = (dot_back(joined[...], w_cat[...]) + low).astype(BF)

    if ids == tuple(range(len(ids))):
        repeat(len(ids), lambda i: one(i, i))
    else:
        for i, at in enumerate(ids):
            one(i, at)


def add_pieces(total, pieces, i, half):
    part = rows_at(i, half)
    total = total + pieces[0][part, :].astype(F32) + pieces[1][part, :].astype(F32)
    halves = pieces[2:]
    number = len(halves) // 2
    for k in range(number):
        total = total + halves[i * number + k][...].astype(F32)
    return total


def input_back_body(tokens, grad_mid, gain, *refs):
    out, upstream = refs[-2:]
    half = tokens.shape[0] // 2
    for i in range(2):
        upstream[pl.ds(i * half, half), :] = add_pieces(0.0, refs[:-2], i, half)

    def one(i):
        part = rows_at(i, half)
        unit, inv = norm_parts(tokens[part, :].astype(F32))
        out[part, :] = grad_mid[part, :] + norm_back(unit, inv, upstream[part, :] * gain[...])

    repeat(2, one)


def result_body(mid, bias, *refs):
    out = refs[-1]
    half = out.shape[0] // 2
    for i in range(2):
        part = pl.ds(i * half, half)
        out[part, :] = add_pieces(mid[part, :] + bias[...], refs[:-1], i, half)


def spread_hidden_body(hid, found, up_out, down_in):
    pick = found[:, 2 * hid :]
    up_out[...] = dot_over(pick, found[:, :hid])
    down_in[...] = dot_over(found[:, hid : 2 * hid], pick)


def spread_wide_body(width, found, proj_in, wide):
    pick = found[:, 4 * width :]
    for k in range(3):
        wide[pl.ds(k * 128, 128), :] = dot_over(pick, found[:, k * width : (k + 1) * width]).astype(BF)
    proj_in[...] = dot_over(found[:, 3 * width : 4 * width], pick)


def spread_late_body(width, found, qkv_out, wide):
    pick = found[:, 4 * width :]
    for k in range(3):
        qkv_out[k] = dot_over(pick, found[:, k * width : (k + 1) * width])
    wide[...] = dot_over(pick, found[:, 3 * width : 4 * width]).astype(BF)


def place_wide_body(count, me, *refs):
    messages = refs[:count]
    up_in, down_out, proj_out = refs[count:]
    width = messages[0].shape[1]
    for d in range(count):
        span = pl.ds(pl.multiple_of(owner_of(me[0], d, count) * width, width), width)
        up_in[span, :] = messages[d][pl.ds(0, 128), :].astype(F32).T
        down_out[:, span] = messages[d][pl.ds(128, 128), :].astype(F32)
        proj_out[:, span] = messages[d][pl.ds(256, 128), :].astype(F32)


def place_late_body(count, me, *refs):
    messages = refs[:count]
    qkv_in = refs[count]
    width = messages[0].shape[1]
    for d in range(count):
        qkv_in[pl.ds(pl.multiple_of(owner_of(me[0], d, count) * width, width), width), :] = messages[d][...].astype(F32).T


def tie(value, *others):
    return lax.optimization_barrier((value, *others))[0]


def body(
    tensor_size,
    dp_size,
    tokens,
    cotangent,
    lengths,
    order,
    adapter_ids,
    norm1_gain,
    norm1_shift,
    qkv_weight,
    qv_bias,
    proj_weight,
    proj_bias,
    norm2_gain,
    norm2_shift,
    up_weight,
    up_bias,
    down_weight,
    down_bias,
    adapt_qkv_in,
    adapt_qkv_out,
    adapt_proj_in,
    adapt_proj_out,
    adapt_up_in,
    adapt_up_out,
    adapt_down_in,
    adapt_down_out,
):
    count = tensor_size
    chips = count // 2
    own, wide = tokens.shape
    width = qkv_weight.shape[2]
    pairs = width // PAIR
    hid = up_weight.shape[1]
    rows = order.shape[1]
    seqs = lengths.shape[1]
    seq_len = rows // seqs
    ranks = seqs * RANK
    near = 2 * own
    far = rows - near
    cols = adapt_qkv_in.shape[1]
    near_ids = (0, 1)
    even_ids = tuple(range(2, count, 2))
    odd_ids = tuple(range(3, count, 2))
    me = lax.axis_index("tensor")

    core_perm = [(t, t ^ 1) for t in range(count)]

    def core_swap(value):
        return lax.ppermute(value, "tensor", core_perm)

    def chip_hop(value, k):
        return lax.ppermute(value, "tensor", [(t, ((t // 2 + k) % chips) * 2 + t % 2) for t in range(count)])

    def hops_of(value):
        return [chip_hop(value, k) for k in range(1, chips)]

    def weave(value, swapped, moved):
        found = [value, swapped]
        for item in moved:
            found += [item, core_swap(item)]
        return found

    def exchange(messages):
        out = [messages[0], core_swap(messages[1])] + [None] * (count - 2)
        for k in range(1, chips):
            flat = [(t, ((t // 2 - k) % chips) * 2 + t % 2) for t in range(count)]
            cross = [(t, ((t // 2 - k) % chips) * 2 + (t % 2 ^ 1)) for t in range(count)]
            out[2 * (chips - k)] = lax.ppermute(messages[2 * k], "tensor", flat)
            out[2 * (chips - k) + 1] = lax.ppermute(messages[2 * k + 1], "tensor", cross)
        return out

    def join(left, right, name):
        return whole_call(add_body, [left, right], [shape(left.shape, BF)], name)[0]

    def send_far(joined):
        return [chip_hop(joined[(k - 1) * own : k * own] if chips > 2 else joined, -k) for k in range(1, chips)]

    def send_half(joined, part):
        half = own // 2
        return [
            chip_hop(joined[(k - 1) * own + part * half : (k - 1) * own + (part + 1) * half], -k)
            for k in range(1, chips)
        ]

    def dp_swap(value, stride):
        return lax.ppermute(value, "dp", [(i, i ^ stride) for i in range(dp_size)])

    def double(value, moved):
        return jnp.concatenate([value, moved], 0)

    def widen(value, stride):
        while stride:
            value = double(value, dp_swap(value, stride))
            stride //= 2
        return value

    place = me.reshape(1)
    dp_at = lax.axis_index("dp").reshape(1)
    weight_three = jnp.transpose(qkv_weight, (1, 0, 2))
    out_three = jnp.transpose(adapt_qkv_out, (1, 0, 2))
    row = lambda v: v.reshape(1, -1)

    top = dp_size // 2
    token_core = core_swap(tokens)
    token_hops = hops_of(tokens)
    grad_own = tie(cotangent, token_core).astype(BF)
    grad_core = core_swap(grad_own)

    prepared = whole_call(
        functools.partial(prep_body, seq_len, own, count),
        [order, proj_weight, adapt_qkv_in, out_three, adapt_proj_in, adapt_proj_out, adapt_up_in, adapt_up_out, adapt_down_in,
         adapt_down_out],
        [shape((ranks, wide), BF), shape((3, ranks, width), BF), shape((width + 16, wide), BF),
         shape((ranks, wide), BF), shape((ranks, wide), BF), shape((ranks, hid), BF),
         shape((ranks, hid), BF), shape((ranks, wide), BF), shape((rows, near), BF), shape((rows, far), BF),
         shape((rows, rows), BF), shape((rows, ranks), F32), shape((ranks, cols), BF), shape((1, rows), jnp.int32),
         shape((width // 2 + 16, wide), BF)],
        "prep",
        smem=[place, dp_at, lengths, adapter_ids],
        loose=tuple(range(10)),
        scratch=[pltpu.VMEM((rows, 1), jnp.int32)],
    )
    c_qkv_in, c_qkv_out, proj_own, c_proj_out, c_up_in, c_up_out, c_down_in, c_down_out = prepared[:8]
    pull_near, pull_far, push, mask, pick, limit, proj_half = prepared[8:]
    proj_core = core_swap(proj_own)
    proj_hops = hops_of(proj_half)

    norm1 = [row(norm1_gain), row(norm1_shift), weight_three, qv_bias, c_qkv_in, c_qkv_out]
    n1_near, low1_near, moved_near = whole_call(
        functools.partial(qkv_body, near_ids, False),
        [mask] + norm1 + [pull_near, tokens, token_core],
        [shape((near, wide), BF), shape((near, ranks), BF), shape((rows, 3 * width), F32)],
        "qkv_near",
        loose=(1, 2, 3, 4, 8, 9),
        long=True,
        scratch=[pltpu.VMEM((near, 3 * width), BF), pltpu.VMEM((near, wide), BF), pltpu.VMEM((near, ranks), F32)],
    )
    token_hops = [tie(item, low1_near) for item in token_hops]
    token_blocks = weave(tokens, token_core, token_hops)
    n1_far, low1_far, qkv_seq = whole_call(
        functools.partial(qkv_body, tuple(range(2, count)), True),
        [mask] + norm1 + [pull_far] + token_blocks[2:] + [moved_near],
        [shape((far, wide), BF), shape((far, ranks), BF), shape((rows, 3 * width), BF)],
        "qkv_far",
        scratch=[pltpu.VMEM((far, 3 * width), BF), pltpu.VMEM((far, wide), BF), pltpu.VMEM((far, ranks), F32)],
    )

    grad_hops = hops_of(tie(grad_own, low1_far))
    sums = []
    attended = []
    seq_in = qkv_seq
    for pair in range(pairs):
        part, kept = whole_call(
            functools.partial(attend_body, seq_len, pair),
            [limit, seq_in, push],
            [shape((rows, PAIR), BF), shape((seqs, 2, seq_len, seq_len), BF)],
            f"attend{pair}",
            scratch=[pltpu.VMEM((PAIR, rows), BF)],
        )
        sums.append(kept)
        attended.append(part)
        if pair == 0:
            seq_in = tie(qkv_seq, part)
    after = attended[-1]
    gathered_heads = []
    for part in attended:
        gathered_heads.append(weave(part, core_swap(part), hops_of(part)))
    heads = [gathered_heads[p][d] for d in range(count) for p in range(pairs)]

    proj_parts = []
    for item in proj_hops:
        item = tie(item, after)
        other = dp_swap(item[: width // 2], 1)
        proj_parts += [item, other, core_swap(item), core_swap(other)]
    grad_blocks = weave(grad_own, grad_core, [tie(item, after) for item in grad_hops])
    w_all, in_all, w_cat, low_t = whole_call(
        functools.partial(join_body, count),
        [low1_near, low1_far, push, weight_three, proj_own, proj_core] + proj_parts,
        [shape((wide, wide), BF), shape((ranks, wide), BF), shape((wide, 3 * width), BF), shape((ranks, rows), BF)],
        "join",
        smem=[dp_at],
    )

    def block_call(ids, gate, name):
        size = len(ids) * own
        extra = [shape((size, ranks), BF), shape((size, wide), F32)] if 0 in ids else []
        keep = mask if gate is None else tie(mask, gate)
        return whole_call(
            functools.partial(block_body, ids, count, pairs, min(512, hid)),
            [keep, w_all, in_all, c_proj_out, row(proj_bias), row(norm2_gain), row(norm2_shift), c_up_in, up_weight,
             row(up_bias), c_up_out, down_weight, c_down_in, c_down_out]
            + [token_blocks[i] for i in ids] + [grad_blocks[i] for i in ids] + heads,
            [shape((size, wide), BF), shape((size, wide), BF), shape((size, ranks), BF), shape((size, ranks), BF),
             shape((size, ranks), BF), shape((size, hid), BF), shape((size, hid), BF), shape((size, ranks), BF)]
            + extra,
            name,
            scratch=[pltpu.VMEM((size, wide), BF)] * 3
            + [pltpu.VMEM((size, ranks), F32), pltpu.VMEM((own, wide), F32)] + [pltpu.VMEM((own, ranks), F32)] * 2,
            long=gate is not None,
        )

    odd = block_call(odd_ids, None, "block_odd")
    odd_moved = core_swap(odd[0])
    even = block_call(even_ids, odd[3], "block_even")
    up_joined = join(even[0], odd_moved, "up_join")
    up_hops = send_far(up_joined)
    mine = block_call(near_ids, up_joined, "block_near")
    up_swap = core_swap(mine[0][own:])
    groups = (mine, even, odd)
    order_ids = (near_ids, even_ids, odd_ids)
    pack_hidden, p_up_in, p_down_out = whole_call(
        functools.partial(hidden_grads_body, 3, tuple(len(i) for i in order_ids)),
        [pick] + [g[k] for k in (2, 6, 4, 5, 3, 1, 7) for g in groups]
        + [grad_blocks[i] for ids in order_ids for i in ids],
        [shape((ranks, 2 * hid + cols), BF), shape((ranks, wide), F32), shape((ranks, wide), F32)],
        "hidden_grads",
    )
    up_hops = [tie(item, p_up_in) for item in up_hops]
    proj_low, mid = mine[8:]
    back = whole_call(
        functools.partial(mid_back_body, (2 + len(up_hops), count)),
        [mask, cotangent, mid, row(norm2_gain), c_proj_out, w_all, in_all, mine[0], up_swap] + up_hops,
        [shape((own, wide), F32), shape((own, wide), BF), shape((own, ranks), BF)]
        + [shape((own, width), BF)] * count,
        "mid_back",
        long=True,
    )
    grad_mid, grad_attn, grad_proj_low = back[:3]
    grad_att = exchange(back[3:])
    hidden_moved = dp_swap(tie(pack_hidden, grad_proj_low), top)

    messages = whole_call(
        functools.partial(message_body, count, pairs),
        [p_up_in, p_down_out, proj_low, grad_attn, grad_proj_low] + heads,
        [shape((4 * ranks, width), BF)] * count,
        "message",
        smem=[place],
        scratch=[pltpu.VMEM((ranks, wide), F32)],
        long=True,
    )
    down_parts = whole_call(
        functools.partial(down_body, 3, own),
        [tie(down_weight, messages[0]), c_down_out] + [g[5] for g in groups] + [g[7] for g in groups],
        [shape(g[0].shape, BF) for g in groups],
        "down",
        long=True,
    )
    down_mine, down_even, down_odd = down_parts
    grad_att = [grad_att[0]] + [tie(item, down_mine) for item in grad_att[1:]]
    wide_messages = exchange([tie(item, *grad_att[1:]) for item in messages])
    down_moved = core_swap(tie(down_odd, *grad_att[1:]))
    down_swap = core_swap(tie(down_mine[own:], *grad_att[1:]))

    back_pieces = []
    grad_seq = None
    for pair in range(pairs):
        last = pair == pairs - 1
        inputs = [qkv_seq, sums[pair]]
        outs = [shape((PAIR, rows), BF), shape((rows, PAIR), BF), shape((rows, PAIR), BF)]
        scratch = []
        if pair == 0:
            inputs += [pull_near, pull_far] + grad_att
        else:
            inputs += [grad_seq]
        if last:
            inputs += [push, low_t, n1_near, n1_far, c_qkv_out] + back_pieces
            outs = [shape((width, rows), BF), shape((rows, width), BF), shape((rows, width), BF),
                    shape((ranks, rows), BF), shape((ranks, 3 * width), BF)] + [shape((ranks, width), BF)] * count
        if pair == 0:
            if last:
                scratch += [pltpu.VMEM((rows, width), BF)]
            else:
                outs += [shape((rows, width), BF)]
            scratch += [pltpu.VMEM((rows, width), BF)]
        if last:
            scratch += [pltpu.VMEM((ranks, rows), BF), pltpu.VMEM((ranks, wide), F32)]
        results = whole_call(
            functools.partial(attend_back_body, pair, pairs, count, seq_len),
            inputs,
            outs,
            f"attend_back{pair}",
            smem=[place] if last else [],
            scratch=scratch,
            long=True,
        )
        if pair == 0:
            passed = results[0]
            wide_messages = [wide_messages[0]] + [tie(item, passed) for item in wide_messages[1:]]
            (pack_wide,) = whole_call(
                functools.partial(pack_body, count, 0),
                [pick] + wide_messages,
                [shape((ranks, 4 * width + cols), BF)],
                "pack_wide",
            )
            hidden_half = double(pack_hidden, tie(hidden_moved, passed, *wide_messages))
            hidden_moved = dp_swap(hidden_half, top // 2)
            hidden_first = dp_swap(hidden_half, top // 4)
            wide_moved = dp_swap(pack_wide, top)
            down_joined = join(down_even, tie(down_moved, passed, *wide_messages), "down_join")
            down_first = send_half(down_joined, 0)
        if not last:
            back_pieces += list(results[:3])
            grad_seq = tie(results[3], pack_wide, hidden_half, down_joined)
    grad_q, grad_k, grad_v, part_t, g_qkv_out = results[:5]
    down_first = [tie(item, part_t) for item in down_first]
    hidden_moved = tie(hidden_moved, part_t)
    hidden_first = tie(hidden_first, part_t)
    late_messages = exchange(results[5:])
    hidden_second = dp_swap(hidden_moved, top // 4)
    wide_moved_first = tie(wide_moved, part_t)
    wide_found = double(pack_wide, wide_moved_first)
    wide_moved = dp_swap(wide_found, top // 2)

    def unproject(ids, gates, name):
        size = len(ids) * own
        return whole_call(
            functools.partial(qkv_back_body, ids),
            [push, w_cat, c_qkv_in, grad_q, grad_k, grad_v, tie(part_t, *gates)],
            [shape((size, wide), BF)],
            name,
            scratch=[pltpu.VMEM((own, 3 * width), BF)],
            long=True,
        )[0]

    odd_part = unproject(odd_ids, [wide_moved_first, hidden_moved, hidden_first, *down_first], "qkv_back_odd")
    odd_moved = core_swap(odd_part)
    even_part = unproject(even_ids, [odd_part], "qkv_back_even")
    qkv_joined = join(even_part, tie(odd_moved, *late_messages[1:], wide_moved), "qkv_join")
    qkv_first = send_half(qkv_joined, 0)
    late_messages = [late_messages[0]] + [tie(item, qkv_joined) for item in late_messages[1:]]
    (pack_late,) = whole_call(
        functools.partial(pack_body, count, 1),
        [pick, g_qkv_out] + late_messages,
        [shape((ranks, 4 * width + cols), BF)],
        "pack_late",
    )
    late_moved = dp_swap(pack_late, top)
    wide_found = double(wide_found, wide_moved)
    wide_moved = dp_swap(wide_found, top // 4)
    near_part = unproject(near_ids, [qkv_joined, pack_late], "qkv_back_near")
    qkv_swap = core_swap(near_part[own:])
    qkv_first = [tie(item, near_part) for item in qkv_first]
    qkv_second = send_half(tie(qkv_joined, *qkv_first), 1)
    late_found = double(pack_late, tie(late_moved, near_part, hidden_second, *qkv_first))
    late_moved = dp_swap(late_found, top // 2)
    late_moved = tie(late_moved, *qkv_second)
    wide_found = widen(double(wide_found, tie(wide_moved, late_moved)), top // 8)
    proj_in_full, wide_part = whole_call(
        functools.partial(spread_wide_body, width),
        [wide_found],
        [shape((width, cols), F32), shape((3 * cols, width), BF)],
        "spread_wide",
        final=(0,),
    )
    wide_blocks = weave(wide_part, core_swap(wide_part), hops_of(wide_part))
    late_found = double(late_found, late_moved)
    late_moved = dp_swap(late_found, top // 4)
    down_second = send_half(tie(down_joined, *qkv_second), 1)
    (grad_input,) = whole_call(
        input_back_body,
        [tokens, grad_mid, row(norm1_gain), near_part, qkv_swap, *qkv_first, *qkv_second],
        [shape((own, wide), F32)],
        "input_back",
        scratch=[pltpu.VMEM((own, wide), F32)],
        final=(0,),
    )
    late_found = widen(double(late_found, tie(late_moved, grad_input)), top // 8)
    qkv_out_full, late_part = whole_call(
        functools.partial(spread_late_body, width),
        [late_found],
        [shape((3, cols, width), F32), shape((cols, width), BF)],
        "spread_late",
        final=(0,),
    )
    late_swap = core_swap(late_part)
    late_hops = hops_of(late_part)
    hidden_found = jnp.concatenate([hidden_half, hidden_moved, hidden_first, tie(hidden_second, late_part)], 0)
    up_out_full, down_in_full = whole_call(
        functools.partial(spread_hidden_body, hid),
        [widen(hidden_found, top // 8)],
        [shape((cols, hid), F32), shape((hid, cols), F32)],
        "spread_hidden",
        final=(0, 1),
    )
    up_in_full, down_out_full, proj_out_full = whole_call(
        functools.partial(place_wide_body, count),
        [tie(wide_blocks[0], up_out_full)] + wide_blocks[1:],
        [shape((wide, cols), F32), shape((cols, wide), F32), shape((cols, wide), F32)],
        "place_wide",
        smem=[place],
        final=(0, 1, 2),
    )
    late_blocks = weave(late_part, late_swap, [tie(item, up_in_full) for item in late_hops])
    (result,) = whole_call(
        result_body,
        [mid, row(down_bias), down_mine, down_swap, *down_first, *[tie(item, up_in_full) for item in down_second]],
        [shape((own, wide), F32)],
        "result",
        final=(0,),
    )
    (qkv_in_full,) = whole_call(
        functools.partial(place_late_body, count),
        late_blocks,
        [shape((wide, cols), F32)],
        "place_late",
        smem=[place],
        final=(0,),
    )
    return (
        result,
        grad_input,
        qkv_in_full,
        jnp.transpose(qkv_out_full, (1, 0, 2)),
        proj_in_full,
        proj_out_full,
        up_in_full,
        up_out_full,
        down_in_full,
        down_out_full,
    )


def solution(mesh):
    in_specs = (
        P(("dp", "tensor"), None),
        P(("dp", "tensor"), None),
        P("dp", None),
        P("dp", None),
        P("dp", None),
        P(),
        P(),
        P(None, None, "tensor"),
        P(None, "tensor"),
        P("tensor", None),
        P(),
        P(),
        P(),
        P(None, "tensor"),
        P("tensor"),
        P("tensor", None),
        P(),
        P(),
        P(None, None, "tensor"),
        P("tensor", None),
        P(),
        P(),
        P(None, "tensor"),
        P("tensor", None),
        P(),
    )
    out_specs = (
        P(("dp", "tensor"), None),
        P(("dp", "tensor"), None),
        P(),
        P(None, None, "tensor"),
        P("tensor", None),
        P(),
        P(),
        P(None, "tensor"),
        P("tensor", None),
        P(),
    )
    run = functools.partial(body, mesh.shape["tensor"], mesh.shape["dp"])
    return jax.shard_map(run, mesh=mesh, in_specs=in_specs, out_specs=out_specs, check_vma=False)
```
